512 devices in a mesh: region: 64 (over z, y_hi, core), tracer: 8 (over x, y_lo).
Axes of the slice: x: 4, y: 4 (y_hi: 2, y_lo: 2; y = y_hi * 2 + y_lo), z: 16, core: 2. Of those that a mesh axis runs over, the one named last changes fastest.
Arguments:
- cotangent: float32 [32, 32768], P('tracer', 'region'), may hold values from -6 to 6
- states: float32 [6, 32, 32768], P(None, 'tracer', 'region'), may hold values from -6 to 6
- implicit_inverse: float32 [1024, 32, 32], P('region'), may hold values from -3 to 3
- wet_levels: int32 [1024], P('region'), may hold values from 1 to 32
- explicit_tiles: bfloat16 [64, 5, 512, 512], P('region'), may hold values from -0.125 to 0.125
- tile_offset: int32 [64, 5], P('region'), may hold values from -2 to 2, as said below
- tile_count: int32 [64], P('region'), may hold values from 1 to 5
- uptake_weight: float32 [32, 32], replicated, may hold values from -1 to 1
- release_weight: float32 [32, 32], replicated, may hold values from -1 to 1
Outputs:
- initial_adjoint: float32 [32, 32768], P('tracer', 'region')
The draws below stay inside these ranges and needn't reach their ends.
Inputs may be any that keep to these rules, and one draw needn't show every extreme that they name: `tile_offset`: the offsets of one region are distinct; only the first tile_count slots of a region are used.
All inputs are finite; a program needn't handle non-finite values.
Results may differ from the reference program's by a relative error of at most 0.0032.
Values sent between devices are 32-bit elements; how exact they have to be, the bound alone decides.
No kernel may reach another device: no remote copies, remote signals or barrier semaphores. Data moves between devices by JAX's collectives and lax.ppermute only.
A program may use at most 64 MiB of HBM per device.

```python
import math
import jax
import jax.numpy as jnp
from jax import lax

NTR = 32
LEV = 32
STEPS = 6
REACH = 2
TILES = 5
BOX_DEV = 512
REGIONS = 64
BOXES = 32768
NCOL = 1024


def draw_implicit_inverse(key, part):
    noise = jax.random.normal(key, (NCOL, LEV, LEV), jnp.float32)
    identity = jnp.eye(LEV, dtype=jnp.float32)
    return jnp.clip(identity[None] + 0.5 * noise / math.sqrt(LEV), -3.0, 3.0)


def one_order(subkey):
    return jax.random.permutation(subkey, TILES)


def draw_tile_offset(key, part):
    subkeys = jax.random.split(jax.random.fold_in(key, 17), REGIONS)
    return (jax.vmap(one_order)(subkeys).astype(jnp.int32) - REACH).astype(jnp.int32)


def with_ends(entries, rng, smallest, top_value):
    extent = entries.shape
    place = [jax.random.randint(jax.random.fold_in(rng, axis), (), 0, extent[axis]) for axis in range(len(extent))]
    entries = entries.at[tuple(place)].set(smallest)
    longest = extent.index(max(extent))
    place[longest] = (place[longest] + 1) % extent[longest]
    return entries.at[tuple(place)].set(top_value)


def steps_of(own_key, dims, pieces, low, largest):
    level, own = 1.0, jax.random.fold_in(own_key, 6)
    for dim, shards_of in pieces:
        steps = jnp.exp(jax.random.uniform(jax.random.fold_in(own, dim), (shards_of,), jnp.float32, low / len(pieces), largest / len(pieces)))
        level = level * jnp.repeat(steps, dims[dim] // shards_of).reshape([-1 if axis == dim else 1 for axis in range(len(dims))])
    return level


def normal_values(key, dims, spread, reach, shards=(), held_as=jnp.bfloat16):
    level = steps_of(key, dims, shards, -0.22, 0.18) if shards else 1.0
    result = jax.random.normal(key, dims, jnp.float32) * spread * level
    return jnp.minimum(jnp.maximum(result, -reach), reach).astype(held_as)


def setup_inputs(seed: int = 0) -> dict:
    seeds = jax.random.split(jax.random.key(seed), 10)
    return {
        "cotangent": normal_values(seeds[0], (NTR, BOXES), 1.0, 6.0, ((0, 8), (1, 64)), jnp.float32),
        "states": normal_values(seeds[1], (STEPS, NTR, BOXES), 1.0, 6.0, ((1, 8), (2, 64)), jnp.float32),
        "implicit_inverse": draw_implicit_inverse(jax.random.fold_in(seeds[9], 71), 0),
        "wet_levels": with_ends(jax.random.randint(seeds[3], (NCOL,), 1, LEV + 1), jax.random.fold_in(seeds[3], 1), 1, LEV).astype(jnp.int32),
        "explicit_tiles": normal_values(seeds[4], (REGIONS, TILES, BOX_DEV, BOX_DEV), (4 * BOX_DEV) ** -0.5, 0.125, ((0, 64),)),
        "tile_offset": draw_tile_offset(jax.random.fold_in(seeds[9], 71), 0),
        "tile_count": with_ends(jax.random.randint(seeds[6], (REGIONS,), 1, TILES + 1), jax.random.fold_in(seeds[6], 1), 1, TILES).astype(jnp.int32),
        "uptake_weight": normal_values(seeds[7], (NTR, NTR), NTR ** -0.5, 1.0, (), jnp.float32),
        "release_weight": normal_values(seeds[8], (NTR, NTR), NTR ** -0.5, 1.0, (), jnp.float32),
    }


def region_terms(paired):
    region_block, tile_block = paired
    return jnp.einsum('tb,kbc->ktc', region_block.astype(jnp.float32), tile_block.astype(jnp.float32), precision=lax.Precision.HIGHEST)


def reference(cotangent, states, implicit_inverse, wet_levels, explicit_tiles, tile_offset, tile_count, uptake_weight, release_weight):
    highest = lax.Precision.HIGHEST
    wet_mask = (jnp.arange(LEV, dtype=jnp.int32)[None, :] < wet_levels[:, None]).astype(jnp.float32).reshape(1, BOXES)
    live_slots = (jnp.arange(TILES, dtype=jnp.int32)[None, :] < tile_count[:, None]).astype(jnp.float32)
    targets = ((jnp.arange(REGIONS, dtype=jnp.int32)[:, None] + tile_offset) % REGIONS).astype(jnp.int32)
    adjoint = cotangent
    for section in range(STEPS - 1, -1, -1):
        columns = adjoint.reshape(NTR, NCOL, LEV)
        settled = jnp.einsum('tcm,cml->tcl', columns, implicit_inverse, precision=highest).reshape(NTR, BOXES) * wet_mask
        settled_half = settled.astype(jnp.bfloat16)
        by_region = settled_half.reshape(NTR, REGIONS, BOX_DEV).transpose(1, 0, 2)
        terms = lax.map(region_terms, (by_region, explicit_tiles))
        terms = terms * live_slots[:, :, None, None]
        inflow = jnp.zeros((REGIONS, NTR, BOX_DEV), jnp.float32)
        inflow = inflow.at[targets.reshape(-1)].add(terms.reshape(REGIONS * TILES, NTR, BOX_DEV))
        inflow = inflow.transpose(1, 0, 2).reshape(NTR, BOXES)
        uptake = jnp.dot(uptake_weight, states[section], precision=highest)
        pushed = jnp.dot(release_weight.T, settled, precision=highest)
        reacted = jnp.dot(uptake_weight.T, (1.0 - jnp.tanh(uptake) ** 2) * pushed, precision=highest)
        adjoint = wet_mask * (inflow + reacted)
    return adjoint
```

```python
import jax
import jax.numpy as jnp
from jax import lax
from jax.experimental import pallas as pl
from jax.experimental.pallas import tpu as pltpu
from jax.sharding import Mesh, PartitionSpec as P

REGION = ("z", "yhi", "core")
TRACER = ("x", "ylo")
EVERY = REGION + TRACER
SPAN = 128


def device_at(sizes, chip, core, x, ylo):
    nq, nx, ny = sizes
    return (((chip % nq) * 2 + core) * nx + x) * ny + ylo


def neighbour_groups(sizes):
    nq, nx, ny = sizes
    return [
        [device_at(sizes, q, 1, x, yl), device_at(sizes, q + 1, 0, x, ny - 1 - yl)]
        for q in range(nq)
        for x in range(nx)
        for yl in range(ny)
    ]


def halves(value):
    high = value.astype(jnp.bfloat16)
    low = (value - high.astype(jnp.float32)).astype(jnp.bfloat16)
    return high, low


def dot(a, b):
    return lax.dot_general(a, b, (((1,), (0,)), ((), ())), preferred_element_type=jnp.float32)


def dot_split(a_high, a_low, b_high, b_low):
    rows = a_high.shape[0]
    both = dot(jnp.concatenate([a_high, a_low], axis=0), b_high)
    return both[:rows] + both[rows:] + dot(a_high, b_low)


def slot_at(offsets, distance):
    slots = offsets.shape[0]
    slot = jnp.int32(0)
    for k in range(slots):
        slot = slot + jnp.where(offsets[k] == distance, k, 0)
    return slot


def slot_live(offsets, count, distance):
    slots = offsets.shape[0]
    live = jnp.int32(0)
    for k in range(slots):
        live = live + jnp.where((offsets[k] == distance) & (k < count[0]), 1, 0)
    return live > 0


def away(core):
    return 2 * core[0] - 1


def lend_kernel(offsets, count, core, wet, tile, inverse, cotangent, lent, shared):
    live = slot_live(offsets, count, -2 * away(core))
    lent[...] = jnp.where(live, tile[0, 0].astype(jnp.float32), 0.0)
    columns, levels, _ = inverse.shape
    lane = lax.broadcasted_iota(jnp.int32, (levels, levels), 1)
    row = lax.broadcasted_iota(jnp.int32, (8, levels), 1)
    tracers = cotangent.shape[0]
    for c in range(columns):
        at = slice(c * levels, (c + 1) * levels)
        shared[0:levels, at] = jnp.where(lane < wet[c], inverse[c], 0.0)
        shared[levels : levels + 8, at] = jnp.where(row < wet[c], 1.0, 0.0)
    shared[levels + 8 - tracers :, :] = cotangent[...]


def prepare_kernel(core, shared, gathered, borrowed, uptake_weight, tile_out, block_high, block_low, wet_out, slopes, start):
    tile_out[...] = borrowed[...].astype(jnp.bfloat16)
    own = core[0]
    levels = 32
    boxes = shared.shape[2]
    spans = boxes // SPAN
    same = (
        lax.broadcasted_iota(jnp.int32, (SPAN, SPAN), 0) // levels
        == lax.broadcasted_iota(jnp.int32, (SPAN, SPAN), 1) // levels
    )
    for which in range(2):
        side = own if which == 0 else 1 - own
        for s in range(spans):
            part = shared[side, 0:levels, s * SPAN : (s + 1) * SPAN]
            full = jnp.concatenate([part] * (SPAN // levels), axis=0)
            high, low = halves(jnp.where(same, full, 0.0))
            block_high[which * spans + s] = high
            block_low[which * spans + s] = low
        wet_out[which : which + 1, :] = shared[side, levels : levels + 1, :]
    peers = gathered.shape[0]
    tracers = 4
    for t in range(peers):
        at = slice(t * tracers, (t + 1) * tracers)
        start[at, :] = gathered[t, 0:tracers, :]
        start[slice(t * tracers + peers * tracers, (t + 1) * tracers + peers * tracers), :] = gathered[
            t, tracers : 2 * tracers, :
        ]
        for n in range(slopes.shape[0]):
            slopes[n, at, :] = gathered[t, (2 + n) * tracers : (3 + n) * tracers, :]
    weight_high, weight_low = halves(uptake_weight[...])
    for n in range(slopes.shape[0]):
        state_high, state_low = halves(slopes[n])
        reach = jnp.tanh(dot_split(weight_high, weight_low, state_high, state_low))
        slopes[n] = 1.0 - reach * reach


def step_kernel(
    offsets, count, core, adjoint, tiles, borrowed, block_high, block_low, wet, slope, uptake_t, release_t, send, keep, settled,
    *, first,
):
    own = core[0]
    direction = away(core)
    boxes = tiles.shape[3]
    tracers = send.shape[0] // 2
    spans = boxes // SPAN
    if first:
        pair = (adjoint[0:tracers, :], adjoint[tracers:, :])
    else:
        pair = (
            wet[0:1, :] * (adjoint[own, 0:tracers, :] + adjoint[1 - own, tracers:, :]),
            wet[1:2, :] * (adjoint[own, tracers:, :] + adjoint[1 - own, 0:tracers, :]),
        )
    for which in range(2):
        high, low = halves(pair[which])
        for s in range(spans):
            at = slice(s * SPAN, (s + 1) * SPAN)
            k = which * spans + s
            settled[which, :, at] = dot_split(high[:, at], low[:, at], block_high[k], block_low[k])
    own_high, own_low = halves(settled[0])
    other = settled[1].astype(jnp.bfloat16)

    def term(distance):
        product = dot(own_high, tiles[0, slot_at(offsets, distance)])
        return jnp.where(slot_live(offsets, count, distance), product, 0.0)

    send[0:tracers, :] = term(direction) + dot(other, borrowed[...])
    send[tracers:, :] = term(2 * direction)
    release_high, release_low = halves(release_t[...])
    pushed = slope[0] * dot_split(release_high, release_low, own_high, own_low)
    pushed_high, pushed_low = halves(pushed)
    uptake_high, uptake_low = halves(uptake_t[...])
    keep[0:tracers, :] = term(0) + dot_split(uptake_high, uptake_low, pushed_high, pushed_low)
    keep[tracers:, :] = term(-direction)


def local(
    cotangent,
    states,
    implicit_inverse,
    wet_levels,
    explicit_tiles,
    tile_offset,
    tile_count,
    uptake_weight,
    release_weight,
    *,
    sizes,
):
    tracers_here, boxes = cotangent.shape
    sections = states.shape[0]
    columns, levels, _ = implicit_inverse.shape
    tracers = uptake_weight.shape[0]
    spans = boxes // SPAN
    peers = tracers // tracers_here
    f32, bf16 = jnp.float32, jnp.bfloat16
    shape = jax.ShapeDtypeStruct
    vmem = pl.BlockSpec(memory_space=pltpu.VMEM)
    smem = pl.BlockSpec(memory_space=pltpu.SMEM)
    core_index = lax.axis_index("core")
    core = core_index.astype(jnp.int32).reshape(1)
    offsets = tile_offset.reshape(-1)
    groups = neighbour_groups(sizes)

    def whole(dims):
        return pl.BlockSpec(dims, lambda i, *_: (0,) * len(dims))

    lent, shared = pl.pallas_call(
        lend_kernel,
        grid_spec=pltpu.PrefetchScalarGridSpec(
            num_scalar_prefetch=4,
            grid=(1,),
            in_specs=[
                pl.BlockSpec((1, 1, boxes, boxes), lambda i, o, n, c, w: (0, slot_at(o, -2 * away(c)), 0, 0)),
                whole((columns, levels, levels)),
                whole((tracers_here, boxes)),
            ],
            out_specs=[whole((boxes, boxes)), whole((levels + 8, boxes))],
        ),
        out_shape=[shape((boxes, boxes), f32), shape((levels + 8, boxes), f32)],
        name="lend",
    )(offsets, tile_count, core, wet_levels, explicit_tiles, implicit_inverse, cotangent)
    borrowed = lax.ppermute(lent, "core", [(0, 1), (1, 0)])
    shared = lax.all_gather(shared, "core")
    other_cotangent = lax.dynamic_index_in_dim(shared, 1 - core_index, 0, keepdims=False)[levels + 8 - tracers_here :]
    outgoing = jnp.concatenate([cotangent, other_cotangent, states.reshape(-1, boxes)], axis=0)
    gathered = lax.all_to_all(
        jnp.broadcast_to(outgoing, (peers, *outgoing.shape)), TRACER, split_axis=0, concat_axis=0, tiled=True
    )
    borrowed, block_high, block_low, wet, slopes, adjoint = pl.pallas_call(
        prepare_kernel,
        in_specs=[smem] + [vmem] * 4,
        out_specs=[vmem] * 6,
        out_shape=[
            shape((boxes, boxes), bf16),
            shape((2 * spans, SPAN, SPAN), bf16),
            shape((2 * spans, SPAN, SPAN), bf16),
            shape((2, boxes), f32),
            shape((sections, tracers, boxes), f32),
            shape((2 * tracers, boxes), f32),
        ],
        name="prepare",
    )(core, shared, gathered, borrowed, uptake_weight)
    uptake_t, release_t = uptake_weight.T, release_weight.T
    for section in range(sections - 1, -1, -1):
        first = section == sections - 1

        def step(*refs, first=first):
            step_kernel(*refs, first=first)

        send, keep = pl.pallas_call(
            step,
            in_specs=[smem] * 3 + [vmem] * 9,
            out_specs=[vmem] * 2,
            out_shape=[shape((2 * tracers, boxes), f32)] * 2,
            scratch_shapes=[pltpu.VMEM((2, tracers, boxes), f32)],
            name="step_first" if first else "step",
        )(offsets, tile_count, core, adjoint, explicit_tiles, borrowed, block_high, block_low, wet,
          slopes[section : section + 1], uptake_t, release_t)
        arrived = lax.all_gather(send, EVERY, axis_index_groups=groups)
        keep = keep + lax.dynamic_index_in_dim(arrived, core_index, 0, keepdims=False)
        adjoint = lax.all_gather(keep, "core")
    row = (lax.axis_index("x") * lax.axis_size("ylo") + lax.axis_index("ylo")) * tracers_here
    mine = lax.dynamic_slice(adjoint, (core_index, row, 0), (1, tracers_here, boxes))[0]
    theirs = lax.dynamic_slice(adjoint, (1 - core_index, tracers + row, 0), (1, tracers_here, boxes))[0]
    return wet[0:1] * (mine + theirs)


def solution(mesh):
    regions, tracer_devices = mesh.devices.shape
    nq, nx, ny = regions // 2, tracer_devices // 2, 2
    fine = Mesh(mesh.devices.reshape(nq // 2, 2, 2, nx, ny), EVERY)
    placed = (
        P(TRACER, REGION),
        P(None, TRACER, REGION),
        P(REGION, None, None),
        P(REGION),
        P(REGION, None, None, None),
        P(REGION, None),
        P(REGION),
        P(),
        P(),
    )

    def body(*args):
        return local(*args, sizes=(nq, nx, ny))

    return jax.shard_map(body, mesh=fine, in_specs=placed, out_specs=P(TRACER, REGION), check_vma=False)
```

```python
import jax
import jax.numpy as jnp
from jax import lax
from jax.experimental import pallas as pl
from jax.experimental.pallas import tpu as pltpu
from jax.sharding import Mesh, PartitionSpec as P

REGION = ("z", "yhi", "core")
TRACER = ("x", "ylo")
EVERY = REGION + TRACER
SPAN = 128
VMEM_LIMIT = 16 * 2**20


def device_at(sizes, chip, core, x, ylo):
    nq, nx, ny = sizes
    return (((chip % nq) * 2 + core) * nx + x) * ny + ylo


def neighbour_groups(sizes):
    nq, nx, ny = sizes
    return [
        [device_at(sizes, q, 1, x, yl), device_at(sizes, q + 1, 0, x, ny - 1 - yl)]
        for q in range(nq)
        for x in range(nx)
        for yl in range(ny)
    ]


def halves(value):
    high = value.astype(jnp.bfloat16)
    low = (value - high.astype(jnp.float32)).astype(jnp.bfloat16)
    return high, low


def dot(a, b):
    return lax.dot_general(a, b, (((1,), (0,)), ((), ())), preferred_element_type=jnp.float32)


def dot_split(a_high, a_low, b_high, b_low):
    rows = a_high.shape[0]
    both = dot(jnp.concatenate([a_high, a_low], axis=0), b_high)
    return both[:rows] + both[rows:] + dot(a_high, b_low)


def slot_at(offsets, distance):
    slots = offsets.shape[0]
    slot = jnp.int32(0)
    for k in range(slots):
        slot = slot + jnp.where(offsets[k] == distance, k, 0)
    return slot


def slot_live(offsets, count, distance):
    slots = offsets.shape[0]
    live = jnp.int32(0)
    for k in range(slots):
        live = live + jnp.where((offsets[k] == distance) & (k < count[0]), 1, 0)
    return live > 0


def away(core):
    return 2 * core[0] - 1


def lend_kernel(offsets, count, core, wet, tile, inverse, cotangent, lent, shared):
    live = slot_live(offsets, count, -2 * away(core))
    lent[...] = jnp.where(live, tile[0, 0].astype(jnp.float32), 0.0)
    columns, levels, _ = inverse.shape
    lane = lax.broadcasted_iota(jnp.int32, (levels, levels), 1)
    row = lax.broadcasted_iota(jnp.int32, (8, levels), 1)
    tracers = cotangent.shape[0]
    for c in range(columns):
        at = slice(c * levels, (c + 1) * levels)
        shared[0:levels, at] = jnp.where(lane < wet[c], inverse[c], 0.0)
        shared[levels : levels + 8, at] = jnp.where(row < wet[c], 1.0, 0.0)
    shared[levels + 8 - tracers :, :] = cotangent[...]


def prepare_kernel(core, shared, gathered, borrowed, uptake_weight, tile_out, block_high, block_low, wet_out, slopes, start):
    tile_out[...] = borrowed[...].astype(jnp.bfloat16)
    own = core[0]
    levels = 32
    boxes = shared.shape[2]
    spans = boxes // SPAN
    same = (
        lax.broadcasted_iota(jnp.int32, (SPAN, SPAN), 0) // levels
        == lax.broadcasted_iota(jnp.int32, (SPAN, SPAN), 1) // levels
    )
    for which in range(2):
        side = own if which == 0 else 1 - own
        for s in range(spans):
            part = shared[side, 0:levels, s * SPAN : (s + 1) * SPAN]
            full = jnp.concatenate([part] * (SPAN // levels), axis=0)
            high, low = halves(jnp.where(same, full, 0.0))
            block_high[which * spans + s] = high
            block_low[which * spans + s] = low
        wet_out[which : which + 1, :] = shared[side, levels : levels + 1, :]
    peers = gathered.shape[0]
    tracers = 4
    for t in range(peers):
        at = slice(t * tracers, (t + 1) * tracers)
        start[at, :] = gathered[t, 0:tracers, :]
        start[slice(t * tracers + peers * tracers, (t + 1) * tracers + peers * tracers), :] = gathered[
            t, tracers : 2 * tracers, :
        ]
        for n in range(slopes.shape[0]):
            slopes[n, at, :] = gathered[t, (2 + n) * tracers : (3 + n) * tracers, :]
    weight_high, weight_low = halves(uptake_weight[...])
    for n in range(slopes.shape[0]):
        state_high, state_low = halves(slopes[n])
        reach = jnp.tanh(dot_split(weight_high, weight_low, state_high, state_low))
        slopes[n] = 1.0 - reach * reach


def step_kernel(
    offsets, count, core, adjoint, tiles, borrowed, block_high, block_low, wet, slope, uptake_t, release_t, send, keep, settled,
    *, first,
):
    own = core[0]
    direction = away(core)
    boxes = tiles.shape[3]
    tracers = send.shape[0] // 2
    spans = boxes // SPAN
    if first:
        pair = (adjoint[0:tracers, :], adjoint[tracers:, :])
    else:
        pair = (
            wet[0:1, :] * (adjoint[own, 0:tracers, :] + adjoint[1 - own, tracers:, :]),
            wet[1:2, :] * (adjoint[own, tracers:, :] + adjoint[1 - own, 0:tracers, :]),
        )
    for which in range(2):
        high, low = halves(pair[which])
        for s in range(spans):
            at = slice(s * SPAN, (s + 1) * SPAN)
            k = which * spans + s
            settled[which, :, at] = dot_split(high[:, at], low[:, at], block_high[k], block_low[k])
    own_high, own_low = halves(settled[0])
    other = settled[1].astype(jnp.bfloat16)

    def term(distance):
        product = dot(own_high, tiles[0, slot_at(offsets, distance)])
        return jnp.where(slot_live(offsets, count, distance), product, 0.0)

    send[0:tracers, :] = term(direction) + dot(other, borrowed[...])
    send[tracers:, :] = term(2 * direction)
    release_high, release_low = halves(release_t[...])
    pushed = slope[0] * dot_split(release_high, release_low, own_high, own_low)
    pushed_high, pushed_low = halves(pushed)
    uptake_high, uptake_low = halves(uptake_t[...])
    keep[0:tracers, :] = term(0) + dot_split(uptake_high, uptake_low, pushed_high, pushed_low)
    keep[tracers:, :] = term(-direction)


def local(
    cotangent,
    states,
    implicit_inverse,
    wet_levels,
    explicit_tiles,
    tile_offset,
    tile_count,
    uptake_weight,
    release_weight,
    *,
    sizes,
):
    tracers_here, boxes = cotangent.shape
    sections = states.shape[0]
    columns, levels, _ = implicit_inverse.shape
    tracers = uptake_weight.shape[0]
    spans = boxes // SPAN
    peers = tracers // tracers_here
    f32, bf16 = jnp.float32, jnp.bfloat16
    shape = jax.ShapeDtypeStruct
    vmem = pl.BlockSpec(memory_space=pltpu.VMEM)
    smem = pl.BlockSpec(memory_space=pltpu.SMEM)
    core_index = lax.axis_index("core")
    core = core_index.astype(jnp.int32).reshape(1)
    offsets = tile_offset.reshape(-1)
    groups = neighbour_groups(sizes)

    def whole(dims):
        return pl.BlockSpec(dims, lambda i, *_: (0,) * len(dims))

    lent, shared = pl.pallas_call(
        lend_kernel,
        grid_spec=pltpu.PrefetchScalarGridSpec(
            num_scalar_prefetch=4,
            grid=(1,),
            in_specs=[
                pl.BlockSpec((1, 1, boxes, boxes), lambda i, o, n, c, w: (0, slot_at(o, -2 * away(c)), 0, 0)),
                whole((columns, levels, levels)),
                whole((tracers_here, boxes)),
            ],
            out_specs=[whole((boxes, boxes)), whole((levels + 8, boxes))],
        ),
        out_shape=[shape((boxes, boxes), f32), shape((levels + 8, boxes), f32)],
        compiler_params=pltpu.CompilerParams(vmem_limit_bytes=VMEM_LIMIT),
        name="lend",
    )(offsets, tile_count, core, wet_levels, explicit_tiles, implicit_inverse, cotangent)
    borrowed = lax.ppermute(lent, "core", [(0, 1), (1, 0)])
    shared = lax.all_gather(shared, "core")
    other_cotangent = lax.dynamic_index_in_dim(shared, 1 - core_index, 0, keepdims=False)[levels + 8 - tracers_here :]
    outgoing = jnp.concatenate([cotangent, other_cotangent, states.reshape(-1, boxes)], axis=0)
    gathered = lax.all_to_all(
        jnp.broadcast_to(outgoing, (peers, *outgoing.shape)), TRACER, split_axis=0, concat_axis=0, tiled=True
    )
    borrowed, block_high, block_low, wet, slopes, adjoint = pl.pallas_call(
        prepare_kernel,
        in_specs=[smem] + [vmem] * 4,
        out_specs=[vmem] * 6,
        out_shape=[
            shape((boxes, boxes), bf16),
            shape((2 * spans, SPAN, SPAN), bf16),
            shape((2 * spans, SPAN, SPAN), bf16),
            shape((2, boxes), f32),
            shape((sections, tracers, boxes), f32),
            shape((2 * tracers, boxes), f32),
        ],
        compiler_params=pltpu.CompilerParams(vmem_limit_bytes=VMEM_LIMIT),
        name="prepare",
    )(core, shared, gathered, borrowed, uptake_weight)
    uptake_t, release_t = uptake_weight.T, release_weight.T
    for section in range(sections - 1, -1, -1):
        first = section == sections - 1

        def step(*refs, first=first):
            step_kernel(*refs, first=first)

        send, keep = pl.pallas_call(
            step,
            in_specs=[smem] * 3 + [vmem] * 9,
            out_specs=[vmem] * 2,
            out_shape=[shape((2 * tracers, boxes), f32)] * 2,
            scratch_shapes=[pltpu.VMEM((2, tracers, boxes), f32)],
            compiler_params=pltpu.CompilerParams(vmem_limit_bytes=VMEM_LIMIT),
            name="step_first" if first else "step",
        )(offsets, tile_count, core, adjoint, explicit_tiles, borrowed, block_high, block_low, wet,
          slopes[section : section + 1], uptake_t, release_t)
        arrived = lax.all_gather(send, EVERY, axis_index_groups=groups)
        keep = keep + lax.dynamic_index_in_dim(arrived, core_index, 0, keepdims=False)
        adjoint = lax.all_gather(keep, "core")
    row = (lax.axis_index("x") * lax.axis_size("ylo") + lax.axis_index("ylo")) * tracers_here
    mine = lax.dynamic_slice(adjoint, (core_index, row, 0), (1, tracers_here, boxes))[0]
    theirs = lax.dynamic_slice(adjoint, (1 - core_index, tracers + row, 0), (1, tracers_here, boxes))[0]
    return wet[0:1] * (mine + theirs)


def solution(mesh):
    regions, tracer_devices = mesh.devices.shape
    nq, nx, ny = regions // 2, tracer_devices // 2, 2
    fine = Mesh(mesh.devices.reshape(nq // 2, 2, 2, nx, ny), EVERY)
    placed = (
        P(TRACER, REGION),
        P(None, TRACER, REGION),
        P(REGION, None, None),
        P(REGION),
        P(REGION, None, None, None),
        P(REGION, None),
        P(REGION),
        P(),
        P(),
    )

    def body(*args):
        return local(*args, sizes=(nq, nx, ny))

    return jax.shard_map(body, mesh=fine, in_specs=placed, out_specs=P(TRACER, REGION), check_vma=False)
```

```python
import jax
import jax.numpy as jnp
from jax import lax
from jax.experimental import pallas as pl
from jax.experimental.pallas import tpu as pltpu
from jax.sharding import Mesh, PartitionSpec as P


REGION = ("z", "yhi", "core")
TRACER = ("x", "ylo")
EVERY = REGION + TRACER
SPAN = 128
VMEM_LIMIT = 8 * 2**20


def device_at(sizes, chip, core, x, ylo):
    nq, nx, ny = sizes
    return (((chip % nq) * 2 + core) * nx + x) * ny + ylo


def neighbour_groups(sizes):
    nq, nx, ny = sizes
    return [
        [device_at(sizes, q, 1, x, yl), device_at(sizes, q + 1, 0, x, ny - 1 - yl)]
        for q in range(nq)
        for x in range(nx)
        for yl in range(ny)
    ]


def halves(value):
    high = value.astype(jnp.bfloat16)
    low = (value - high.astype(jnp.float32)).astype(jnp.bfloat16)
    return high, low


def dot(a, b):
    return lax.dot_general(a, b, (((1,), (0,)), ((), ())), preferred_element_type=jnp.float32)


def dot_split(a_high, a_low, b_high, b_low):
    rows = a_high.shape[0]
    both = dot(jnp.concatenate([a_high, a_low], axis=0), b_high)
    return both[:rows] + both[rows:] + dot(a_high, b_low)


def slot_at(offsets, distance):
    slots = offsets.shape[0]
    slot = jnp.int32(0)
    for k in range(slots):
        slot = slot + jnp.where(offsets[k] == distance, k, 0)
    return slot


def slot_live(offsets, count, distance):
    slots = offsets.shape[0]
    live = jnp.int32(0)
    for k in range(slots):
        live = live + jnp.where((offsets[k] == distance) & (k < count[0]), 1, 0)
    return live > 0


def away(core):
    return 2 * core[0] - 1


def lend_kernel(offsets, count, core, wet, tiles, inverse, lent, shared, buffer, arrival):
    distance = -2 * away(core)
    fetch = pltpu.make_async_copy(tiles.at[0, slot_at(offsets, distance)], buffer, arrival)
    fetch.start()
    columns, levels, _ = inverse.shape
    lane = lax.broadcasted_iota(jnp.int32, (levels, levels), 1)
    row = lax.broadcasted_iota(jnp.int32, (8, levels), 1)
    for c in range(columns):
        at = slice(c * levels, (c + 1) * levels)
        shared[0:levels, at] = jnp.where(lane < wet[c], inverse[c], 0.0)
        shared[levels : levels + 8, at] = jnp.where(row < wet[c], 1.0, 0.0)
    fetch.wait()
    live = slot_live(offsets, count, distance)
    lent[...] = jnp.where(live, buffer[...].astype(jnp.float32), 0.0)


def blocks_kernel(core, shared, borrowed, tile_out, block_high, block_low, wet_out):
    tile_out[...] = borrowed[...].astype(jnp.bfloat16)
    own = core[0]
    levels = shared.shape[1] - 8
    boxes = shared.shape[2]
    spans = boxes // SPAN
    same = (
        lax.broadcasted_iota(jnp.int32, (SPAN, SPAN), 0) // levels
        == lax.broadcasted_iota(jnp.int32, (SPAN, SPAN), 1) // levels
    )
    for which in range(2):
        side = own if which == 0 else 1 - own
        for s in range(spans):
            part = shared[side, 0:levels, s * SPAN : (s + 1) * SPAN]
            full = jnp.concatenate([part] * (SPAN // levels), axis=0)
            high, low = halves(jnp.where(same, full, 0.0))
            block_high[which * spans + s] = high
            block_low[which * spans + s] = low
        wet_out[which : which + 1, :] = shared[side, levels : levels + 1, :]


def gathered_kernel(gathered, uptake_weight, start, slopes):
    peers = gathered.shape[0]
    sections = slopes.shape[0]
    tracers = start.shape[0] // peers
    for t in range(peers):
        at = slice(t * tracers, (t + 1) * tracers)
        start[at, :] = gathered[t, 0:tracers, :]
        for n in range(sections):
            slopes[n, at, :] = gathered[t, (1 + n) * tracers : (2 + n) * tracers, :]
    weight_high, weight_low = halves(uptake_weight[...])
    for n in range(sections):
        state_high, state_low = halves(slopes[n])
        reach = jnp.tanh(dot_split(weight_high, weight_low, state_high, state_low))
        slopes[n] = 1.0 - reach * reach


def step_kernel(
    offsets, count, core, tracer, adjoint, tiles, borrowed, block_high, block_low, wet, slopes, uptake_t, release_t,
    send, keep, settled, rows,
    *, section, first, last,
):
    own = core[0]
    direction = away(core)
    boxes = tiles.shape[3]
    tracers = uptake_t.shape[0]
    spans = boxes // SPAN
    if first:
        pair = (adjoint[own], adjoint[1 - own])
    else:
        pair = (
            wet[0:1, :] * (adjoint[own, 0:tracers, :] + adjoint[1 - own, tracers:, :]),
            wet[1:2, :] * (adjoint[own, tracers:, :] + adjoint[1 - own, 0:tracers, :]),
        )
    for which in range(2):
        high, low = halves(pair[which])
        for s in range(spans):
            at = slice(s * SPAN, (s + 1) * SPAN)
            k = which * spans + s
            settled[which, :, at] = dot_split(high[:, at], low[:, at], block_high[k], block_low[k])
    own_high, own_low = halves(settled[0])
    other = settled[1].astype(jnp.bfloat16)

    def term(distance):
        product = dot(own_high, tiles[0, slot_at(offsets, distance)])
        return jnp.where(slot_live(offsets, count, distance), product, 0.0)

    def put(out, part, value, peer):
        if last:
            peers, few, _ = rows.shape
            for t in range(peers):
                rows[t] = value[t * few : (t + 1) * few]
            out[part * few : (part + 1) * few, :] = rows[peer]
        else:
            out[part * tracers : (part + 1) * tracers, :] = value

    put(send, 0, term(direction) + dot(other, borrowed[...]), tracer[1])
    put(send, 1, term(2 * direction), tracer[1])
    release_high, release_low = halves(release_t[...])
    pushed = slopes[section] * dot_split(release_high, release_low, own_high, own_low)
    pushed_high, pushed_low = halves(pushed)
    uptake_high, uptake_low = halves(uptake_t[...])
    put(keep, 0, term(0) + dot_split(uptake_high, uptake_low, pushed_high, pushed_low), tracer[0])
    put(keep, 1, term(-direction), tracer[0])


def local(
    cotangent,
    states,
    implicit_inverse,
    wet_levels,
    explicit_tiles,
    tile_offset,
    tile_count,
    uptake_weight,
    release_weight,
    *,
    sizes,
):
    tracers_here, boxes = cotangent.shape
    sections = states.shape[0]
    _, levels, _ = implicit_inverse.shape
    tracers = uptake_weight.shape[0]
    spans = boxes // SPAN
    peers = tracers // tracers_here
    f32, bf16 = jnp.float32, jnp.bfloat16
    shape = jax.ShapeDtypeStruct
    vmem = pl.BlockSpec(memory_space=pltpu.VMEM)
    smem = pl.BlockSpec(memory_space=pltpu.SMEM)
    core_index = lax.axis_index("core")
    core = core_index.astype(jnp.int32).reshape(1)
    here = lax.axis_index("x") * lax.axis_size("ylo")
    flip = lax.axis_index("ylo")
    tracer = jnp.stack([here + flip, here + lax.axis_size("ylo") - 1 - flip]).astype(jnp.int32)
    offsets = tile_offset.reshape(-1)
    groups = neighbour_groups(sizes)
    lean = pltpu.CompilerParams(vmem_limit_bytes=VMEM_LIMIT)

    outgoing = jnp.concatenate([cotangent, states.reshape(-1, boxes)], axis=0)
    copies = jnp.broadcast_to(outgoing, (peers, *outgoing.shape))
    gathered = lax.all_to_all(copies, TRACER, split_axis=0, concat_axis=0, tiled=True)
    lent, shared = pl.pallas_call(
        lend_kernel,
        in_specs=[smem] * 4 + [pl.BlockSpec(memory_space=pltpu.HBM), vmem],
        out_specs=[vmem] * 2,
        out_shape=[shape((boxes, boxes), f32), shape((levels + 8, boxes), f32)],
        scratch_shapes=[pltpu.VMEM((boxes, boxes), bf16), pltpu.SemaphoreType.DMA],
        compiler_params=lean,
        name="lend",
    )(offsets, tile_count, core, wet_levels, pltpu.with_memory_space_constraint(explicit_tiles, pltpu.HBM), implicit_inverse)
    borrowed = lax.ppermute(lent, "core", [(0, 1), (1, 0)])
    shared = lax.all_gather(shared, "core")
    borrowed, block_high, block_low, wet = pl.pallas_call(
        blocks_kernel,
        in_specs=[smem] + [vmem] * 2,
        out_specs=[vmem] * 4,
        out_shape=[
            shape((boxes, boxes), bf16),
            shape((2 * spans, SPAN, SPAN), bf16),
            shape((2 * spans, SPAN, SPAN), bf16),
            shape((2, boxes), f32),
        ],
        compiler_params=lean,
        name="blocks",
    )(core, shared, borrowed)
    start, slopes = pl.pallas_call(
        gathered_kernel,
        in_specs=[vmem] * 2,
        out_specs=[vmem] * 2,
        out_shape=[shape((tracers, boxes), f32), shape((sections, tracers, boxes), f32)],
        compiler_params=lean,
        name="gathered",
    )(gathered, uptake_weight)
    adjoint = lax.all_gather(start, "core")
    uptake_t, release_t = uptake_weight.T, release_weight.T
    for section in range(sections - 1, -1, -1):
        first, last = section == sections - 1, section == 0

        def step(*refs, section=section, first=first, last=last):
            step_kernel(*refs, section=section, first=first, last=last)

        exchanged = 2 * tracers_here if last else 2 * tracers
        send, keep = pl.pallas_call(
            step,
            in_specs=[smem] * 4 + [vmem] * 9,
            out_specs=[vmem] * 2,
            out_shape=[shape((exchanged, boxes), f32)] * 2,
            scratch_shapes=[pltpu.VMEM((2, tracers, boxes), f32), pltpu.VMEM((peers, tracers_here, boxes), f32)],
            compiler_params=lean,
        )(offsets, tile_count, core, tracer, adjoint, explicit_tiles, borrowed, block_high, block_low, wet,
          slopes, uptake_t, release_t)
        arrived = lax.all_gather(send, EVERY, axis_index_groups=groups)
        keep = keep + lax.dynamic_index_in_dim(arrived, core_index, 0, keepdims=False)
        adjoint = lax.all_gather(keep, "core")
    mine = lax.dynamic_index_in_dim(adjoint, core_index, 0, keepdims=False)[:tracers_here]
    theirs = lax.dynamic_index_in_dim(adjoint, 1 - core_index, 0, keepdims=False)[tracers_here:]
    return wet[0:1] * (mine + theirs)


def solution(mesh):
    regions, tracer_devices = mesh.devices.shape
    nq, nx, ny = regions // 2, tracer_devices // 2, 2
    fine = Mesh(mesh.devices.reshape(nq // 2, 2, 2, nx, ny), EVERY)
    placed = (
        P(TRACER, REGION),
        P(None, TRACER, REGION),
        P(REGION, None, None),
        P(REGION),
        P(REGION, None, None, None),
        P(REGION, None),
        P(REGION),
        P(),
        P(),
    )

    def body(*args):
        return local(*args, sizes=(nq, nx, ny))

    return jax.shard_map(body, mesh=fine, in_specs=placed, out_specs=P(TRACER, REGION), check_vma=False)
```

```python
import jax
import jax.numpy as jnp
from jax import lax
from jax.experimental import pallas as pl
from jax.experimental.pallas import tpu as pltpu
from jax.sharding import Mesh, PartitionSpec as P


REGION = ("z", "yhi", "core")
TRACER = ("x", "ylo")
EVERY = REGION + TRACER
SPAN = 128
VMEM_LIMIT = 8 * 2**20
OFFSETS_AT, COUNT_AT, CORE_AT, X_AT, WET_AT = 0, 5, 6, 7, 8


def neighbour_groups(sizes):
    nq, nx, ny = sizes

    def at(chip, core, x, ylo):
        return (((chip % nq) * 2 + core) * nx + x) * ny + ylo

    groups = []
    for q in range(nq):
        for x in range(nx):
            joined, alone = (1, 0) if q % 2 == 0 else (0, 1)
            groups.append([at(q, 1, x, joined), at(q + 1, 0, x, 1 - joined)])
            groups.append([at(q, 1, x, alone), at(q, 0, x, alone)])
    return groups


def halves(value):
    high = value.astype(jnp.bfloat16)
    low = (value - high.astype(jnp.float32)).astype(jnp.bfloat16)
    return high, low


def dot(a, b):
    return lax.dot_general(a, b, (((1,), (0,)), ((), ())), preferred_element_type=jnp.float32)


def dot_split(a_high, a_low, b_high, b_low):
    rows = a_high.shape[0]
    both = dot(jnp.concatenate([a_high, a_low], axis=0), b_high)
    return both[:rows] + both[rows:] + dot(a_high, b_low)


def slot_at(facts, slots, distance):
    slot = jnp.int32(0)
    for k in range(slots):
        slot = slot + jnp.where(facts[OFFSETS_AT + k] == distance, k, 0)
    return slot


def slot_live(facts, slots, distance):
    live = jnp.int32(0)
    for k in range(slots):
        live = live + jnp.where((facts[OFFSETS_AT + k] == distance) & (k < facts[COUNT_AT]), 1, 0)
    return live > 0


def away(facts):
    return 2 * facts[CORE_AT] - 1


def pack_kernel(cotangent, states, copies, buffer, fetched, sent):
    first = pltpu.make_async_copy(cotangent, buffer.at[0], fetched.at[0])
    rest = pltpu.make_async_copy(states, buffer.at[pl.ds(1, states.shape[0])], fetched.at[1])
    first.start()
    rest.start()
    first.wait()
    rest.wait()
    sends = [pltpu.make_async_copy(buffer, copies.at[t], sent.at[t]) for t in range(copies.shape[0])]
    for send in sends:
        send.start()
    for send in sends:
        send.wait()


def lend_kernel(facts, tiles, lent, buffer, arrival):
    slots = tiles.shape[1]
    distance = -2 * away(facts)
    fetch = pltpu.make_async_copy(tiles.at[0, slot_at(facts, slots, distance)], buffer, arrival)
    fetch.start()
    fetch.wait()
    lent[...] = jnp.where(slot_live(facts, slots, distance), buffer[...].astype(jnp.float32), 0.0)


def share_kernel(facts, inverse_hbm, shared, inverse, arrival):
    fetch = pltpu.make_async_copy(inverse_hbm, inverse, arrival)
    fetch.start()
    fetch.wait()
    columns, levels, _ = inverse.shape
    lane = lax.broadcasted_iota(jnp.int32, (levels, levels), 1)
    row = lax.broadcasted_iota(jnp.int32, (8, levels), 1)
    for c in range(columns):
        at = slice(c * levels, (c + 1) * levels)
        shared[0:levels, at] = jnp.where(lane < facts[WET_AT + c], inverse[c], 0.0)
        shared[levels : levels + 8, at] = jnp.where(row < facts[WET_AT + c], 1.0, 0.0)


def blocks_kernel(facts, shared, borrowed, tile_out, blocks, wet_out):
    own = facts[CORE_AT]
    levels = shared.shape[1] - 8
    boxes = shared.shape[2]
    spans = boxes // SPAN
    same = (
        lax.broadcasted_iota(jnp.int32, (SPAN, SPAN), 0) // levels
        == lax.broadcasted_iota(jnp.int32, (SPAN, SPAN), 1) // levels
    )
    for which in range(2):
        side = own if which == 0 else 1 - own
        for s in range(spans):
            part = shared[side, 0:levels, s * SPAN : (s + 1) * SPAN]
            full = jnp.concatenate([part] * (SPAN // levels), axis=0)
            high, low = halves(jnp.where(same, full, 0.0))
            blocks[0, which * spans + s] = high
            blocks[1, which * spans + s] = low
        wet_out[which : which + 1, :] = shared[side, levels : levels + 1, :]
    tile_out[...] = borrowed[...].astype(jnp.bfloat16)


def gathered_kernel(gathered, uptake_weight, start, slopes):
    peers, _, few, _ = gathered.shape
    for t in range(peers):
        at = slice(t * few, (t + 1) * few)
        start[at, :] = gathered[t, 0]
        for n in range(slopes.shape[0]):
            slopes[n, at, :] = gathered[t, 1 + n]
    weight_high, weight_low = halves(uptake_weight[...])
    for n in range(slopes.shape[0]):
        state_high, state_low = halves(slopes[n])
        reach = jnp.tanh(dot_split(weight_high, weight_low, state_high, state_low))
        slopes[n] = 1.0 - reach * reach


def step_kernel(
    facts, adjoint, tiles, borrowed, blocks, wet, slopes, uptake_t, release_t, send, keep, settled, rows,
    *, section, first, last,
):
    own = facts[CORE_AT]
    direction = away(facts)
    slots, boxes = tiles.shape[1], tiles.shape[3]
    tracers = uptake_t.shape[0]
    spans = boxes // SPAN
    if first:
        pair = (adjoint[own], adjoint[1 - own])
    else:
        pair = (
            wet[0:1, :] * (adjoint[own, 0:tracers, :] + adjoint[1 - own, tracers:, :]),
            wet[1:2, :] * (adjoint[own, tracers:, :] + adjoint[1 - own, 0:tracers, :]),
        )
    for which in range(2):
        high, low = halves(pair[which])
        for s in range(spans):
            at = slice(s * SPAN, (s + 1) * SPAN)
            k = which * spans + s
            settled[which, :, at] = dot_split(high[:, at], low[:, at], blocks[0, k], blocks[1, k])
    own_high, own_low = halves(settled[0])
    other = settled[1].astype(jnp.bfloat16)

    def term(distance):
        product = dot(own_high, tiles[0, slot_at(facts, slots, distance)])
        return jnp.where(slot_live(facts, slots, distance), product, 0.0)

    def put(out, part, value):
        few = out.shape[0] // 2
        if last:
            for x in range(rows.shape[0]):
                rows[x] = value[x * few : (x + 1) * few]
            value = rows[facts[X_AT]]
        out[part * few : (part + 1) * few, :] = value

    put(send, 0, term(direction) + dot(other, borrowed[...]))
    put(send, 1, term(2 * direction))
    release_high, release_low = halves(release_t[...])
    pushed = slopes[section] * dot_split(release_high, release_low, own_high, own_low)
    pushed_high, pushed_low = halves(pushed)
    uptake_high, uptake_low = halves(uptake_t[...])
    put(keep, 0, term(0) + dot_split(uptake_high, uptake_low, pushed_high, pushed_low))
    put(keep, 1, term(-direction))


def local(
    cotangent,
    states,
    implicit_inverse,
    wet_levels,
    explicit_tiles,
    tile_offset,
    tile_count,
    uptake_weight,
    release_weight,
    *,
    sizes,
):
    tracers_here, boxes = cotangent.shape
    sections = states.shape[0]
    columns, levels, _ = implicit_inverse.shape
    tracers = uptake_weight.shape[0]
    spans = boxes // SPAN
    peers = tracers // tracers_here
    f32, bf16 = jnp.float32, jnp.bfloat16
    shape = jax.ShapeDtypeStruct
    vmem = pl.BlockSpec(memory_space=pltpu.VMEM)
    smem = pl.BlockSpec(memory_space=pltpu.SMEM)
    hbm = pl.BlockSpec(memory_space=pltpu.HBM)
    lean = pltpu.CompilerParams(vmem_limit_bytes=VMEM_LIMIT)
    dma = pltpu.SemaphoreType.DMA
    core_index = lax.axis_index("core")
    x_index = lax.axis_index("x")
    ylo_index = lax.axis_index("ylo")
    ylo_size = lax.axis_size("ylo")
    joined = lax.axis_index("yhi") + ylo_index == 1
    groups = neighbour_groups(sizes)

    def in_hbm(array):
        return pltpu.with_memory_space_constraint(array, pltpu.HBM)

    copies = pl.pallas_call(
        pack_kernel,
        in_specs=[hbm] * 2,
        out_specs=hbm,
        out_shape=shape((peers, 1 + sections, tracers_here, boxes), f32),
        scratch_shapes=[pltpu.VMEM((1 + sections, tracers_here, boxes), f32), dma((2,)), dma((peers,))],
        compiler_params=lean,
        name="pack",
    )(in_hbm(cotangent), in_hbm(states))
    gathered = lax.all_to_all(copies, TRACER, split_axis=0, concat_axis=0, tiled=True)
    facts = jnp.concatenate(
        [tile_offset.reshape(-1), tile_count, jnp.stack([core_index, x_index]).astype(jnp.int32), wet_levels]
    )
    lent = pl.pallas_call(
        lend_kernel,
        in_specs=[smem, hbm],
        out_specs=vmem,
        out_shape=shape((boxes, boxes), f32),
        scratch_shapes=[pltpu.VMEM((boxes, boxes), bf16), dma],
        compiler_params=lean,
        name="lend",
    )(facts, in_hbm(explicit_tiles))
    borrowed = lax.ppermute(lent, "core", [(0, 1), (1, 0)])
    shared = pl.pallas_call(
        share_kernel,
        in_specs=[smem, hbm],
        out_specs=vmem,
        out_shape=shape((levels + 8, boxes), f32),
        scratch_shapes=[pltpu.VMEM((columns, levels, levels), f32), dma],
        compiler_params=lean,
        name="share",
    )(facts, in_hbm(implicit_inverse))
    shared = lax.all_gather(shared, "core")
    borrowed, blocks, wet = pl.pallas_call(
        blocks_kernel,
        in_specs=[smem] + [vmem] * 2,
        out_specs=[vmem] * 3,
        out_shape=[shape((boxes, boxes), bf16), shape((2, 2 * spans, SPAN, SPAN), bf16), shape((2, boxes), f32)],
        compiler_params=lean,
        name="blocks",
    )(facts, shared, borrowed)
    start, slopes = pl.pallas_call(
        gathered_kernel,
        in_specs=[vmem] * 2,
        out_specs=[vmem] * 2,
        out_shape=[shape((tracers, boxes), f32), shape((sections, tracers, boxes), f32)],
        compiler_params=lean,
        name="gathered",
    )(gathered, uptake_weight)
    adjoint = lax.all_gather(start, "core")
    uptake_t, release_t = uptake_weight.T, release_weight.T
    last_rows = ylo_size * tracers_here
    for section in range(sections - 1, -1, -1):
        first, last = section == sections - 1, section == 0

        def step(*refs, section=section, first=first, last=last):
            step_kernel(*refs, section=section, first=first, last=last)

        exchanged = 2 * last_rows if last else 2 * tracers
        send, keep = pl.pallas_call(
            step,
            in_specs=[smem] + [vmem] * 8,
            out_specs=[vmem] * 2,
            out_shape=[shape((exchanged, boxes), f32)] * 2,
            scratch_shapes=[
                pltpu.VMEM((2, tracers, boxes), f32),
                pltpu.VMEM((tracers // last_rows, last_rows, boxes), f32),
            ],
            compiler_params=lean,
        )(facts, adjoint, explicit_tiles, borrowed, blocks, wet, slopes, uptake_t, release_t)
        arrived = lax.all_gather(send, EVERY, axis_index_groups=groups)
        keep = keep + lax.dynamic_index_in_dim(arrived, core_index, 0, keepdims=False)
        adjoint = lax.all_gather(keep, "core")
    mine = lax.dynamic_index_in_dim(adjoint, core_index, 0, keepdims=False)[:last_rows]
    theirs = lax.dynamic_index_in_dim(adjoint, 1 - core_index, 0, keepdims=False)[last_rows:]
    result = (wet[0:1] * (mine + theirs)).reshape(ylo_size, tracers_here, boxes)
    passed = lax.dynamic_index_in_dim(result, 1 - ylo_index, 0, keepdims=False)
    passed = lax.dynamic_index_in_dim(lax.all_gather(passed, "ylo"), 1 - ylo_index, 0, keepdims=False)
    return jnp.where(joined, lax.dynamic_index_in_dim(result, ylo_index, 0, keepdims=False), passed)


def solution(mesh):
    regions, tracer_devices = mesh.devices.shape
    nq, nx, ny = regions // 2, tracer_devices // 2, 2
    fine = Mesh(mesh.devices.reshape(nq // 2, 2, 2, nx, ny), EVERY)
    placed = (
        P(TRACER, REGION),
        P(None, TRACER, REGION),
        P(REGION, None, None),
        P(REGION),
        P(REGION, None, None, None),
        P(REGION, None),
        P(REGION),
        P(),
        P(),
    )

    def body(*args):
        return local(*args, sizes=(nq, nx, ny))

    return jax.shard_map(body, mesh=fine, in_specs=placed, out_specs=P(TRACER, REGION), check_vma=False)
```

```python
import jax
import jax.numpy as jnp
from jax import lax
from jax.experimental import pallas as pl
from jax.experimental.pallas import tpu as pltpu
from jax.sharding import Mesh, PartitionSpec as P


REGION = ("z", "yhi", "core")
TRACER = ("x", "ylo")
EVERY = REGION + TRACER
SPAN = 128
VMEM_LIMIT = 8 * 2**20
OFFSETS_AT, COUNT_AT, CORE_AT, TRACER_AT, NEIGHBOUR_AT, WET_AT = 0, 5, 6, 7, 8, 9


def neighbour_groups(sizes):
    nq, nx, ny = sizes

    def at(chip, core, x, ylo):
        return (((chip % nq) * 2 + core) * nx + x) * ny + ylo

    groups = []
    for q in range(nq):
        for x in range(nx):
            joined, alone = (1, 0) if q % 2 == 0 else (0, 1)
            groups.append([at(q, 1, x, joined), at(q + 1, 0, x, 1 - joined)])
            groups.append([at(q, 1, x, alone), at(q, 0, x, alone)])
    return groups


def final_groups(sizes):
    nq, nx, ny = sizes

    def at(chip, core, x, ylo):
        return (((chip % nq) * 2 + core) * nx + x) * ny + ylo

    groups = []
    for q in range(nq):
        for x in range(nx):
            j = 1 if q % 2 == 0 else 0
            groups.append([at(q, 1, x, j), at(q + 1, 0, x, 1 - j), at(q, 1, x, 1 - j), at(q + 1, 0, x, j)])
    return groups


def halves(value):
    high = value.astype(jnp.bfloat16)
    low = (value - high.astype(jnp.float32)).astype(jnp.bfloat16)
    return high, low


def dot(a, b):
    return lax.dot_general(a, b, (((1,), (0,)), ((), ())), preferred_element_type=jnp.float32)


def dot_split(a_high, a_low, b_high, b_low):
    rows = a_high.shape[0]
    both = dot(jnp.concatenate([a_high, a_low], axis=0), b_high)
    return both[:rows] + both[rows:] + dot(a_high, b_low)


def slot_at(facts, slots, distance):
    slot = jnp.int32(0)
    for k in range(slots):
        slot = slot + jnp.where(facts[OFFSETS_AT + k] == distance, k, 0)
    return slot


def slot_live(facts, slots, distance):
    live = jnp.int32(0)
    for k in range(slots):
        live = live + jnp.where((facts[OFFSETS_AT + k] == distance) & (k < facts[COUNT_AT]), 1, 0)
    return live > 0


def away(facts):
    return 2 * facts[CORE_AT] - 1


def pack_kernel(cotangent, states, copies, buffer, fetched):
    first = pltpu.make_async_copy(cotangent, buffer.at[0], fetched.at[0])
    rest = pltpu.make_async_copy(states, buffer.at[pl.ds(1, states.shape[0])], fetched.at[1])
    first.start()
    rest.start()
    first.wait()
    rest.wait()
    for t in range(copies.shape[0]):
        copies[t] = buffer[...]


def lend_kernel(facts, tiles, lent, buffer, arrival):
    slots = tiles.shape[1]
    distance = -2 * away(facts)
    fetch = pltpu.make_async_copy(tiles.at[0, slot_at(facts, slots, distance)], buffer, arrival)
    fetch.start()
    fetch.wait()
    lent[...] = jnp.where(slot_live(facts, slots, distance), buffer[...].astype(jnp.float32), 0.0)


def share_kernel(facts, inverse_hbm, shared, inverse, arrival):
    fetch = pltpu.make_async_copy(inverse_hbm, inverse, arrival)
    fetch.start()
    fetch.wait()
    columns, levels, _ = inverse.shape
    lane = lax.broadcasted_iota(jnp.int32, (levels, levels), 1)
    row = lax.broadcasted_iota(jnp.int32, (8, levels), 1)
    for c in range(columns):
        at = slice(c * levels, (c + 1) * levels)
        shared[0:levels, at] = jnp.where(lane < facts[WET_AT + c], inverse[c], 0.0)
        shared[levels : levels + 8, at] = jnp.where(row < facts[WET_AT + c], 1.0, 0.0)


def gathered_kernel(facts, gathered, shared, uptake_weight, start, slopes, blocks, wet_out):
    peers, _, few, _ = gathered.shape
    for t in range(peers):
        at = slice(t * few, (t + 1) * few)
        start[at, :] = gathered[t, 0]
        for n in range(slopes.shape[0]):
            slopes[n, at, :] = gathered[t, 1 + n]
    weight_high, weight_low = halves(uptake_weight[...])
    for n in range(slopes.shape[0]):
        state_high, state_low = halves(slopes[n])
        reach = jnp.tanh(dot_split(weight_high, weight_low, state_high, state_low))
        slopes[n] = 1.0 - reach * reach
    own = facts[CORE_AT]
    levels = shared.shape[1] - 8
    boxes = shared.shape[2]
    spans = boxes // SPAN
    same = (
        lax.broadcasted_iota(jnp.int32, (SPAN, SPAN), 0) // levels
        == lax.broadcasted_iota(jnp.int32, (SPAN, SPAN), 1) // levels
    )
    for which in range(2):
        side = own if which == 0 else 1 - own
        for s in range(spans):
            high, low = halves(shared[side, 0:levels, s * SPAN : (s + 1) * SPAN])
            full_high = jnp.concatenate([high] * (SPAN // levels), axis=0)
            full_low = jnp.concatenate([low] * (SPAN // levels), axis=0)
            blocks[0, which * spans + s] = jnp.where(same, full_high, jnp.zeros_like(full_high))
            blocks[1, which * spans + s] = jnp.where(same, full_low, jnp.zeros_like(full_low))
        wet_out[which : which + 1, :] = shared[side, levels : levels + 1, :]


def step_kernel(
    facts, adjoint, tiles, borrowed, blocks, wet, slopes, uptake_t, release_t, *outputs, section, first, last,
):
    own = facts[CORE_AT]
    direction = away(facts)
    slots, boxes = tiles.shape[1], tiles.shape[3]
    tracers = uptake_t.shape[0]
    spans = boxes // SPAN
    if first:
        send, keep, tile_out, settled = outputs
        pair = (adjoint[own], adjoint[1 - own])
        tile_out[...] = borrowed[...].astype(jnp.bfloat16)
        borrowed = tile_out
    else:
        pair = (
            wet[0:1, :] * (adjoint[own, 0:tracers, :] + adjoint[1 - own, tracers:, :]),
            wet[1:2, :] * (adjoint[own, tracers:, :] + adjoint[1 - own, 0:tracers, :]),
        )
        if last:
            parcels, settled, send, keep = outputs
        else:
            send, keep, settled = outputs
    for which in range(2):
        high, low = halves(pair[which])
        for s in range(spans):
            at = slice(s * SPAN, (s + 1) * SPAN)
            k = which * spans + s
            settled[which, :, at] = dot_split(high[:, at], low[:, at], blocks[0, k], blocks[1, k])
    own_high, own_low = halves(settled[0])
    other = settled[1].astype(jnp.bfloat16)

    def term(distance):
        product = dot(own_high, tiles[0, slot_at(facts, slots, distance)])
        return jnp.where(slot_live(facts, slots, distance), product, 0.0)

    def put(out, part, value):
        if last:
            few = out.shape[2]
            for t in range(tracers // few):
                out[t, part] = value[t * few : (t + 1) * few]
        else:
            out[part * tracers : (part + 1) * tracers, :] = value

    put(send, 0, term(direction) + dot(other, borrowed[...]))
    put(send, 1, term(2 * direction))
    release_high, release_low = halves(release_t[...])
    pushed = slopes[section] * dot_split(release_high, release_low, own_high, own_low)
    pushed_high, pushed_low = halves(pushed)
    uptake_high, uptake_low = halves(uptake_t[...])
    put(keep, 0, term(0) + dot_split(uptake_high, uptake_low, pushed_high, pushed_low))
    put(keep, 1, term(-direction))
    if last:
        here, there = facts[TRACER_AT], facts[NEIGHBOUR_AT]
        upper = own == 1
        parcels[0] = jnp.where(upper, keep[here], send[there])
        parcels[1] = jnp.where(upper, send[there], keep[here])
        parcels[2] = jnp.where(upper, keep[there], send[here])
        parcels[3] = jnp.where(upper, send[here], keep[there])


def local(
    cotangent,
    states,
    implicit_inverse,
    wet_levels,
    explicit_tiles,
    tile_offset,
    tile_count,
    uptake_weight,
    release_weight,
    *,
    sizes,
):
    tracers_here, boxes = cotangent.shape
    sections = states.shape[0]
    columns, levels, _ = implicit_inverse.shape
    tracers = uptake_weight.shape[0]
    spans = boxes // SPAN
    peers = tracers // tracers_here
    f32, bf16 = jnp.float32, jnp.bfloat16
    shape = jax.ShapeDtypeStruct
    vmem = pl.BlockSpec(memory_space=pltpu.VMEM)
    smem = pl.BlockSpec(memory_space=pltpu.SMEM)
    hbm = pl.BlockSpec(memory_space=pltpu.HBM)
    lean = pltpu.CompilerParams(vmem_limit_bytes=VMEM_LIMIT)
    dma = pltpu.SemaphoreType.DMA
    core_index = lax.axis_index("core")
    ylo_index, ylo_size = lax.axis_index("ylo"), lax.axis_size("ylo")
    tracer_here = lax.axis_index("x") * ylo_size + ylo_index
    neighbour = tracer_here + 1 - 2 * ylo_index
    groups = neighbour_groups(sizes)

    def in_hbm(array):
        return pltpu.with_memory_space_constraint(array, pltpu.HBM)

    copies = pl.pallas_call(
        pack_kernel,
        in_specs=[hbm] * 2,
        out_specs=vmem,
        out_shape=shape((peers, 1 + sections, tracers_here, boxes), f32),
        scratch_shapes=[pltpu.VMEM((1 + sections, tracers_here, boxes), f32), dma((2,))],
        compiler_params=lean,
        name="pack",
    )(in_hbm(cotangent), in_hbm(states))
    gathered = lax.all_to_all(copies, TRACER, split_axis=0, concat_axis=0, tiled=True)
    facts = jnp.concatenate(
        [tile_offset.reshape(-1), tile_count, jnp.stack([core_index, tracer_here, neighbour]).astype(jnp.int32), wet_levels]
    )
    lent = pl.pallas_call(
        lend_kernel,
        in_specs=[smem, hbm],
        out_specs=vmem,
        out_shape=shape((boxes, boxes), f32),
        scratch_shapes=[pltpu.VMEM((boxes, boxes), bf16), dma],
        compiler_params=lean,
        name="lend",
    )(facts, in_hbm(explicit_tiles))
    borrowed = lax.ppermute(lent, "core", [(0, 1), (1, 0)])
    shared = pl.pallas_call(
        share_kernel,
        in_specs=[smem, hbm],
        out_specs=vmem,
        out_shape=shape((levels + 8, boxes), f32),
        scratch_shapes=[pltpu.VMEM((columns, levels, levels), f32), dma],
        compiler_params=lean,
        name="share",
    )(facts, in_hbm(implicit_inverse))
    shared = lax.all_gather(shared, "core")
    start, slopes, blocks, wet = pl.pallas_call(
        gathered_kernel,
        in_specs=[smem] + [vmem] * 3,
        out_specs=[vmem] * 4,
        out_shape=[
            shape((tracers, boxes), f32),
            shape((sections, tracers, boxes), f32),
            shape((2, 2 * spans, SPAN, SPAN), bf16),
            shape((2, boxes), f32),
        ],
        compiler_params=lean,
        name="gathered",
    )(facts, gathered, shared, uptake_weight)
    adjoint = lax.all_gather(start, "core")
    uptake_t, release_t = uptake_weight.T, release_weight.T
    for section in range(sections - 1, -1, -1):
        first, last = section == sections - 1, section == 0

        def step(*refs, section=section, first=first, last=last):
            step_kernel(*refs, section=section, first=first, last=last)

        pieces = pltpu.VMEM((peers, 2, tracers_here, boxes), f32)
        if last:
            out_shape = [shape((4, 2, tracers_here, boxes), f32)]
        else:
            out_shape = [shape((2 * tracers, boxes), f32)] * 2 + [shape((boxes, boxes), bf16)] * first
        results = pl.pallas_call(
            step,
            in_specs=[smem] + [vmem] * 8,
            out_specs=[vmem] * len(out_shape),
            out_shape=out_shape,
            scratch_shapes=[pltpu.VMEM((2, tracers, boxes), f32)] + [pieces] * (2 * last),
            compiler_params=lean,
        )(facts, adjoint, explicit_tiles, borrowed, blocks, wet, slopes, uptake_t, release_t)
        if last:
            parcels = lax.all_to_all(
                results[0], EVERY, split_axis=0, concat_axis=0, tiled=True, axis_index_groups=final_groups(sizes)
            )
            keep = parcels[0] + parcels[1]
        else:
            if first:
                borrowed = results[2]
            arrived = lax.all_gather(results[0], EVERY, axis_index_groups=groups)
            keep = results[1] + lax.dynamic_index_in_dim(arrived, core_index, 0, keepdims=False)
        adjoint = lax.all_gather(keep, "core")
    mine = lax.dynamic_index_in_dim(adjoint, core_index, 0, keepdims=False)[0]
    theirs = lax.dynamic_index_in_dim(adjoint, 1 - core_index, 0, keepdims=False)[1]
    return wet[0:1] * (mine + theirs)


def solution(mesh):
    regions, tracer_devices = mesh.devices.shape
    nq, nx, ny = regions // 2, tracer_devices // 2, 2
    fine = Mesh(mesh.devices.reshape(nq // 2, 2, 2, nx, ny), EVERY)
    placed = (
        P(TRACER, REGION),
        P(None, TRACER, REGION),
        P(REGION, None, None),
        P(REGION),
        P(REGION, None, None, None),
        P(REGION, None),
        P(REGION),
        P(),
        P(),
    )

    def body(*args):
        return local(*args, sizes=(nq, nx, ny))

    return jax.shard_map(body, mesh=fine, in_specs=placed, out_specs=P(TRACER, REGION), check_vma=False)
```

```python
import jax
import jax.numpy as jnp
from jax import lax
from jax.experimental import pallas as pl
from jax.experimental.pallas import tpu as pltpu
from jax.sharding import Mesh, PartitionSpec as P


REGION = ("z", "yhi", "core")
TRACER = ("x", "ylo")
EVERY = REGION + TRACER
SPAN = 256
VMEM_LIMIT = 8 * 2**20
COUNT_AT, CORE_AT, X_AT = 5, 6, 7


def neighbour_groups(sizes):
    nq, nx, ny = sizes

    def at(chip, core, x, ylo):
        return (((chip % nq) * 2 + core) * nx + x) * ny + ylo

    groups = []
    for q in range(nq):
        for x in range(nx):
            joined, alone = (1, 0) if q % 2 == 0 else (0, 1)
            groups.append([at(q, 1, x, joined), at(q + 1, 0, x, 1 - joined)])
            groups.append([at(q, 1, x, alone), at(q, 0, x, alone)])
    return groups


def halves(value):
    high = value.astype(jnp.bfloat16)
    low = (value - high.astype(jnp.float32)).astype(jnp.bfloat16)
    return high, low


def dot(a, b):
    return lax.dot_general(a, b, (((1,), (0,)), ((), ())), preferred_element_type=jnp.float32)


def dot_split(a_high, a_low, b_high, b_low):
    rows = a_high.shape[0]
    both = dot(jnp.concatenate([a_high, a_low], axis=0), b_high)
    return both[:rows] + both[rows:] + dot(a_high, b_low)


def slot_at(offsets, slots, distance):
    slot = jnp.int32(0)
    for k in range(slots):
        slot = slot + jnp.where(offsets[k] == distance, k, 0)
    return slot


def slot_live(offsets, count, slots, distance):
    live = jnp.int32(0)
    for k in range(slots):
        live = live + jnp.where((offsets[k] == distance) & (k < count), 1, 0)
    return live > 0


def pack_kernel(cotangent, states, copies, buffer, fetched):
    first = pltpu.make_async_copy(cotangent, buffer.at[0], fetched.at[0])
    rest = pltpu.make_async_copy(states, buffer.at[pl.ds(1, states.shape[0])], fetched.at[1])
    first.start()
    rest.start()
    first.wait()
    rest.wait()
    for t in range(copies.shape[0]):
        copies[t] = buffer[...]


def lend_kernel(core, count, offsets_hbm, wet_hbm, tiles, inverse_hbm, lent, shared, offsets, wet, buffer, inverse, arrival):
    fetches = [
        pltpu.make_async_copy(source, target, arrival.at[n])
        for n, (source, target) in enumerate(
            [(offsets_hbm, offsets), (wet_hbm, wet), (inverse_hbm, inverse)]
        )
    ]
    for fetch in fetches:
        fetch.start()
    fetches[0].wait()
    slots = tiles.shape[1]
    distance = -2 * (2 * core[0] - 1)
    tile = pltpu.make_async_copy(tiles.at[0, slot_at(offsets.at[0], slots, distance)], buffer, arrival.at[3])
    tile.start()
    for fetch in fetches[1:]:
        fetch.wait()
    columns, levels, _ = inverse.shape
    lane = lax.broadcasted_iota(jnp.int32, (levels, levels), 1)
    row = lax.broadcasted_iota(jnp.int32, (8, levels), 1)
    for c in range(columns):
        at = slice(c * levels, (c + 1) * levels)
        shared[0:levels, at] = jnp.where(lane < wet[c], inverse[c], 0.0)
        shared[levels : levels + 8, at] = jnp.where(row < wet[c], 1.0, 0.0)
    tile.wait()
    lent[...] = jnp.where(slot_live(offsets.at[0], count[0], slots, distance), buffer[...].astype(jnp.float32), 0.0)


def round_kernel(borrowed, tile_out):
    tile_out[...] = borrowed[...].astype(jnp.bfloat16)


def gathered_kernel(facts, gathered, shared, uptake_weight, start, slopes, blocks, wet_out):
    peers, _, few, _ = gathered.shape
    for t in range(peers):
        at = slice(t * few, (t + 1) * few)
        start[at, :] = gathered[t, 0]
        for n in range(slopes.shape[0]):
            slopes[n, at, :] = gathered[t, 1 + n]
    weight_high, weight_low = halves(uptake_weight[...])
    for n in range(slopes.shape[0]):
        state_high, state_low = halves(slopes[n])
        reach = jnp.tanh(dot_split(weight_high, weight_low, state_high, state_low))
        slopes[n] = 1.0 - reach * reach
    own = facts[CORE_AT]
    levels = shared.shape[1] - 8
    boxes = shared.shape[2]
    spans = boxes // SPAN
    same = (
        lax.broadcasted_iota(jnp.int32, (SPAN, SPAN), 0) // levels
        == lax.broadcasted_iota(jnp.int32, (SPAN, SPAN), 1) // levels
    )
    for which in range(2):
        side = own if which == 0 else 1 - own
        for s in range(spans):
            high, low = halves(shared[side, 0:levels, s * SPAN : (s + 1) * SPAN])
            full_high = jnp.concatenate([high] * (SPAN // levels), axis=0)
            full_low = jnp.concatenate([low] * (SPAN // levels), axis=0)
            blocks[0, which * spans + s] = jnp.where(same, full_high, jnp.zeros_like(full_high))
            blocks[1, which * spans + s] = jnp.where(same, full_low, jnp.zeros_like(full_low))
        wet_out[which : which + 1, :] = shared[side, levels : levels + 1, :]


def step_kernel(
    facts, adjoint, tiles, borrowed, blocks, wet, slopes, uptake_t, release_t, send, keep, settled, rows,
    *, section, first, last,
):
    own = facts[CORE_AT]
    direction = 2 * own - 1
    slots, boxes = tiles.shape[1], tiles.shape[3]
    tracers = uptake_t.shape[0]
    spans = boxes // SPAN
    if first:
        pair = (adjoint[own], adjoint[1 - own])
    else:
        pair = (
            wet[0:1, :] * (adjoint[own, 0:tracers, :] + adjoint[1 - own, tracers:, :]),
            wet[1:2, :] * (adjoint[own, tracers:, :] + adjoint[1 - own, 0:tracers, :]),
        )
    for which in range(2):
        high, low = halves(pair[which])
        for s in range(spans):
            at = slice(s * SPAN, (s + 1) * SPAN)
            k = which * spans + s
            settled[which, :, at] = dot_split(high[:, at], low[:, at], blocks[0, k], blocks[1, k])
    own_high, own_low = halves(settled[0])
    other = settled[1].astype(jnp.bfloat16)

    def term(distance):
        product = dot(own_high, tiles[0, slot_at(facts, slots, distance)])
        return jnp.where(slot_live(facts, facts[COUNT_AT], slots, distance), product, 0.0)

    def put(out, part, value):
        few = out.shape[0] // 2
        if last:
            for x in range(rows.shape[0]):
                rows[x] = value[x * few : (x + 1) * few]
            value = rows[facts[X_AT]]
        out[part * few : (part + 1) * few, :] = value

    put(send, 0, term(direction) + dot(other, borrowed[...]))
    put(send, 1, term(2 * direction))
    release_high, release_low = halves(release_t[...])
    pushed = slopes[section] * dot_split(release_high, release_low, own_high, own_low)
    pushed_high, pushed_low = halves(pushed)
    uptake_high, uptake_low = halves(uptake_t[...])
    put(keep, 0, term(0) + dot_split(uptake_high, uptake_low, pushed_high, pushed_low))
    put(keep, 1, term(-direction))


def local(
    cotangent,
    states,
    implicit_inverse,
    wet_levels,
    explicit_tiles,
    tile_offset,
    tile_count,
    uptake_weight,
    release_weight,
    *,
    sizes,
):
    tracers_here, boxes = cotangent.shape
    sections = states.shape[0]
    columns, levels, _ = implicit_inverse.shape
    tracers = uptake_weight.shape[0]
    spans = boxes // SPAN
    peers = tracers // tracers_here
    f32, bf16 = jnp.float32, jnp.bfloat16
    shape = jax.ShapeDtypeStruct
    vmem = pl.BlockSpec(memory_space=pltpu.VMEM)
    smem = pl.BlockSpec(memory_space=pltpu.SMEM)
    hbm = pl.BlockSpec(memory_space=pltpu.HBM)
    lean = pltpu.CompilerParams(vmem_limit_bytes=VMEM_LIMIT)
    dma = pltpu.SemaphoreType.DMA
    core_index = lax.axis_index("core")
    core = core_index.astype(jnp.int32).reshape(1)
    x_index = lax.axis_index("x").astype(jnp.int32).reshape(1)
    ylo_index, ylo_size = lax.axis_index("ylo"), lax.axis_size("ylo")
    joined = lax.axis_index("yhi") + ylo_index == 1
    groups = neighbour_groups(sizes)

    def in_hbm(array):
        return pltpu.with_memory_space_constraint(array, pltpu.HBM)

    copies = pl.pallas_call(
        pack_kernel,
        in_specs=[hbm] * 2,
        out_specs=vmem,
        out_shape=shape((peers, 1 + sections, tracers_here, boxes), f32),
        scratch_shapes=[pltpu.VMEM((1 + sections, tracers_here, boxes), f32), dma((2,))],
        compiler_params=lean,
        name="pack",
    )(in_hbm(cotangent), in_hbm(states))
    gathered = lax.all_to_all(copies, TRACER, split_axis=0, concat_axis=0, tiled=True)
    facts = jnp.concatenate([tile_offset.reshape(-1), tile_count, core, x_index])
    lent, shared = pl.pallas_call(
        lend_kernel,
        in_specs=[smem] * 2 + [hbm] * 4,
        out_specs=[vmem] * 2,
        out_shape=[shape((boxes, boxes), f32), shape((levels + 8, boxes), f32)],
        scratch_shapes=[
            pltpu.SMEM(tile_offset.shape, jnp.int32),
            pltpu.SMEM((columns,), jnp.int32),
            pltpu.VMEM((boxes, boxes), bf16),
            pltpu.VMEM((columns, levels, levels), f32),
            dma((4,)),
        ],
        compiler_params=lean,
        name="lend",
    )(core, tile_count, *map(in_hbm, (tile_offset, wet_levels, explicit_tiles, implicit_inverse)))
    borrowed = lax.ppermute(lent, "core", [(0, 1), (1, 0)])
    shared = lax.all_gather(shared, "core")
    borrowed = pl.pallas_call(
        round_kernel,
        in_specs=[vmem],
        out_specs=vmem,
        out_shape=shape((boxes, boxes), bf16),
        compiler_params=lean,
        name="round",
    )(borrowed)
    start, slopes, blocks, wet = pl.pallas_call(
        gathered_kernel,
        in_specs=[smem] + [vmem] * 3,
        out_specs=[vmem] * 4,
        out_shape=[
            shape((tracers, boxes), f32),
            shape((sections, tracers, boxes), f32),
            shape((2, 2 * spans, SPAN, SPAN), bf16),
            shape((2, boxes), f32),
        ],
        compiler_params=lean,
        name="gathered",
    )(facts, gathered, shared, uptake_weight)
    adjoint = lax.all_gather(start, "core")
    uptake_t, release_t = uptake_weight.T, release_weight.T
    last_rows = ylo_size * tracers_here
    for section in range(sections - 1, -1, -1):
        first, last = section == sections - 1, section == 0

        def step(*refs, section=section, first=first, last=last):
            step_kernel(*refs, section=section, first=first, last=last)

        exchanged = 2 * last_rows if last else 2 * tracers
        send, keep = pl.pallas_call(
            step,
            in_specs=[smem] + [vmem] * 8,
            out_specs=[vmem] * 2,
            out_shape=[shape((exchanged, boxes), f32)] * 2,
            scratch_shapes=[
                pltpu.VMEM((2, tracers, boxes), f32),
                pltpu.VMEM((tracers // last_rows, last_rows, boxes), f32),
            ],
            compiler_params=lean,
        )(facts, adjoint, explicit_tiles, borrowed, blocks, wet, slopes, uptake_t, release_t)
        arrived = lax.all_gather(send, EVERY, axis_index_groups=groups)
        keep = keep + lax.dynamic_index_in_dim(arrived, core_index, 0, keepdims=False)
        adjoint = lax.all_gather(keep, "core")
    mine = lax.dynamic_index_in_dim(adjoint, core_index, 0, keepdims=False)[:last_rows]
    theirs = lax.dynamic_index_in_dim(adjoint, 1 - core_index, 0, keepdims=False)[last_rows:]
    result = (wet[0:1] * (mine + theirs)).reshape(ylo_size, tracers_here, boxes)
    passed = lax.dynamic_index_in_dim(result, 1 - ylo_index, 0, keepdims=False)
    passed = lax.dynamic_index_in_dim(lax.all_gather(passed, "ylo"), 1 - ylo_index, 0, keepdims=False)
    return jnp.where(joined, lax.dynamic_index_in_dim(result, ylo_index, 0, keepdims=False), passed)


def solution(mesh):
    regions, tracer_devices = mesh.devices.shape
    nq, nx, ny = regions // 2, tracer_devices // 2, 2
    fine = Mesh(mesh.devices.reshape(nq // 2, 2, 2, nx, ny), EVERY)
    placed = (
        P(TRACER, REGION),
        P(None, TRACER, REGION),
        P(REGION, None, None),
        P(REGION),
        P(REGION, None, None, None),
        P(REGION, None),
        P(REGION),
        P(),
        P(),
    )

    def body(*args):
        return local(*args, sizes=(nq, nx, ny))

    return jax.shard_map(body, mesh=fine, in_specs=placed, out_specs=P(TRACER, REGION), check_vma=False)
```

```python
import jax
import jax.numpy as jnp
from jax import lax
from jax.experimental import pallas as pl
from jax.experimental.pallas import tpu as pltpu
from jax.sharding import Mesh, PartitionSpec as P


REGION = ("z", "yhi", "core")
TRACER = ("x", "ylo")
EVERY = REGION + TRACER
SPAN = 256
VMEM_LIMIT = 8 * 2**20
COUNT_AT, CORE_AT = 5, 6


def neighbour_groups(sizes):
    nq, nx, ny = sizes

    def at(chip, core, x, ylo):
        return (((chip % nq) * 2 + core) * nx + x) * ny + ylo

    groups = []
    for q in range(nq):
        for x in range(nx):
            joined, alone = (1, 0) if q % 2 == 0 else (0, 1)
            groups.append([at(q, 1, x, joined), at(q + 1, 0, x, 1 - joined)])
            groups.append([at(q, 1, x, alone), at(q, 0, x, alone)])
    return groups


def halves(value):
    high = value.astype(jnp.bfloat16)
    low = (value - high.astype(jnp.float32)).astype(jnp.bfloat16)
    return high, low


def dot(a, b):
    return lax.dot_general(a, b, (((1,), (0,)), ((), ())), preferred_element_type=jnp.float32)


def dot_split(a_high, a_low, b_high, b_low):
    rows = a_high.shape[0]
    both = dot(jnp.concatenate([a_high, a_low], axis=0), b_high)
    return both[:rows] + both[rows:] + dot(a_high, b_low)


def slot_at(offsets, slots, distance):
    slot = jnp.int32(0)
    for k in range(slots):
        slot = slot + jnp.where(offsets[k] == distance, k, 0)
    return slot


def slot_live(offsets, slots, distance):
    live = jnp.int32(0)
    for k in range(slots):
        live = live + jnp.where((offsets[k] == distance) & (k < offsets[COUNT_AT]), 1, 0)
    return live > 0


def pack_kernel(cotangent, states, copies, buffer, fetched):
    first = pltpu.make_async_copy(cotangent, buffer.at[0], fetched.at[0])
    rest = pltpu.make_async_copy(states, buffer.at[pl.ds(1, states.shape[0])], fetched.at[1])
    first.start()
    rest.start()
    first.wait()
    rest.wait()
    for t in range(copies.shape[0]):
        copies[t] = buffer[...]


def lend_kernel(facts, tiles, lent, buffer, arrival):
    slots = tiles.shape[1]
    distance = 2 - 4 * facts[CORE_AT]
    fetch = pltpu.make_async_copy(tiles.at[0, slot_at(facts, slots, distance)], buffer, arrival)
    fetch.start()
    fetch.wait()
    lent[...] = jnp.where(slot_live(facts, slots, distance), buffer[...].astype(jnp.float32), 0.0)


def arrange_kernel(facts, wet, tiles, inverse, ordered, shared, upper, arrival):
    slots = tiles.shape[1]
    direction = 2 * facts[CORE_AT] - 1
    uses = (direction, 2 * direction, 0, -direction)
    fetches = [
        pltpu.make_async_copy(tiles.at[0, slot_at(facts, slots, distance)], ordered.at[n], arrival.at[n])
        for n, distance in enumerate(uses)
    ]
    for fetch in fetches:
        fetch.start()
    columns, levels, _ = inverse.shape
    lane = lax.broadcasted_iota(jnp.int32, (levels, levels), 1)
    row = lax.broadcasted_iota(jnp.int32, (8, levels), 1)
    for c in range(columns):
        at = slice(c * levels, (c + 1) * levels)
        shared[0:levels, at] = jnp.where(lane < wet[c], inverse[c], 0.0)
        shared[levels : levels + 8, at] = jnp.where(row < wet[c], 1.0, 0.0)
    upper[...] = jnp.full(upper.shape, facts[CORE_AT], jnp.int32).astype(jnp.float32)
    for fetch in fetches:
        fetch.wait()
    for n, distance in enumerate(uses):

        @pl.when(jnp.logical_not(slot_live(facts, slots, distance)))
        def _():
            ordered[n] = jnp.zeros(ordered.shape[1:], ordered.dtype)


def round_kernel(borrowed, tile_out):
    tile_out[...] = borrowed[...].astype(jnp.bfloat16)


def gathered_kernel(gathered, shared, uptake_weight, start, slopes):
    peers, _, few, _ = gathered.shape
    tracers = uptake_weight.shape[0]
    start[tracers:, :] = shared[...]
    for t in range(peers):
        at = slice(t * few, (t + 1) * few)
        start[at, :] = gathered[t, 0]
        for n in range(slopes.shape[0]):
            slopes[n, at, :] = gathered[t, 1 + n]
    weight_high, weight_low = halves(uptake_weight[...])
    for n in range(slopes.shape[0]):
        state_high, state_low = halves(slopes[n])
        reach = jnp.tanh(dot_split(weight_high, weight_low, state_high, state_low))
        slopes[n] = 1.0 - reach * reach


def lay_out_blocks(adjoint, tracers, levels, blocks, wet):
    spans = adjoint.shape[2] // SPAN
    same = (
        lax.broadcasted_iota(jnp.int32, (SPAN, SPAN), 0) // levels
        == lax.broadcasted_iota(jnp.int32, (SPAN, SPAN), 1) // levels
    )
    for side in range(2):
        for s in range(spans):
            high, low = halves(adjoint[side, tracers : tracers + levels, s * SPAN : (s + 1) * SPAN])
            full_high = jnp.concatenate([high] * (SPAN // levels), axis=0)
            full_low = jnp.concatenate([low] * (SPAN // levels), axis=0)
            blocks[0, side * spans + s] = jnp.where(same, full_high, jnp.zeros_like(full_high))
            blocks[1, side * spans + s] = jnp.where(same, full_low, jnp.zeros_like(full_low))
        wet[side : side + 1, :] = adjoint[side, tracers + levels : tracers + levels + 1, :]


def step_kernel(adjoint, ordered, borrowed, upper, slopes, uptake_t, release_t, *rest, section, levels, first):
    tracers = uptake_t.shape[0]
    if first:
        send, keep, blocks, wet, settled = rest
        lay_out_blocks(adjoint, tracers, levels, blocks, wet)
        pair = (adjoint[0, 0:tracers, :], adjoint[1, 0:tracers, :])
    else:
        blocks, wet, send, keep, settled = rest
        pair = (
            wet[0:1, :] * (adjoint[0, 0:tracers, :] + adjoint[1, tracers:, :]),
            wet[1:2, :] * (adjoint[1, 0:tracers, :] + adjoint[0, tracers:, :]),
        )
    spans = adjoint.shape[2] // SPAN
    for side in range(2):
        high, low = halves(pair[side])
        for s in range(spans):
            at = slice(s * SPAN, (s + 1) * SPAN)
            k = side * spans + s
            settled[side, :, at] = dot_split(high[:, at], low[:, at], blocks[0, k], blocks[1, k])
    is_upper = upper[0:1, :] > 0.5
    own_high, own_low = halves(jnp.where(is_upper, settled[1], settled[0]))
    other = jnp.where(is_upper, settled[0], settled[1]).astype(jnp.bfloat16)
    send[0:tracers, :] = dot(own_high, ordered[0]) + dot(other, borrowed[...])
    send[tracers:, :] = dot(own_high, ordered[1])
    release_high, release_low = halves(release_t[...])
    pushed = slopes[section] * dot_split(release_high, release_low, own_high, own_low)
    pushed_high, pushed_low = halves(pushed)
    uptake_high, uptake_low = halves(uptake_t[...])
    keep[0:tracers, :] = dot(own_high, ordered[2]) + dot_split(uptake_high, uptake_low, pushed_high, pushed_low)
    keep[tracers:, :] = dot(own_high, ordered[3])


def local(
    cotangent,
    states,
    implicit_inverse,
    wet_levels,
    explicit_tiles,
    tile_offset,
    tile_count,
    uptake_weight,
    release_weight,
    *,
    sizes,
):
    tracers_here, boxes = cotangent.shape
    sections = states.shape[0]
    _, levels, _ = implicit_inverse.shape
    tracers = uptake_weight.shape[0]
    spans = boxes // SPAN
    peers = tracers // tracers_here
    f32, bf16 = jnp.float32, jnp.bfloat16
    shape = jax.ShapeDtypeStruct
    vmem = pl.BlockSpec(memory_space=pltpu.VMEM)
    smem = pl.BlockSpec(memory_space=pltpu.SMEM)
    hbm = pl.BlockSpec(memory_space=pltpu.HBM)
    lean = pltpu.CompilerParams(vmem_limit_bytes=VMEM_LIMIT)
    dma = pltpu.SemaphoreType.DMA
    core_index = lax.axis_index("core")
    core = core_index.astype(jnp.int32).reshape(1)
    ylo_index, ylo_size = lax.axis_index("ylo"), lax.axis_size("ylo")
    joined = lax.axis_index("yhi") + ylo_index == 1
    groups = neighbour_groups(sizes)

    def in_hbm(array):
        return pltpu.with_memory_space_constraint(array, pltpu.HBM)

    copies = pl.pallas_call(
        pack_kernel,
        in_specs=[hbm] * 2,
        out_specs=vmem,
        out_shape=shape((peers, 1 + sections, tracers_here, boxes), f32),
        scratch_shapes=[pltpu.VMEM((1 + sections, tracers_here, boxes), f32), dma((2,))],
        compiler_params=lean,
        name="pack",
    )(in_hbm(cotangent), in_hbm(states))
    gathered = lax.all_to_all(copies, TRACER, split_axis=0, concat_axis=0, tiled=True)
    facts = jnp.concatenate([tile_offset.reshape(-1), tile_count, core])
    lent = pl.pallas_call(
        lend_kernel,
        in_specs=[smem, hbm],
        out_specs=vmem,
        out_shape=shape((boxes, boxes), f32),
        scratch_shapes=[pltpu.VMEM((boxes, boxes), bf16), dma],
        compiler_params=lean,
        name="lend",
    )(facts, in_hbm(explicit_tiles))
    borrowed = lax.ppermute(lent, "core", [(0, 1), (1, 0)])
    ordered, shared, upper = pl.pallas_call(
        arrange_kernel,
        in_specs=[smem] * 2 + [hbm, vmem],
        out_specs=[vmem] * 3,
        out_shape=[
            shape((4, boxes, boxes), bf16),
            shape((levels + 8, boxes), f32),
            shape((8, boxes), f32),
        ],
        scratch_shapes=[dma((4,))],
        compiler_params=lean,
        name="arrange",
    )(facts, wet_levels, in_hbm(explicit_tiles), implicit_inverse)
    borrowed = pl.pallas_call(
        round_kernel,
        in_specs=[vmem],
        out_specs=vmem,
        out_shape=shape((boxes, boxes), bf16),
        compiler_params=lean,
        name="round",
    )(borrowed)
    start, slopes = pl.pallas_call(
        gathered_kernel,
        in_specs=[vmem] * 3,
        out_specs=[vmem] * 2,
        out_shape=[shape((tracers + levels + 8, boxes), f32), shape((sections, tracers, boxes), f32)],
        compiler_params=lean,
        name="gathered",
    )(gathered, shared, uptake_weight)
    adjoint = lax.all_gather(start, "core")
    uptake_t, release_t = uptake_weight.T, release_weight.T
    kept_shapes = [shape((2, 2 * spans, SPAN, SPAN), bf16), shape((2, boxes), f32)]
    kept = []
    for section in range(sections - 1, -1, -1):
        first = section == sections - 1

        def step(*refs, section=section, first=first):
            step_kernel(*refs, section=section, levels=levels, first=first)

        out_shape = [shape((2 * tracers, boxes), f32)] * 2 + kept_shapes * first
        send, keep, *made = pl.pallas_call(
            step,
            in_specs=[vmem] * (7 + len(kept)),
            out_specs=[vmem] * len(out_shape),
            out_shape=out_shape,
            scratch_shapes=[pltpu.VMEM((2, tracers, boxes), f32)],
            compiler_params=lean,
        )(adjoint, ordered, borrowed, upper, slopes, uptake_t, release_t, *kept)
        kept = made or kept
        if section == 0:
            rows = ylo_size * tracers_here
            at = (0, lax.axis_index("x") * rows, 0)
            send, keep = (
                lax.dynamic_slice(part.reshape(2, tracers, boxes), at, (2, rows, boxes)).reshape(2 * rows, boxes)
                for part in (send, keep)
            )
        arrived = lax.all_gather(send, EVERY, axis_index_groups=groups)
        keep = keep + lax.dynamic_index_in_dim(arrived, core_index, 0, keepdims=False)
        adjoint = lax.all_gather(keep, "core")
    mine = lax.dynamic_index_in_dim(adjoint, core_index, 0, keepdims=False)[:rows]
    theirs = lax.dynamic_index_in_dim(adjoint, 1 - core_index, 0, keepdims=False)[rows:]
    wet = lax.dynamic_index_in_dim(kept[1], core_index, 0, keepdims=True)
    result = (wet * (mine + theirs)).reshape(ylo_size, tracers_here, boxes)
    passed = lax.dynamic_index_in_dim(result, 1 - ylo_index, 0, keepdims=False)
    passed = lax.dynamic_index_in_dim(lax.all_gather(passed, "ylo"), 1 - ylo_index, 0, keepdims=False)
    return jnp.where(joined, lax.dynamic_index_in_dim(result, ylo_index, 0, keepdims=False), passed)


def solution(mesh):
    regions, tracer_devices = mesh.devices.shape
    nq, nx, ny = regions // 2, tracer_devices // 2, 2
    fine = Mesh(mesh.devices.reshape(nq // 2, 2, 2, nx, ny), EVERY)
    placed = (
        P(TRACER, REGION),
        P(None, TRACER, REGION),
        P(REGION, None, None),
        P(REGION),
        P(REGION, None, None, None),
        P(REGION, None),
        P(REGION),
        P(),
        P(),
    )

    def body(*args):
        return local(*args, sizes=(nq, nx, ny))

    return jax.shard_map(body, mesh=fine, in_specs=placed, out_specs=P(TRACER, REGION), check_vma=False)
```

```python
import jax
import jax.numpy as jnp
from jax import lax
from jax.experimental import pallas as pl
from jax.experimental.pallas import tpu as pltpu
from jax.sharding import Mesh, PartitionSpec as P


REGION = ("z", "yhi", "core")
TRACER = ("x", "ylo")
EVERY = REGION + TRACER
SPAN = 256
VMEM_LIMIT = 8 * 2**20
COUNT_AT, CORE_AT = 5, 6


def neighbour_groups(sizes):
    nq, nx, ny = sizes

    def at(chip, core, x, ylo):
        return (((chip % nq) * 2 + core) * nx + x) * ny + ylo

    groups = []
    for q in range(nq):
        for x in range(nx):
            joined, alone = (1, 0) if q % 2 == 0 else (0, 1)
            groups.append([at(q, 1, x, joined), at(q + 1, 0, x, 1 - joined)])
            groups.append([at(q, 1, x, alone), at(q, 0, x, alone)])
    return groups


def halves(value):
    high = value.astype(jnp.bfloat16)
    low = (value - high.astype(jnp.float32)).astype(jnp.bfloat16)
    return high, low


def dot(a, b):
    return lax.dot_general(a, b, (((1,), (0,)), ((), ())), preferred_element_type=jnp.float32)


def dot_split(a_high, a_low, b_high, b_low):
    rows = a_high.shape[0]
    both = dot(jnp.concatenate([a_high, a_low], axis=0), b_high)
    return both[:rows] + both[rows:] + dot(a_high, b_low)


def slot_at(offsets, slots, distance):
    slot = jnp.int32(0)
    for k in range(slots):
        slot = slot + jnp.where(offsets[k] == distance, k, 0)
    return slot


def slot_live(offsets, slots, distance):
    live = jnp.int32(0)
    for k in range(slots):
        live = live + jnp.where((offsets[k] == distance) & (k < offsets[COUNT_AT]), 1, 0)
    return live > 0


def open_kernel(cotangent, states, inverse_hbm, wet_hbm, copies, shared, buffer, inverse, wet, arrival):
    pairs = [
        (cotangent, buffer.at[0]),
        (states, buffer.at[pl.ds(1, states.shape[0])]),
        (wet_hbm, wet),
        (inverse_hbm, inverse),
    ]
    fetches = [pltpu.make_async_copy(source, target, arrival.at[n]) for n, (source, target) in enumerate(pairs)]
    for fetch in fetches:
        fetch.start()
    for fetch in fetches[:2]:
        fetch.wait()
    for t in range(copies.shape[0]):
        copies[t] = buffer[...]
    for fetch in fetches[2:]:
        fetch.wait()
    columns, levels, _ = inverse.shape
    lane = lax.broadcasted_iota(jnp.int32, (levels, levels), 1)
    row = lax.broadcasted_iota(jnp.int32, (8, levels), 1)
    for c in range(columns):
        at = slice(c * levels, (c + 1) * levels)
        shared[0:levels, at] = jnp.where(lane < wet[c], inverse[c], 0.0)
        shared[levels : levels + 8, at] = jnp.where(row < wet[c], 1.0, 0.0)


def lend_kernel(facts, tiles, lent, ordered, upper, buffer, arrival):
    slots = tiles.shape[1]
    core = facts[CORE_AT]
    direction = 2 * core - 1
    uses = (-2 * direction, direction, 2 * direction, 0, -direction)
    fetches = [
        pltpu.make_async_copy(
            tiles.at[0, slot_at(facts, slots, distance)], ordered.at[n - 1] if n else buffer, arrival.at[n]
        )
        for n, distance in enumerate(uses)
    ]
    for fetch in fetches:
        fetch.start()
    upper[...] = jnp.full(upper.shape, core, jnp.int32).astype(jnp.float32)
    fetches[0].wait()
    lent[...] = jnp.where(slot_live(facts, slots, uses[0]), buffer[...].astype(jnp.float32), 0.0)
    for n, distance in enumerate(uses[1:]):
        fetches[n + 1].wait()

        @pl.when(jnp.logical_not(slot_live(facts, slots, distance)))
        def _():
            ordered[n] = jnp.zeros(ordered.shape[1:], ordered.dtype)


def round_kernel(borrowed, tile_out):
    tile_out[...] = borrowed[...].astype(jnp.bfloat16)


def gathered_kernel(gathered, shared, uptake_weight, start, slopes):
    peers, _, few, _ = gathered.shape
    tracers = uptake_weight.shape[0]
    start[tracers:, :] = shared[...]
    for t in range(peers):
        at = slice(t * few, (t + 1) * few)
        start[at, :] = gathered[t, 0]
        for n in range(slopes.shape[0]):
            slopes[n, at, :] = gathered[t, 1 + n]
    weight_high, weight_low = halves(uptake_weight[...])
    for n in range(slopes.shape[0]):
        state_high, state_low = halves(slopes[n])
        reach = jnp.tanh(dot_split(weight_high, weight_low, state_high, state_low))
        slopes[n] = 1.0 - reach * reach


def lay_out_blocks(adjoint, tracers, levels, blocks, wet):
    spans = adjoint.shape[2] // SPAN
    same = (
        lax.broadcasted_iota(jnp.int32, (SPAN, SPAN), 0) // levels
        == lax.broadcasted_iota(jnp.int32, (SPAN, SPAN), 1) // levels
    )
    for side in range(2):
        for s in range(spans):
            high, low = halves(adjoint[side, tracers : tracers + levels, s * SPAN : (s + 1) * SPAN])
            full_high = jnp.concatenate([high] * (SPAN // levels), axis=0)
            full_low = jnp.concatenate([low] * (SPAN // levels), axis=0)
            blocks[0, side * spans + s] = jnp.where(same, full_high, jnp.zeros_like(full_high))
            blocks[1, side * spans + s] = jnp.where(same, full_low, jnp.zeros_like(full_low))
        wet[side : side + 1, :] = adjoint[side, tracers + levels : tracers + levels + 1, :]


def step_kernel(adjoint, ordered, borrowed, upper, slopes, uptake_t, release_t, *rest, section, levels, first):
    tracers = uptake_t.shape[0]
    if first:
        send, keep, blocks, wet, settled = rest
        lay_out_blocks(adjoint, tracers, levels, blocks, wet)
        pair = (adjoint[0, 0:tracers, :], adjoint[1, 0:tracers, :])
    else:
        blocks, wet, send, keep, settled = rest
        pair = (
            wet[0:1, :] * (adjoint[0, 0:tracers, :] + adjoint[1, tracers:, :]),
            wet[1:2, :] * (adjoint[1, 0:tracers, :] + adjoint[0, tracers:, :]),
        )
    spans = adjoint.shape[2] // SPAN
    for side in range(2):
        high, low = halves(pair[side])
        for s in range(spans):
            at = slice(s * SPAN, (s + 1) * SPAN)
            k = side * spans + s
            settled[side, :, at] = dot_split(high[:, at], low[:, at], blocks[0, k], blocks[1, k])
    is_upper = upper[0:1, :] > 0.5
    own_high, own_low = halves(jnp.where(is_upper, settled[1], settled[0]))
    other = jnp.where(is_upper, settled[0], settled[1]).astype(jnp.bfloat16)
    send[0:tracers, :] = dot(own_high, ordered[0]) + dot(other, borrowed[...])
    send[tracers:, :] = dot(own_high, ordered[1])
    release_high, release_low = halves(release_t[...])
    pushed = slopes[section] * dot_split(release_high, release_low, own_high, own_low)
    pushed_high, pushed_low = halves(pushed)
    uptake_high, uptake_low = halves(uptake_t[...])
    keep[0:tracers, :] = dot(own_high, ordered[2]) + dot_split(uptake_high, uptake_low, pushed_high, pushed_low)
    keep[tracers:, :] = dot(own_high, ordered[3])


def local(
    cotangent,
    states,
    implicit_inverse,
    wet_levels,
    explicit_tiles,
    tile_offset,
    tile_count,
    uptake_weight,
    release_weight,
    *,
    sizes,
):
    tracers_here, boxes = cotangent.shape
    sections = states.shape[0]
    _, levels, _ = implicit_inverse.shape
    tracers = uptake_weight.shape[0]
    spans = boxes // SPAN
    peers = tracers // tracers_here
    f32, bf16 = jnp.float32, jnp.bfloat16
    shape = jax.ShapeDtypeStruct
    vmem = pl.BlockSpec(memory_space=pltpu.VMEM)
    smem = pl.BlockSpec(memory_space=pltpu.SMEM)
    hbm = pl.BlockSpec(memory_space=pltpu.HBM)
    lean = pltpu.CompilerParams(vmem_limit_bytes=VMEM_LIMIT)
    dma = pltpu.SemaphoreType.DMA
    core_index = lax.axis_index("core")
    core = core_index.astype(jnp.int32).reshape(1)
    ylo_index, ylo_size = lax.axis_index("ylo"), lax.axis_size("ylo")
    joined = lax.axis_index("yhi") + ylo_index == 1
    groups = neighbour_groups(sizes)

    def in_hbm(array):
        return pltpu.with_memory_space_constraint(array, pltpu.HBM)

    copies, shared = pl.pallas_call(
        open_kernel,
        in_specs=[hbm] * 4,
        out_specs=[vmem] * 2,
        out_shape=[
            shape((peers, 1 + sections, tracers_here, boxes), f32),
            shape((levels + 8, boxes), f32),
        ],
        scratch_shapes=[
            pltpu.VMEM((1 + sections, tracers_here, boxes), f32),
            pltpu.VMEM(implicit_inverse.shape, f32),
            pltpu.SMEM(wet_levels.shape, jnp.int32),
            dma((4,)),
        ],
        compiler_params=lean,
        name="open",
    )(*map(in_hbm, (cotangent, states, implicit_inverse, wet_levels)))
    gathered = lax.all_to_all(copies, TRACER, split_axis=0, concat_axis=0, tiled=True)
    facts = jnp.concatenate([tile_offset.reshape(-1), tile_count, core])
    lent, ordered, upper = pl.pallas_call(
        lend_kernel,
        in_specs=[smem, hbm],
        out_specs=[vmem] * 3,
        out_shape=[shape((boxes, boxes), f32), shape((4, boxes, boxes), bf16), shape((8, boxes), f32)],
        scratch_shapes=[pltpu.VMEM((boxes, boxes), bf16), dma((5,))],
        compiler_params=lean,
        name="lend",
    )(facts, in_hbm(explicit_tiles))
    borrowed = lax.ppermute(lent, "core", [(0, 1), (1, 0)])
    borrowed = pl.pallas_call(
        round_kernel,
        in_specs=[vmem],
        out_specs=vmem,
        out_shape=shape((boxes, boxes), bf16),
        compiler_params=lean,
        name="round",
    )(borrowed)
    start, slopes = pl.pallas_call(
        gathered_kernel,
        in_specs=[vmem] * 3,
        out_specs=[vmem] * 2,
        out_shape=[shape((tracers + levels + 8, boxes), f32), shape((sections, tracers, boxes), f32)],
        compiler_params=lean,
        name="gathered",
    )(gathered, shared, uptake_weight)
    adjoint = lax.all_gather(start, "core")
    uptake_t, release_t = uptake_weight.T, release_weight.T
    kept_shapes = [shape((2, 2 * spans, SPAN, SPAN), bf16), shape((2, boxes), f32)]
    kept = []
    for section in range(sections - 1, -1, -1):
        first = section == sections - 1

        def step(*refs, section=section, first=first):
            step_kernel(*refs, section=section, levels=levels, first=first)

        out_shape = [shape((2 * tracers, boxes), f32)] * 2 + kept_shapes * first
        send, keep, *made = pl.pallas_call(
            step,
            in_specs=[vmem] * (7 + len(kept)),
            out_specs=[vmem] * len(out_shape),
            out_shape=out_shape,
            scratch_shapes=[pltpu.VMEM((2, tracers, boxes), f32)],
            compiler_params=lean,
        )(adjoint, ordered, borrowed, upper, slopes, uptake_t, release_t, *kept)
        kept = made or kept
        if section == 0:
            rows = ylo_size * tracers_here
            at = (0, lax.axis_index("x") * rows, 0)
            send, keep = (
                lax.dynamic_slice(part.reshape(2, tracers, boxes), at, (2, rows, boxes)).reshape(2 * rows, boxes)
                for part in (send, keep)
            )
        arrived = lax.all_gather(send, EVERY, axis_index_groups=groups)
        keep = keep + lax.dynamic_index_in_dim(arrived, core_index, 0, keepdims=False)
        adjoint = lax.all_gather(keep, "core")
    mine = lax.dynamic_index_in_dim(adjoint, core_index, 0, keepdims=False)[:rows]
    theirs = lax.dynamic_index_in_dim(adjoint, 1 - core_index, 0, keepdims=False)[rows:]
    wet = lax.dynamic_index_in_dim(kept[1], core_index, 0, keepdims=True)
    result = (wet * (mine + theirs)).reshape(ylo_size, tracers_here, boxes)
    passed = lax.dynamic_index_in_dim(result, 1 - ylo_index, 0, keepdims=False)
    passed = lax.dynamic_index_in_dim(lax.all_gather(passed, "ylo"), 1 - ylo_index, 0, keepdims=False)
    return jnp.where(joined, lax.dynamic_index_in_dim(result, ylo_index, 0, keepdims=False), passed)


def solution(mesh):
    regions, tracer_devices = mesh.devices.shape
    nq, nx, ny = regions // 2, tracer_devices // 2, 2
    fine = Mesh(mesh.devices.reshape(nq // 2, 2, 2, nx, ny), EVERY)
    placed = (
        P(TRACER, REGION),
        P(None, TRACER, REGION),
        P(REGION, None, None),
        P(REGION),
        P(REGION, None, None, None),
        P(REGION, None),
        P(REGION),
        P(),
        P(),
    )

    def body(*args):
        return local(*args, sizes=(nq, nx, ny))

    return jax.shard_map(body, mesh=fine, in_specs=placed, out_specs=P(TRACER, REGION), check_vma=False)
```

```python
import jax
import jax.numpy as jnp
from jax import lax
from jax.experimental import pallas as pl
from jax.experimental.pallas import tpu as pltpu
from jax.sharding import Mesh, PartitionSpec as P


REGION = ("z", "yhi", "core")
TRACER = ("x", "ylo")
EVERY = REGION + TRACER
SPAN = 256
VMEM_LIMIT = 8 * 2**20
COUNT_AT, CORE_AT = 5, 6


def neighbour_groups(sizes):
    nq, nx, ny = sizes

    def at(chip, core, x, ylo):
        return (((chip % nq) * 2 + core) * nx + x) * ny + ylo

    groups = []
    for q in range(nq):
        for x in range(nx):
            joined, alone = (1, 0) if q % 2 == 0 else (0, 1)
            groups.append([at(q, 1, x, joined), at(q + 1, 0, x, 1 - joined)])
            groups.append([at(q, 1, x, alone), at(q, 0, x, alone)])
    return groups


def halves(value):
    high = value.astype(jnp.bfloat16)
    low = (value - high.astype(jnp.float32)).astype(jnp.bfloat16)
    return high, low


def dot(a, b):
    return lax.dot_general(a, b, (((1,), (0,)), ((), ())), preferred_element_type=jnp.float32)


def dot_split(a_high, a_low, b_high, b_low):
    rows = a_high.shape[0]
    both = dot(jnp.concatenate([a_high, a_low], axis=0), b_high)
    return both[:rows] + both[rows:] + dot(a_high, b_low)


def slot_at(offsets, slots, distance):
    slot = jnp.int32(0)
    for k in range(slots):
        slot = slot + jnp.where(offsets[k] == distance, k, 0)
    return slot


def slot_live(offsets, slots, distance):
    live = jnp.int32(0)
    for k in range(slots):
        live = live + jnp.where((offsets[k] == distance) & (k < offsets[COUNT_AT]), 1, 0)
    return live > 0


def pack_kernel(cotangent, states, copies, buffer, fetched):
    first = pltpu.make_async_copy(cotangent, buffer.at[0], fetched.at[0])
    rest = pltpu.make_async_copy(states, buffer.at[pl.ds(1, states.shape[0])], fetched.at[1])
    first.start()
    rest.start()
    first.wait()
    rest.wait()
    for t in range(copies.shape[0]):
        copies[t] = buffer[...]


def lend_kernel(offsets_hbm, tiles, lent, offsets, buffer, arrival):
    ask = pltpu.make_async_copy(offsets_hbm, offsets, arrival.at[0])
    ask.start()
    ask.wait()
    distance = 2 - 4 * lax.axis_index("core")
    fetch = pltpu.make_async_copy(tiles.at[0, slot_at(offsets.at[0], tiles.shape[1], distance)], buffer, arrival.at[1])
    fetch.start()
    fetch.wait()
    lent[...] = buffer[...].astype(jnp.float32)


def arrange_kernel(facts, wet, tiles, inverse, ordered, shared, upper, arrival):
    slots = tiles.shape[1]
    direction = 2 * facts[CORE_AT] - 1
    uses = (direction, 2 * direction, 0, -direction)
    fetches = [
        pltpu.make_async_copy(tiles.at[0, slot_at(facts, slots, distance)], ordered.at[n], arrival.at[n])
        for n, distance in enumerate(uses)
    ]
    for fetch in fetches:
        fetch.start()
    columns, levels, _ = inverse.shape
    lane = lax.broadcasted_iota(jnp.int32, (levels, levels), 1)
    row = lax.broadcasted_iota(jnp.int32, (8, levels), 1)
    for c in range(columns):
        at = slice(c * levels, (c + 1) * levels)
        shared[0:levels, at] = jnp.where(lane < wet[c], inverse[c], 0.0)
        shared[levels : levels + 8, at] = jnp.where(row < wet[c], 1.0, 0.0)
    lending = jnp.where(slot_live(facts, slots, -2 * direction), 1.0, 0.0)
    shared[levels + 4 :, :] = jnp.full((4, shared.shape[1]), lending, jnp.float32)
    upper[...] = jnp.full(upper.shape, facts[CORE_AT], jnp.int32).astype(jnp.float32)
    for fetch in fetches:
        fetch.wait()
    for n, distance in enumerate(uses):

        @pl.when(jnp.logical_not(slot_live(facts, slots, distance)))
        def _():
            ordered[n] = jnp.zeros(ordered.shape[1:], ordered.dtype)


def round_kernel(borrowed, tile_out):
    tile_out[...] = borrowed[...].astype(jnp.bfloat16)


def gathered_kernel(gathered, shared, uptake_weight, start, slopes):
    peers, _, few, _ = gathered.shape
    tracers = uptake_weight.shape[0]
    start[tracers:, :] = shared[...]
    for t in range(peers):
        at = slice(t * few, (t + 1) * few)
        start[at, :] = gathered[t, 0]
        for n in range(slopes.shape[0]):
            slopes[n, at, :] = gathered[t, 1 + n]
    weight_high, weight_low = halves(uptake_weight[...])
    for n in range(slopes.shape[0]):
        state_high, state_low = halves(slopes[n])
        reach = jnp.tanh(dot_split(weight_high, weight_low, state_high, state_low))
        slopes[n] = 1.0 - reach * reach


def lay_out_blocks(adjoint, tracers, levels, blocks, wet):
    spans = adjoint.shape[2] // SPAN
    same = (
        lax.broadcasted_iota(jnp.int32, (SPAN, SPAN), 0) // levels
        == lax.broadcasted_iota(jnp.int32, (SPAN, SPAN), 1) // levels
    )
    for side in range(2):
        for s in range(spans):
            high, low = halves(adjoint[side, tracers : tracers + levels, s * SPAN : (s + 1) * SPAN])
            full_high = jnp.concatenate([high] * (SPAN // levels), axis=0)
            full_low = jnp.concatenate([low] * (SPAN // levels), axis=0)
            blocks[0, side * spans + s] = jnp.where(same, full_high, jnp.zeros_like(full_high))
            blocks[1, side * spans + s] = jnp.where(same, full_low, jnp.zeros_like(full_low))
        wet[side : side + 1, :] = adjoint[side, tracers + levels : tracers + levels + 1, :]
        wet[2 + side : 3 + side, :] = adjoint[side, tracers + levels + 4 : tracers + levels + 5, :]


def step_kernel(adjoint, ordered, borrowed, upper, slopes, uptake_t, release_t, *rest, section, levels, first):
    tracers = uptake_t.shape[0]
    if first:
        send, keep, blocks, wet, settled = rest
        lay_out_blocks(adjoint, tracers, levels, blocks, wet)
        pair = (adjoint[0, 0:tracers, :], adjoint[1, 0:tracers, :])
    else:
        blocks, wet, send, keep, settled = rest
        pair = (
            wet[0:1, :] * (adjoint[0, 0:tracers, :] + adjoint[1, tracers:, :]),
            wet[1:2, :] * (adjoint[1, 0:tracers, :] + adjoint[0, tracers:, :]),
        )
    spans = adjoint.shape[2] // SPAN
    for side in range(2):
        high, low = halves(pair[side])
        for s in range(spans):
            at = slice(s * SPAN, (s + 1) * SPAN)
            k = side * spans + s
            settled[side, :, at] = dot_split(high[:, at], low[:, at], blocks[0, k], blocks[1, k])
    is_upper = upper[0:1, :] > 0.5
    own_high, own_low = halves(jnp.where(is_upper, settled[1], settled[0]))
    other = jnp.where(is_upper, wet[2:3, :] * settled[0], wet[3:4, :] * settled[1]).astype(jnp.bfloat16)
    send[0:tracers, :] = dot(own_high, ordered[0]) + dot(other, borrowed[...])
    send[tracers:, :] = dot(own_high, ordered[1])
    release_high, release_low = halves(release_t[...])
    pushed = slopes[section] * dot_split(release_high, release_low, own_high, own_low)
    pushed_high, pushed_low = halves(pushed)
    uptake_high, uptake_low = halves(uptake_t[...])
    keep[0:tracers, :] = dot(own_high, ordered[2]) + dot_split(uptake_high, uptake_low, pushed_high, pushed_low)
    keep[tracers:, :] = dot(own_high, ordered[3])


def local(
    cotangent,
    states,
    implicit_inverse,
    wet_levels,
    explicit_tiles,
    tile_offset,
    tile_count,
    uptake_weight,
    release_weight,
    *,
    sizes,
):
    tracers_here, boxes = cotangent.shape
    sections = states.shape[0]
    _, levels, _ = implicit_inverse.shape
    tracers = uptake_weight.shape[0]
    spans = boxes // SPAN
    peers = tracers // tracers_here
    f32, bf16 = jnp.float32, jnp.bfloat16
    shape = jax.ShapeDtypeStruct
    vmem = pl.BlockSpec(memory_space=pltpu.VMEM)
    smem = pl.BlockSpec(memory_space=pltpu.SMEM)
    hbm = pl.BlockSpec(memory_space=pltpu.HBM)
    lean = pltpu.CompilerParams(vmem_limit_bytes=VMEM_LIMIT)
    dma = pltpu.SemaphoreType.DMA
    core_index = lax.axis_index("core")
    core = core_index.astype(jnp.int32).reshape(1)
    ylo_index, ylo_size = lax.axis_index("ylo"), lax.axis_size("ylo")
    joined = lax.axis_index("yhi") + ylo_index == 1
    groups = neighbour_groups(sizes)

    def in_hbm(array):
        return pltpu.with_memory_space_constraint(array, pltpu.HBM)

    copies = pl.pallas_call(
        pack_kernel,
        in_specs=[hbm] * 2,
        out_specs=vmem,
        out_shape=shape((peers, 1 + sections, tracers_here, boxes), f32),
        scratch_shapes=[pltpu.VMEM((1 + sections, tracers_here, boxes), f32), dma((2,))],
        compiler_params=lean,
        name="pack",
    )(in_hbm(cotangent), in_hbm(states))
    gathered = lax.all_to_all(copies, TRACER, split_axis=0, concat_axis=0, tiled=True)
    facts = jnp.concatenate([tile_offset.reshape(-1), tile_count, core])
    lent = pl.pallas_call(
        lend_kernel,
        in_specs=[hbm] * 2,
        out_specs=vmem,
        out_shape=shape((boxes, boxes), f32),
        scratch_shapes=[pltpu.SMEM(tile_offset.shape, jnp.int32), pltpu.VMEM((boxes, boxes), bf16), dma((2,))],
        compiler_params=lean,
        name="lend",
    )(in_hbm(tile_offset), in_hbm(explicit_tiles))
    borrowed = lax.ppermute(lent, "core", [(0, 1), (1, 0)])
    ordered, shared, upper = pl.pallas_call(
        arrange_kernel,
        in_specs=[smem] * 2 + [hbm, vmem],
        out_specs=[vmem] * 3,
        out_shape=[
            shape((4, boxes, boxes), bf16),
            shape((levels + 8, boxes), f32),
            shape((8, boxes), f32),
        ],
        scratch_shapes=[dma((4,))],
        compiler_params=lean,
        name="arrange",
    )(facts, wet_levels, in_hbm(explicit_tiles), implicit_inverse)
    borrowed = pl.pallas_call(
        round_kernel,
        in_specs=[vmem],
        out_specs=vmem,
        out_shape=shape((boxes, boxes), bf16),
        compiler_params=lean,
        name="round",
    )(borrowed)
    start, slopes = pl.pallas_call(
        gathered_kernel,
        in_specs=[vmem] * 3,
        out_specs=[vmem] * 2,
        out_shape=[shape((tracers + levels + 8, boxes), f32), shape((sections, tracers, boxes), f32)],
        compiler_params=lean,
        name="gathered",
    )(gathered, shared, uptake_weight)
    adjoint = lax.all_gather(start, "core")
    uptake_t, release_t = uptake_weight.T, release_weight.T
    kept_shapes = [shape((2, 2 * spans, SPAN, SPAN), bf16), shape((4, boxes), f32)]
    kept = []
    for section in range(sections - 1, -1, -1):
        first = section == sections - 1

        def step(*refs, section=section, first=first):
            step_kernel(*refs, section=section, levels=levels, first=first)

        out_shape = [shape((2 * tracers, boxes), f32)] * 2 + kept_shapes * first
        send, keep, *made = pl.pallas_call(
            step,
            in_specs=[vmem] * (7 + len(kept)),
            out_specs=[vmem] * len(out_shape),
            out_shape=out_shape,
            scratch_shapes=[pltpu.VMEM((2, tracers, boxes), f32)],
            compiler_params=lean,
        )(adjoint, ordered, borrowed, upper, slopes, uptake_t, release_t, *kept)
        kept = made or kept
        if section == 0:
            rows = ylo_size * tracers_here
            at = (0, lax.axis_index("x") * rows, 0)
            send, keep = (
                lax.dynamic_slice(part.reshape(2, tracers, boxes), at, (2, rows, boxes)).reshape(2 * rows, boxes)
                for part in (send, keep)
            )
        arrived = lax.all_gather(send, EVERY, axis_index_groups=groups)
        keep = keep + lax.dynamic_index_in_dim(arrived, core_index, 0, keepdims=False)
        adjoint = lax.all_gather(keep, "core")
    mine = lax.dynamic_index_in_dim(adjoint, core_index, 0, keepdims=False)[:rows]
    theirs = lax.dynamic_index_in_dim(adjoint, 1 - core_index, 0, keepdims=False)[rows:]
    wet = lax.dynamic_index_in_dim(kept[1], core_index, 0, keepdims=True)
    result = (wet * (mine + theirs)).reshape(ylo_size, tracers_here, boxes)
    passed = lax.dynamic_index_in_dim(result, 1 - ylo_index, 0, keepdims=False)
    passed = lax.dynamic_index_in_dim(lax.all_gather(passed, "ylo"), 1 - ylo_index, 0, keepdims=False)
    return jnp.where(joined, lax.dynamic_index_in_dim(result, ylo_index, 0, keepdims=False), passed)


def solution(mesh):
    regions, tracer_devices = mesh.devices.shape
    nq, nx, ny = regions // 2, tracer_devices // 2, 2
    fine = Mesh(mesh.devices.reshape(nq // 2, 2, 2, nx, ny), EVERY)
    placed = (
        P(TRACER, REGION),
        P(None, TRACER, REGION),
        P(REGION, None, None),
        P(REGION),
        P(REGION, None, None, None),
        P(REGION, None),
        P(REGION),
        P(),
        P(),
    )

    def body(*args):
        return local(*args, sizes=(nq, nx, ny))

    return jax.shard_map(body, mesh=fine, in_specs=placed, out_specs=P(TRACER, REGION), check_vma=False)
```

```python
import jax
import jax.numpy as jnp
from jax import lax
from jax.experimental import pallas as pl
from jax.experimental.pallas import tpu as pltpu
from jax.sharding import Mesh, PartitionSpec as P


REGION = ("z", "yhi", "core")
TRACER = ("x", "ylo")
EVERY = REGION + TRACER
SPAN = 256
VMEM_LIMIT = 8 * 2**20
COUNT_AT, CORE_AT = 5, 6


def neighbour_groups(sizes):
    nq, nx, ny = sizes

    def at(chip, core, x, ylo):
        return (((chip % nq) * 2 + core) * nx + x) * ny + ylo

    groups = []
    for q in range(nq):
        for x in range(nx):
            joined, alone = (1, 0) if q % 2 == 0 else (0, 1)
            groups.append([at(q, 1, x, joined), at(q + 1, 0, x, 1 - joined)])
            groups.append([at(q, 1, x, alone), at(q, 0, x, alone)])
    return groups


def halves(value):
    high = value.astype(jnp.bfloat16)
    low = (value - high.astype(jnp.float32)).astype(jnp.bfloat16)
    return high, low


def dot(a, b):
    return lax.dot_general(a, b, (((1,), (0,)), ((), ())), preferred_element_type=jnp.float32)


def dot_split(a_high, a_low, b_high, b_low):
    rows = a_high.shape[0]
    both = dot(jnp.concatenate([a_high, a_low], axis=0), b_high)
    return both[:rows] + both[rows:] + dot(a_high, b_low)


def slot_at(offsets, slots, distance):
    slot = jnp.int32(0)
    for k in range(slots):
        slot = slot + jnp.where(offsets[k] == distance, k, 0)
    return slot


def slot_live(offsets, slots, distance):
    live = jnp.int32(0)
    for k in range(slots):
        live = live + jnp.where((offsets[k] == distance) & (k < offsets[COUNT_AT]), 1, 0)
    return live > 0


def pack_kernel(cotangent, states, copies, sent):
    peers = copies.shape[0]
    sends = [pltpu.make_async_copy(cotangent, copies.at[t, 0], sent.at[0, t]) for t in range(peers)] + [
        pltpu.make_async_copy(states, copies.at[t, pl.ds(1, states.shape[0])], sent.at[1, t]) for t in range(peers)
    ]
    for send in sends:
        send.start()
    for send in sends:
        send.wait()


def lend_kernel(offsets_hbm, tiles, lent, offsets, buffer, arrival):
    ask = pltpu.make_async_copy(offsets_hbm, offsets, arrival.at[0])
    ask.start()
    ask.wait()
    distance = 2 - 4 * lax.axis_index("core")
    fetch = pltpu.make_async_copy(tiles.at[0, slot_at(offsets.at[0], tiles.shape[1], distance)], buffer, arrival.at[1])
    fetch.start()
    fetch.wait()
    lent[...] = buffer[...].astype(jnp.float32)


def arrange_kernel(facts, wet, tiles, inverse, ordered, shared, upper, arrival):
    slots = tiles.shape[1]
    direction = 2 * facts[CORE_AT] - 1
    uses = (direction, 2 * direction, 0, -direction)
    fetches = [
        pltpu.make_async_copy(tiles.at[0, slot_at(facts, slots, distance)], ordered.at[n], arrival.at[n])
        for n, distance in enumerate(uses)
    ]
    for fetch in fetches:
        fetch.start()
    columns, levels, _ = inverse.shape
    lane = lax.broadcasted_iota(jnp.int32, (levels, levels), 1)
    row = lax.broadcasted_iota(jnp.int32, (8, levels), 1)
    for c in range(columns):
        at = slice(c * levels, (c + 1) * levels)
        shared[0:levels, at] = jnp.where(lane < wet[c], inverse[c], 0.0)
        shared[levels : levels + 8, at] = jnp.where(row < wet[c], 1.0, 0.0)
    lending = jnp.where(slot_live(facts, slots, -2 * direction), 1.0, 0.0)
    shared[levels + 4 :, :] = jnp.full((4, shared.shape[1]), lending, jnp.float32)
    upper[...] = jnp.full(upper.shape, facts[CORE_AT], jnp.int32).astype(jnp.float32)
    for fetch in fetches:
        fetch.wait()
    for n, distance in enumerate(uses):

        @pl.when(jnp.logical_not(slot_live(facts, slots, distance)))
        def _():
            ordered[n] = jnp.zeros(ordered.shape[1:], ordered.dtype)


def round_kernel(borrowed, tile_out):
    tile_out[...] = borrowed[...].astype(jnp.bfloat16)


def gathered_kernel(gathered, shared, uptake_weight, start, slopes):
    peers, _, few, _ = gathered.shape
    tracers = uptake_weight.shape[0]
    start[tracers:, :] = shared[...]
    for t in range(peers):
        at = slice(t * few, (t + 1) * few)
        start[at, :] = gathered[t, 0]
        for n in range(slopes.shape[0]):
            slopes[n, at, :] = gathered[t, 1 + n]
    weight_high, weight_low = halves(uptake_weight[...])
    for n in range(slopes.shape[0]):
        state_high, state_low = halves(slopes[n])
        reach = jnp.tanh(dot_split(weight_high, weight_low, state_high, state_low))
        slopes[n] = 1.0 - reach * reach


def lay_out_blocks(adjoint, tracers, levels, blocks, wet):
    spans = adjoint.shape[2] // SPAN
    same = (
        lax.broadcasted_iota(jnp.int32, (SPAN, SPAN), 0) // levels
        == lax.broadcasted_iota(jnp.int32, (SPAN, SPAN), 1) // levels
    )
    for side in range(2):
        for s in range(spans):
            high, low = halves(adjoint[side, tracers : tracers + levels, s * SPAN : (s + 1) * SPAN])
            full_high = jnp.concatenate([high] * (SPAN // levels), axis=0)
            full_low = jnp.concatenate([low] * (SPAN // levels), axis=0)
            blocks[0, side * spans + s] = jnp.where(same, full_high, jnp.zeros_like(full_high))
            blocks[1, side * spans + s] = jnp.where(same, full_low, jnp.zeros_like(full_low))
        wet[side : side + 1, :] = adjoint[side, tracers + levels : tracers + levels + 1, :]
        wet[2 + side : 3 + side, :] = adjoint[side, tracers + levels + 4 : tracers + levels + 5, :]


def step_kernel(adjoint, ordered, borrowed, upper, slopes, uptake_t, release_t, *rest, section, levels, first):
    tracers = uptake_t.shape[0]
    if first:
        send, keep, blocks, wet, settled = rest
        lay_out_blocks(adjoint, tracers, levels, blocks, wet)
        pair = (adjoint[0, 0:tracers, :], adjoint[1, 0:tracers, :])
    else:
        blocks, wet, send, keep, settled = rest
        pair = (
            wet[0:1, :] * (adjoint[0, 0:tracers, :] + adjoint[1, tracers:, :]),
            wet[1:2, :] * (adjoint[1, 0:tracers, :] + adjoint[0, tracers:, :]),
        )
    spans = adjoint.shape[2] // SPAN
    for side in range(2):
        high, low = halves(pair[side])
        for s in range(spans):
            at = slice(s * SPAN, (s + 1) * SPAN)
            k = side * spans + s
            settled[side, :, at] = dot_split(high[:, at], low[:, at], blocks[0, k], blocks[1, k])
    is_upper = upper[0:1, :] > 0.5
    own_high, own_low = halves(jnp.where(is_upper, settled[1], settled[0]))
    other = jnp.where(is_upper, wet[2:3, :] * settled[0], wet[3:4, :] * settled[1]).astype(jnp.bfloat16)
    send[0:tracers, :] = dot(own_high, ordered[0]) + dot(other, borrowed[...])
    send[tracers:, :] = dot(own_high, ordered[1])
    release_high, release_low = halves(release_t[...])
    pushed = slopes[section] * dot_split(release_high, release_low, own_high, own_low)
    pushed_high, pushed_low = halves(pushed)
    uptake_high, uptake_low = halves(uptake_t[...])
    keep[0:tracers, :] = dot(own_high, ordered[2]) + dot_split(uptake_high, uptake_low, pushed_high, pushed_low)
    keep[tracers:, :] = dot(own_high, ordered[3])


def local(
    cotangent,
    states,
    implicit_inverse,
    wet_levels,
    explicit_tiles,
    tile_offset,
    tile_count,
    uptake_weight,
    release_weight,
    *,
    sizes,
):
    tracers_here, boxes = cotangent.shape
    sections = states.shape[0]
    _, levels, _ = implicit_inverse.shape
    tracers = uptake_weight.shape[0]
    spans = boxes // SPAN
    peers = tracers // tracers_here
    f32, bf16 = jnp.float32, jnp.bfloat16
    shape = jax.ShapeDtypeStruct
    vmem = pl.BlockSpec(memory_space=pltpu.VMEM)
    smem = pl.BlockSpec(memory_space=pltpu.SMEM)
    hbm = pl.BlockSpec(memory_space=pltpu.HBM)
    lean = pltpu.CompilerParams(vmem_limit_bytes=VMEM_LIMIT)
    dma = pltpu.SemaphoreType.DMA
    core_index = lax.axis_index("core")
    core = core_index.astype(jnp.int32).reshape(1)
    ylo_index, ylo_size = lax.axis_index("ylo"), lax.axis_size("ylo")
    joined = lax.axis_index("yhi") + ylo_index == 1
    groups = neighbour_groups(sizes)

    def in_hbm(array):
        return pltpu.with_memory_space_constraint(array, pltpu.HBM)

    copies = pl.pallas_call(
        pack_kernel,
        in_specs=[hbm] * 2,
        out_specs=hbm,
        out_shape=shape((peers, 1 + sections, tracers_here, boxes), f32),
        scratch_shapes=[dma((2, peers))],
        compiler_params=lean,
        name="pack",
    )(in_hbm(cotangent), in_hbm(states))
    gathered = lax.all_to_all(copies, TRACER, split_axis=0, concat_axis=0, tiled=True)
    facts = jnp.concatenate([tile_offset.reshape(-1), tile_count, core])
    lent = pl.pallas_call(
        lend_kernel,
        in_specs=[hbm] * 2,
        out_specs=vmem,
        out_shape=shape((boxes, boxes), f32),
        scratch_shapes=[pltpu.SMEM(tile_offset.shape, jnp.int32), pltpu.VMEM((boxes, boxes), bf16), dma((2,))],
        compiler_params=lean,
        name="lend",
    )(in_hbm(tile_offset), in_hbm(explicit_tiles))
    borrowed = lax.ppermute(lent, "core", [(0, 1), (1, 0)])
    ordered, shared, upper = pl.pallas_call(
        arrange_kernel,
        in_specs=[smem] * 2 + [hbm, vmem],
        out_specs=[vmem] * 3,
        out_shape=[
            shape((4, boxes, boxes), bf16),
            shape((levels + 8, boxes), f32),
            shape((8, boxes), f32),
        ],
        scratch_shapes=[dma((4,))],
        compiler_params=lean,
        name="arrange",
    )(facts, wet_levels, in_hbm(explicit_tiles), implicit_inverse)
    borrowed = pl.pallas_call(
        round_kernel,
        in_specs=[vmem],
        out_specs=vmem,
        out_shape=shape((boxes, boxes), bf16),
        compiler_params=lean,
        name="round",
    )(borrowed)
    start, slopes = pl.pallas_call(
        gathered_kernel,
        in_specs=[vmem] * 3,
        out_specs=[vmem] * 2,
        out_shape=[shape((tracers + levels + 8, boxes), f32), shape((sections, tracers, boxes), f32)],
        compiler_params=lean,
        name="gathered",
    )(gathered, shared, uptake_weight)
    adjoint = lax.all_gather(start, "core")
    uptake_t, release_t = uptake_weight.T, release_weight.T
    kept_shapes = [shape((2, 2 * spans, SPAN, SPAN), bf16), shape((4, boxes), f32)]
    kept = []
    for section in range(sections - 1, -1, -1):
        first = section == sections - 1

        def step(*refs, section=section, first=first):
            step_kernel(*refs, section=section, levels=levels, first=first)

        out_shape = [shape((2 * tracers, boxes), f32)] * 2 + kept_shapes * first
        send, keep, *made = pl.pallas_call(
            step,
            in_specs=[vmem] * (7 + len(kept)),
            out_specs=[vmem] * len(out_shape),
            out_shape=out_shape,
            scratch_shapes=[pltpu.VMEM((2, tracers, boxes), f32)],
            compiler_params=lean,
        )(adjoint, ordered, borrowed, upper, slopes, uptake_t, release_t, *kept)
        kept = made or kept
        if section == 0:
            rows = ylo_size * tracers_here
            at = (0, lax.axis_index("x") * rows, 0)
            send, keep = (
                lax.dynamic_slice(part.reshape(2, tracers, boxes), at, (2, rows, boxes)).reshape(2 * rows, boxes)
                for part in (send, keep)
            )
        arrived = lax.all_gather(send, EVERY, axis_index_groups=groups)
        keep = keep + lax.dynamic_index_in_dim(arrived, core_index, 0, keepdims=False)
        adjoint = lax.all_gather(keep, "core")
    mine = lax.dynamic_index_in_dim(adjoint, core_index, 0, keepdims=False)[:rows]
    theirs = lax.dynamic_index_in_dim(adjoint, 1 - core_index, 0, keepdims=False)[rows:]
    wet = lax.dynamic_index_in_dim(kept[1], core_index, 0, keepdims=True)
    result = (wet * (mine + theirs)).reshape(ylo_size, tracers_here, boxes)
    passed = lax.dynamic_index_in_dim(result, 1 - ylo_index, 0, keepdims=False)
    passed = lax.dynamic_index_in_dim(lax.all_gather(passed, "ylo"), 1 - ylo_index, 0, keepdims=False)
    return jnp.where(joined, lax.dynamic_index_in_dim(result, ylo_index, 0, keepdims=False), passed)


def solution(mesh):
    regions, tracer_devices = mesh.devices.shape
    nq, nx, ny = regions // 2, tracer_devices // 2, 2
    fine = Mesh(mesh.devices.reshape(nq // 2, 2, 2, nx, ny), EVERY)
    placed = (
        P(TRACER, REGION),
        P(None, TRACER, REGION),
        P(REGION, None, None),
        P(REGION),
        P(REGION, None, None, None),
        P(REGION, None),
        P(REGION),
        P(),
        P(),
    )

    def body(*args):
        return local(*args, sizes=(nq, nx, ny))

    return jax.shard_map(body, mesh=fine, in_specs=placed, out_specs=P(TRACER, REGION), check_vma=False)
```

```python
import jax
import jax.numpy as jnp
from jax import lax
from jax.experimental import pallas as pl
from jax.experimental.pallas import tpu as pltpu
from jax.sharding import Mesh, PartitionSpec as P


REGION = ("z", "yhi", "core")
TRACER = ("x", "ylo")
EVERY = REGION + TRACER
SPAN = 256
VMEM_LIMIT = 8 * 2**20
COUNT_AT, CORE_AT = 5, 6


def neighbour_groups(sizes):
    nq, nx, ny = sizes

    def at(chip, core, x, ylo):
        return (((chip % nq) * 2 + core) * nx + x) * ny + ylo

    groups = []
    for q in range(nq):
        for x in range(nx):
            joined, alone = (1, 0) if q % 2 == 0 else (0, 1)
            groups.append([at(q, 1, x, joined), at(q + 1, 0, x, 1 - joined)])
            groups.append([at(q, 1, x, alone), at(q, 0, x, alone)])
    return groups


def halves(value):
    high = value.astype(jnp.bfloat16)
    low = (value - high.astype(jnp.float32)).astype(jnp.bfloat16)
    return high, low


def dot(a, b):
    return lax.dot_general(a, b, (((1,), (0,)), ((), ())), preferred_element_type=jnp.float32)


def dot_split(a_high, a_low, b_high, b_low):
    rows = a_high.shape[0]
    both = dot(jnp.concatenate([a_high, a_low], axis=0), b_high)
    return both[:rows] + both[rows:] + dot(a_high, b_low)


def slot_at(offsets, slots, distance):
    slot = jnp.int32(0)
    for k in range(slots):
        slot = slot + jnp.where(offsets[k] == distance, k, 0)
    return slot


def slot_live(offsets, slots, distance):
    live = jnp.int32(0)
    for k in range(slots):
        live = live + jnp.where((offsets[k] == distance) & (k < offsets[COUNT_AT]), 1, 0)
    return live > 0


def pack_kernel(cotangent, states, copies, buffer, fetched):
    first = pltpu.make_async_copy(cotangent, buffer.at[0], fetched.at[0])
    rest = pltpu.make_async_copy(states, buffer.at[pl.ds(1, states.shape[0])], fetched.at[1])
    first.start()
    rest.start()
    first.wait()
    rest.wait()
    for t in range(copies.shape[0]):
        copies[t] = buffer[...]


def lend_kernel(offsets_hbm, tiles, lent, offsets, buffer, arrival):
    ask = pltpu.make_async_copy(offsets_hbm, offsets, arrival.at[0])
    ask.start()
    ask.wait()
    distance = 2 - 4 * lax.axis_index("core")
    fetch = pltpu.make_async_copy(tiles.at[0, slot_at(offsets.at[0], tiles.shape[1], distance)], buffer, arrival.at[1])
    fetch.start()
    fetch.wait()
    lent[...] = buffer[...].astype(jnp.float32)


def arrange_kernel(facts, wet, tiles, inverse, ordered, shared, upper, arrival):
    slots = tiles.shape[1]
    direction = 2 * facts[CORE_AT] - 1
    uses = (direction, 2 * direction, 0, -direction)
    fetches = [
        pltpu.make_async_copy(tiles.at[0, slot_at(facts, slots, distance)], ordered.at[n], arrival.at[n])
        for n, distance in enumerate(uses)
    ]
    for fetch in fetches:
        fetch.start()
    columns, levels, _ = inverse.shape
    lane = lax.broadcasted_iota(jnp.int32, (levels, levels), 1)
    row = lax.broadcasted_iota(jnp.int32, (8, levels), 1)
    for c in range(columns):
        at = slice(c * levels, (c + 1) * levels)
        shared[0:levels, at] = jnp.where(lane < wet[c], inverse[c], 0.0)
        shared[levels : levels + 8, at] = jnp.where(row < wet[c], 1.0, 0.0)
    lending = jnp.where(slot_live(facts, slots, -2 * direction), 1.0, 0.0)
    shared[levels + 4 :, :] = jnp.full((4, shared.shape[1]), lending, jnp.float32)
    upper[...] = jnp.full(upper.shape, facts[CORE_AT], jnp.int32).astype(jnp.float32)
    for fetch in fetches:
        fetch.wait()
    for n, distance in enumerate(uses):

        @pl.when(jnp.logical_not(slot_live(facts, slots, distance)))
        def _():
            ordered[n] = jnp.zeros(ordered.shape[1:], ordered.dtype)


def gathered_kernel(gathered, shared, uptake_weight, start, slopes):
    peers, _, few, _ = gathered.shape
    tracers = uptake_weight.shape[0]
    start[tracers:, :] = shared[...]
    for t in range(peers):
        at = slice(t * few, (t + 1) * few)
        start[at, :] = gathered[t, 0]
        for n in range(slopes.shape[0]):
            slopes[n, at, :] = gathered[t, 1 + n]
    weight_high, weight_low = halves(uptake_weight[...])
    for n in range(slopes.shape[0]):
        state_high, state_low = halves(slopes[n])
        reach = jnp.tanh(dot_split(weight_high, weight_low, state_high, state_low))
        slopes[n] = 1.0 - reach * reach


def lay_out_blocks(adjoint, tracers, levels, blocks, wet):
    spans = adjoint.shape[2] // SPAN
    same = (
        lax.broadcasted_iota(jnp.int32, (SPAN, SPAN), 0) // levels
        == lax.broadcasted_iota(jnp.int32, (SPAN, SPAN), 1) // levels
    )
    for side in range(2):
        for s in range(spans):
            high, low = halves(adjoint[side, tracers : tracers + levels, s * SPAN : (s + 1) * SPAN])
            full_high = jnp.concatenate([high] * (SPAN // levels), axis=0)
            full_low = jnp.concatenate([low] * (SPAN // levels), axis=0)
            blocks[0, side * spans + s] = jnp.where(same, full_high, jnp.zeros_like(full_high))
            blocks[1, side * spans + s] = jnp.where(same, full_low, jnp.zeros_like(full_low))
        wet[side : side + 1, :] = adjoint[side, tracers + levels : tracers + levels + 1, :]
        wet[2 + side : 3 + side, :] = adjoint[side, tracers + levels + 4 : tracers + levels + 5, :]


def step_kernel(adjoint, ordered, borrowed, upper, slopes, uptake_t, release_t, *rest, section, levels, first):
    tracers = uptake_t.shape[0]
    if first:
        send, keep, blocks, wet, tile, settled, buffer, arrival = rest
        fetch = pltpu.make_async_copy(borrowed, buffer, arrival)
        fetch.start()
        lay_out_blocks(adjoint, tracers, levels, blocks, wet)
        pair = (adjoint[0, 0:tracers, :], adjoint[1, 0:tracers, :])
    else:
        blocks, wet, send, keep, settled = rest
        tile = borrowed
        pair = (
            wet[0:1, :] * (adjoint[0, 0:tracers, :] + adjoint[1, tracers:, :]),
            wet[1:2, :] * (adjoint[1, 0:tracers, :] + adjoint[0, tracers:, :]),
        )
    spans = adjoint.shape[2] // SPAN
    for side in range(2):
        high, low = halves(pair[side])
        for s in range(spans):
            at = slice(s * SPAN, (s + 1) * SPAN)
            k = side * spans + s
            settled[side, :, at] = dot_split(high[:, at], low[:, at], blocks[0, k], blocks[1, k])
    is_upper = upper[0:1, :] > 0.5
    own_high, own_low = halves(jnp.where(is_upper, settled[1], settled[0]))
    other = jnp.where(is_upper, wet[2:3, :] * settled[0], wet[3:4, :] * settled[1]).astype(jnp.bfloat16)
    send[tracers:, :] = dot(own_high, ordered[1])
    release_high, release_low = halves(release_t[...])
    pushed = slopes[section] * dot_split(release_high, release_low, own_high, own_low)
    pushed_high, pushed_low = halves(pushed)
    uptake_high, uptake_low = halves(uptake_t[...])
    keep[0:tracers, :] = dot(own_high, ordered[2]) + dot_split(uptake_high, uptake_low, pushed_high, pushed_low)
    keep[tracers:, :] = dot(own_high, ordered[3])
    if first:
        fetch.wait()
        tile[...] = buffer[...].astype(jnp.bfloat16)
    send[0:tracers, :] = dot(own_high, ordered[0]) + dot(other, tile[...])


def local(
    cotangent,
    states,
    implicit_inverse,
    wet_levels,
    explicit_tiles,
    tile_offset,
    tile_count,
    uptake_weight,
    release_weight,
    *,
    sizes,
):
    tracers_here, boxes = cotangent.shape
    sections = states.shape[0]
    _, levels, _ = implicit_inverse.shape
    tracers = uptake_weight.shape[0]
    spans = boxes // SPAN
    peers = tracers // tracers_here
    f32, bf16 = jnp.float32, jnp.bfloat16
    shape = jax.ShapeDtypeStruct
    vmem = pl.BlockSpec(memory_space=pltpu.VMEM)
    smem = pl.BlockSpec(memory_space=pltpu.SMEM)
    hbm = pl.BlockSpec(memory_space=pltpu.HBM)
    lean = pltpu.CompilerParams(vmem_limit_bytes=VMEM_LIMIT)
    dma = pltpu.SemaphoreType.DMA
    core_index = lax.axis_index("core")
    core = core_index.astype(jnp.int32).reshape(1)
    ylo_index, ylo_size = lax.axis_index("ylo"), lax.axis_size("ylo")
    joined = lax.axis_index("yhi") + ylo_index == 1
    groups = neighbour_groups(sizes)

    def in_hbm(array):
        return pltpu.with_memory_space_constraint(array, pltpu.HBM)

    copies = pl.pallas_call(
        pack_kernel,
        in_specs=[hbm] * 2,
        out_specs=vmem,
        out_shape=shape((peers, 1 + sections, tracers_here, boxes), f32),
        scratch_shapes=[pltpu.VMEM((1 + sections, tracers_here, boxes), f32), dma((2,))],
        compiler_params=lean,
        name="pack",
    )(in_hbm(cotangent), in_hbm(states))
    gathered = lax.all_to_all(copies, TRACER, split_axis=0, concat_axis=0, tiled=True)
    facts = jnp.concatenate([tile_offset.reshape(-1), tile_count, core])
    lent = pl.pallas_call(
        lend_kernel,
        in_specs=[hbm] * 2,
        out_specs=vmem,
        out_shape=shape((boxes, boxes), f32),
        scratch_shapes=[pltpu.SMEM(tile_offset.shape, jnp.int32), pltpu.VMEM((boxes, boxes), bf16), dma((2,))],
        compiler_params=lean,
        name="lend",
    )(in_hbm(tile_offset), in_hbm(explicit_tiles))
    borrowed = in_hbm(lax.ppermute(lent, "core", [(0, 1), (1, 0)]))
    ordered, shared, upper = pl.pallas_call(
        arrange_kernel,
        in_specs=[smem] * 2 + [hbm, vmem],
        out_specs=[vmem] * 3,
        out_shape=[
            shape((4, boxes, boxes), bf16),
            shape((levels + 8, boxes), f32),
            shape((8, boxes), f32),
        ],
        scratch_shapes=[dma((4,))],
        compiler_params=lean,
        name="arrange",
    )(facts, wet_levels, in_hbm(explicit_tiles), implicit_inverse)
    start, slopes = pl.pallas_call(
        gathered_kernel,
        in_specs=[vmem] * 3,
        out_specs=[vmem] * 2,
        out_shape=[shape((tracers + levels + 8, boxes), f32), shape((sections, tracers, boxes), f32)],
        compiler_params=lean,
        name="gathered",
    )(gathered, shared, uptake_weight)
    adjoint = lax.all_gather(start, "core")
    uptake_t, release_t = uptake_weight.T, release_weight.T
    kept_shapes = [shape((2, 2 * spans, SPAN, SPAN), bf16), shape((4, boxes), f32)]
    kept = []
    for section in range(sections - 1, -1, -1):
        first = section == sections - 1

        def step(*refs, section=section, first=first):
            step_kernel(*refs, section=section, levels=levels, first=first)

        out_shape = [shape((2 * tracers, boxes), f32)] * 2 + (kept_shapes + [shape((boxes, boxes), bf16)]) * first
        send, keep, *made = pl.pallas_call(
            step,
            in_specs=[vmem] * 2 + [hbm if first else vmem] + [vmem] * (4 + len(kept)),
            out_specs=[vmem] * len(out_shape),
            out_shape=out_shape,
            scratch_shapes=[pltpu.VMEM((2, tracers, boxes), f32)] + [pltpu.VMEM((boxes, boxes), f32), dma] * first,
            compiler_params=lean,
        )(adjoint, ordered, borrowed, upper, slopes, uptake_t, release_t, *kept)
        if first:
            *kept, borrowed = made
        if section == 0:
            rows = ylo_size * tracers_here
            at = (0, lax.axis_index("x") * rows, 0)
            send, keep = (
                lax.dynamic_slice(part.reshape(2, tracers, boxes), at, (2, rows, boxes)).reshape(2 * rows, boxes)
                for part in (send, keep)
            )
        arrived = lax.all_gather(send, EVERY, axis_index_groups=groups)
        keep = keep + lax.dynamic_index_in_dim(arrived, core_index, 0, keepdims=False)
        adjoint = lax.all_gather(keep, "core")
    mine = lax.dynamic_index_in_dim(adjoint, core_index, 0, keepdims=False)[:rows]
    theirs = lax.dynamic_index_in_dim(adjoint, 1 - core_index, 0, keepdims=False)[rows:]
    wet = lax.dynamic_index_in_dim(kept[1], core_index, 0, keepdims=True)
    result = (wet * (mine + theirs)).reshape(ylo_size, tracers_here, boxes)
    passed = lax.dynamic_index_in_dim(result, 1 - ylo_index, 0, keepdims=False)
    passed = lax.dynamic_index_in_dim(lax.all_gather(passed, "ylo"), 1 - ylo_index, 0, keepdims=False)
    return jnp.where(joined, lax.dynamic_index_in_dim(result, ylo_index, 0, keepdims=False), passed)


def solution(mesh):
    regions, tracer_devices = mesh.devices.shape
    nq, nx, ny = regions // 2, tracer_devices // 2, 2
    fine = Mesh(mesh.devices.reshape(nq // 2, 2, 2, nx, ny), EVERY)
    placed = (
        P(TRACER, REGION),
        P(None, TRACER, REGION),
        P(REGION, None, None),
        P(REGION),
        P(REGION, None, None, None),
        P(REGION, None),
        P(REGION),
        P(),
        P(),
    )

    def body(*args):
        return local(*args, sizes=(nq, nx, ny))

    return jax.shard_map(body, mesh=fine, in_specs=placed, out_specs=P(TRACER, REGION), check_vma=False)
```

```python
import jax
import jax.numpy as jnp
from jax import lax
from jax.experimental import pallas as pl
from jax.experimental.pallas import tpu as pltpu
from jax.sharding import Mesh, PartitionSpec as P


REGION = ("z", "yhi", "core")
TRACER = ("x", "ylo")
EVERY = REGION + TRACER
SPAN = 256
VMEM_LIMIT = 8 * 2**20
COUNT_AT, CORE_AT = 5, 6


def neighbour_groups(sizes):
    nq, nx, ny = sizes

    def at(chip, core, x, ylo):
        return (((chip % nq) * 2 + core) * nx + x) * ny + ylo

    groups = []
    for q in range(nq):
        for x in range(nx):
            joined, alone = (1, 0) if q % 2 == 0 else (0, 1)
            groups.append([at(q, 1, x, joined), at(q + 1, 0, x, 1 - joined)])
            groups.append([at(q, 1, x, alone), at(q, 0, x, alone)])
    return groups


def chip_groups(sizes):
    nq, nx, ny = sizes
    return [
        [((q * 2 + core) * nx + x) * ny + ylo for ylo in range(ny) for core in range(2)]
        for q in range(nq)
        for x in range(nx)
    ]


def halves(value):
    high = value.astype(jnp.bfloat16)
    low = (value - high.astype(jnp.float32)).astype(jnp.bfloat16)
    return high, low


def dot(a, b):
    return lax.dot_general(a, b, (((1,), (0,)), ((), ())), preferred_element_type=jnp.float32)


def dot_split(a_high, a_low, b_high, b_low):
    rows = a_high.shape[0]
    both = dot(jnp.concatenate([a_high, a_low], axis=0), b_high)
    return both[:rows] + both[rows:] + dot(a_high, b_low)


def slot_at(offsets, slots, distance):
    slot = jnp.int32(0)
    for k in range(slots):
        slot = slot + jnp.where(offsets[k] == distance, k, 0)
    return slot


def slot_live(offsets, slots, distance):
    live = jnp.int32(0)
    for k in range(slots):
        live = live + jnp.where((offsets[k] == distance) & (k < offsets[COUNT_AT]), 1, 0)
    return live > 0


def pack_kernel(cotangent, states, copies, buffer, fetched):
    first = pltpu.make_async_copy(cotangent, buffer.at[0], fetched.at[0])
    rest = pltpu.make_async_copy(states, buffer.at[pl.ds(1, states.shape[0])], fetched.at[1])
    first.start()
    rest.start()
    first.wait()
    rest.wait()
    for t in range(copies.shape[0]):
        copies[t] = buffer[...]


def lend_kernel(offsets_hbm, tiles, lent, offsets, buffer, arrival):
    ask = pltpu.make_async_copy(offsets_hbm, offsets, arrival.at[0])
    ask.start()
    ask.wait()
    distance = 2 - 4 * lax.axis_index("core")
    fetch = pltpu.make_async_copy(tiles.at[0, slot_at(offsets.at[0], tiles.shape[1], distance)], buffer, arrival.at[1])
    fetch.start()
    fetch.wait()
    lent[...] = buffer[...].astype(jnp.float32)


def arrange_kernel(facts, wet, tiles, inverse, ordered, shared, upper, arrival):
    slots = tiles.shape[1]
    direction = 2 * facts[CORE_AT] - 1
    uses = (direction, 2 * direction, 0, -direction)
    fetches = [
        pltpu.make_async_copy(tiles.at[0, slot_at(facts, slots, distance)], ordered.at[n], arrival.at[n])
        for n, distance in enumerate(uses)
    ]
    for fetch in fetches:
        fetch.start()
    columns, levels, _ = inverse.shape
    lane = lax.broadcasted_iota(jnp.int32, (levels, levels), 1)
    row = lax.broadcasted_iota(jnp.int32, (8, levels), 1)
    for c in range(columns):
        at = slice(c * levels, (c + 1) * levels)
        shared[0:levels, at] = jnp.where(lane < wet[c], inverse[c], 0.0)
        shared[levels : levels + 8, at] = jnp.where(row < wet[c], 1.0, 0.0)
    lending = jnp.where(slot_live(facts, slots, -2 * direction), 1.0, 0.0)
    shared[levels + 4 :, :] = jnp.full((4, shared.shape[1]), lending, jnp.float32)
    upper[...] = jnp.full(upper.shape, facts[CORE_AT], jnp.int32).astype(jnp.float32)
    for fetch in fetches:
        fetch.wait()
    for n, distance in enumerate(uses):

        @pl.when(jnp.logical_not(slot_live(facts, slots, distance)))
        def _():
            ordered[n] = jnp.zeros(ordered.shape[1:], ordered.dtype)


def gathered_kernel(gathered, shared, uptake_weight, start, slopes):
    peers, _, few, _ = gathered.shape
    tracers = uptake_weight.shape[0]
    start[tracers:, :] = shared[...]
    for t in range(peers):
        at = slice(t * few, (t + 1) * few)
        start[at, :] = gathered[t, 0]
        for n in range(slopes.shape[0]):
            slopes[n, at, :] = gathered[t, 1 + n]
    weight_high, weight_low = halves(uptake_weight[...])
    for n in range(slopes.shape[0]):
        state_high, state_low = halves(slopes[n])
        reach = jnp.tanh(dot_split(weight_high, weight_low, state_high, state_low))
        slopes[n] = 1.0 - reach * reach


def lay_out_blocks(adjoint, is_upper, tracers, levels, blocks, wet):
    spans = adjoint.shape[2] // SPAN
    same = (
        lax.broadcasted_iota(jnp.int32, (SPAN, SPAN), 0) // levels
        == lax.broadcasted_iota(jnp.int32, (SPAN, SPAN), 1) // levels
    )
    for side in range(2):

        def rows(at):
            return jnp.where(is_upper, adjoint[1 - side, at, :], adjoint[side, at, :])

        inverses = rows(slice(tracers, tracers + levels))
        for s in range(spans):
            high, low = halves(inverses[:, s * SPAN : (s + 1) * SPAN])
            full_high = jnp.concatenate([high] * (SPAN // levels), axis=0)
            full_low = jnp.concatenate([low] * (SPAN // levels), axis=0)
            blocks[0, side * spans + s] = jnp.where(same, full_high, jnp.zeros_like(full_high))
            blocks[1, side * spans + s] = jnp.where(same, full_low, jnp.zeros_like(full_low))
        wet[side : side + 1, :] = rows(slice(tracers + levels, tracers + levels + 1))
        wet[2 + side : 3 + side, :] = rows(slice(tracers + levels + 4, tracers + levels + 5))


def settle(value, blocks, side):
    spans = value.shape[1] // SPAN
    high, low = halves(value)
    pieces = []
    for s in range(spans):
        at = slice(s * SPAN, (s + 1) * SPAN)
        k = side * spans + s
        pieces.append(dot_split(high[:, at], low[:, at], blocks[0, k], blocks[1, k]))
    return jnp.concatenate(pieces, axis=1)


def step_kernel(adjoint, ordered, borrowed, upper, slopes, uptake_t, release_t, *rest, section, levels, first):
    tracers = uptake_t.shape[0]
    is_upper = upper[0:1, :] > 0.5
    if first:
        send, keep, blocks, wet, tile, buffer, arrival = rest
        fetch = pltpu.make_async_copy(borrowed, buffer, arrival)
        fetch.start()
        lay_out_blocks(adjoint, is_upper, tracers, levels, blocks, wet)
        lower, higher = adjoint[0, 0:tracers, :], adjoint[1, 0:tracers, :]
    else:
        blocks, wet, send, keep = rest
        tile = borrowed
        lower = adjoint[0, 0:tracers, :] + adjoint[1, tracers:, :]
        higher = adjoint[1, 0:tracers, :] + adjoint[0, tracers:, :]
    own, other = jnp.where(is_upper, higher, lower), jnp.where(is_upper, lower, higher)
    if not first:
        own, other = wet[0:1, :] * own, wet[1:2, :] * other
    own_high, own_low = halves(settle(own, blocks, 0))
    other_high = (wet[3:4, :] * settle(other, blocks, 1)).astype(jnp.bfloat16)
    send[tracers:, :] = dot(own_high, ordered[1])
    release_high, release_low = halves(release_t[...])
    pushed = slopes[section] * dot_split(release_high, release_low, own_high, own_low)
    pushed_high, pushed_low = halves(pushed)
    uptake_high, uptake_low = halves(uptake_t[...])
    keep[0:tracers, :] = dot(own_high, ordered[2]) + dot_split(uptake_high, uptake_low, pushed_high, pushed_low)
    keep[tracers:, :] = dot(own_high, ordered[3])
    if first:
        fetch.wait()
        tile[...] = buffer[...].astype(jnp.bfloat16)
    send[0:tracers, :] = dot(own_high, ordered[0]) + dot(other_high, tile[...])


def local(
    cotangent,
    states,
    implicit_inverse,
    wet_levels,
    explicit_tiles,
    tile_offset,
    tile_count,
    uptake_weight,
    release_weight,
    *,
    sizes,
):
    tracers_here, boxes = cotangent.shape
    sections = states.shape[0]
    _, levels, _ = implicit_inverse.shape
    tracers = uptake_weight.shape[0]
    spans = boxes // SPAN
    peers = tracers // tracers_here
    f32, bf16 = jnp.float32, jnp.bfloat16
    shape = jax.ShapeDtypeStruct
    vmem = pl.BlockSpec(memory_space=pltpu.VMEM)
    smem = pl.BlockSpec(memory_space=pltpu.SMEM)
    hbm = pl.BlockSpec(memory_space=pltpu.HBM)
    lean = pltpu.CompilerParams(vmem_limit_bytes=VMEM_LIMIT)
    dma = pltpu.SemaphoreType.DMA
    core_index = lax.axis_index("core")
    core = core_index.astype(jnp.int32).reshape(1)
    ylo_index, ylo_size = lax.axis_index("ylo"), lax.axis_size("ylo")
    groups = neighbour_groups(sizes)

    def in_hbm(array):
        return pltpu.with_memory_space_constraint(array, pltpu.HBM)

    copies = pl.pallas_call(
        pack_kernel,
        in_specs=[hbm] * 2,
        out_specs=vmem,
        out_shape=shape((peers, 1 + sections, tracers_here, boxes), f32),
        scratch_shapes=[pltpu.VMEM((1 + sections, tracers_here, boxes), f32), dma((2,))],
        compiler_params=lean,
        name="pack",
    )(in_hbm(cotangent), in_hbm(states))
    gathered = lax.all_to_all(copies, TRACER, split_axis=0, concat_axis=0, tiled=True)
    facts = jnp.concatenate([tile_offset.reshape(-1), tile_count, core])
    lent = pl.pallas_call(
        lend_kernel,
        in_specs=[hbm] * 2,
        out_specs=vmem,
        out_shape=shape((boxes, boxes), f32),
        scratch_shapes=[pltpu.SMEM(tile_offset.shape, jnp.int32), pltpu.VMEM((boxes, boxes), bf16), dma((2,))],
        compiler_params=lean,
        name="lend",
    )(in_hbm(tile_offset), in_hbm(explicit_tiles))
    borrowed = in_hbm(lax.ppermute(lent, "core", [(0, 1), (1, 0)]))
    ordered, shared, upper = pl.pallas_call(
        arrange_kernel,
        in_specs=[smem] * 2 + [hbm, vmem],
        out_specs=[vmem] * 3,
        out_shape=[
            shape((4, boxes, boxes), bf16),
            shape((levels + 8, boxes), f32),
            shape((8, boxes), f32),
        ],
        scratch_shapes=[dma((4,))],
        compiler_params=lean,
        name="arrange",
    )(facts, wet_levels, in_hbm(explicit_tiles), implicit_inverse)
    start, slopes = pl.pallas_call(
        gathered_kernel,
        in_specs=[vmem] * 3,
        out_specs=[vmem] * 2,
        out_shape=[shape((tracers + levels + 8, boxes), f32), shape((sections, tracers, boxes), f32)],
        compiler_params=lean,
        name="gathered",
    )(gathered, shared, uptake_weight)
    adjoint = lax.all_gather(start, "core")
    uptake_t, release_t = uptake_weight.T, release_weight.T
    kept_shapes = [shape((2, 2 * spans, SPAN, SPAN), bf16), shape((4, boxes), f32)]
    kept = []
    for section in range(sections - 1, -1, -1):
        first = section == sections - 1

        def step(*refs, section=section, first=first):
            step_kernel(*refs, section=section, levels=levels, first=first)

        out_shape = [shape((2 * tracers, boxes), f32)] * 2 + (kept_shapes + [shape((boxes, boxes), bf16)]) * first
        send, keep, *made = pl.pallas_call(
            step,
            in_specs=[vmem] * 2 + [hbm if first else vmem] + [vmem] * (4 + len(kept)),
            out_specs=[vmem] * len(out_shape),
            out_shape=out_shape,
            scratch_shapes=[pltpu.VMEM((boxes, boxes), f32), dma] * first,
            compiler_params=lean,
        )(adjoint, ordered, borrowed, upper, slopes, uptake_t, release_t, *kept)
        if first:
            *kept, borrowed = made
        if section == 0:
            rows = ylo_size * tracers_here
            at = (0, lax.axis_index("x") * rows, 0)
            send, keep = (
                lax.dynamic_slice(part.reshape(2, tracers, boxes), at, (2, rows, boxes)).reshape(2 * rows, boxes)
                for part in (send, keep)
            )
        arrived = lax.all_gather(send, EVERY, axis_index_groups=groups)
        keep = keep + lax.dynamic_index_in_dim(arrived, core_index, 0, keepdims=False)
        if section > 0:
            adjoint = lax.all_gather(keep, "core")
    final = lax.all_gather(keep, EVERY, axis_index_groups=chip_groups(sizes))
    joined = 2 * (1 - lax.axis_index("yhi"))
    row = ylo_index * tracers_here
    mine = lax.dynamic_slice(final, (joined + core_index, row, 0), (1, tracers_here, boxes))[0]
    theirs = lax.dynamic_slice(final, (joined + 1 - core_index, rows + row, 0), (1, tracers_here, boxes))[0]
    return kept[1][0:1] * (mine + theirs)


def solution(mesh):
    regions, tracer_devices = mesh.devices.shape
    nq, nx, ny = regions // 2, tracer_devices // 2, 2
    fine = Mesh(mesh.devices.reshape(nq // 2, 2, 2, nx, ny), EVERY)
    placed = (
        P(TRACER, REGION),
        P(None, TRACER, REGION),
        P(REGION, None, None),
        P(REGION),
        P(REGION, None, None, None),
        P(REGION, None),
        P(REGION),
        P(),
        P(),
    )

    def body(*args):
        return local(*args, sizes=(nq, nx, ny))

    return jax.shard_map(body, mesh=fine, in_specs=placed, out_specs=P(TRACER, REGION), check_vma=False)
```

```python
import jax
import jax.numpy as jnp
from jax import lax
from jax.experimental import pallas as pl
from jax.experimental.pallas import tpu as pltpu
from jax.sharding import Mesh, PartitionSpec as P


REGION = ("z", "yhi", "core")
TRACER = ("x", "ylo")
EVERY = REGION + TRACER
SPAN = 256
VMEM_LIMIT = 8 * 2**20
COUNT_AT, CORE_AT = 5, 6


def neighbour_groups(sizes):
    nq, nx, ny = sizes

    def at(chip, core, x, ylo):
        return (((chip % nq) * 2 + core) * nx + x) * ny + ylo

    groups = []
    for q in range(nq):
        for x in range(nx):
            joined, alone = (1, 0) if q % 2 == 0 else (0, 1)
            groups.append([at(q, 1, x, joined), at(q + 1, 0, x, 1 - joined)])
            groups.append([at(q, 1, x, alone), at(q, 0, x, alone)])
    return groups


def chip_groups(sizes):
    nq, nx, ny = sizes
    return [
        [((q * 2 + core) * nx + x) * ny + ylo for ylo in range(ny) for core in range(2)]
        for q in range(nq)
        for x in range(nx)
    ]


def halves(value):
    high = value.astype(jnp.bfloat16)
    low = (value - high.astype(jnp.float32)).astype(jnp.bfloat16)
    return high, low


def dot(a, b):
    return lax.dot_general(a, b, (((1,), (0,)), ((), ())), preferred_element_type=jnp.float32)


def dot_split(a_high, a_low, b_high, b_low):
    rows = a_high.shape[0]
    both = dot(jnp.concatenate([a_high, a_low], axis=0), b_high)
    return both[:rows] + both[rows:] + dot(a_high, b_low)


def slot_at(offsets, slots, distance):
    slot = jnp.int32(0)
    for k in range(slots):
        slot = slot + jnp.where(offsets[k] == distance, k, 0)
    return slot


def slot_live(offsets, slots, distance):
    live = jnp.int32(0)
    for k in range(slots):
        live = live + jnp.where((offsets[k] == distance) & (k < offsets[COUNT_AT]), 1, 0)
    return live > 0


def pack_kernel(cotangent, states, copies, buffer, fetched):
    first = pltpu.make_async_copy(cotangent, buffer.at[0], fetched.at[0])
    rest = pltpu.make_async_copy(states, buffer.at[pl.ds(1, states.shape[0])], fetched.at[1])
    first.start()
    rest.start()
    first.wait()
    rest.wait()
    for t in range(copies.shape[0]):
        copies[t] = buffer[...]


def in_parts(source, target, arrival):
    parts = arrival.shape[0]
    rows = target.shape[0] // parts
    ats = [pl.ds(n * rows, rows) for n in range(parts)]
    return [(pltpu.make_async_copy(source.at[at], target.at[at], arrival.at[n]), at) for n, at in enumerate(ats)]


def lend_kernel(offsets_hbm, tiles, lent, offsets, buffer, asked, arrival):
    ask = pltpu.make_async_copy(offsets_hbm, offsets, asked)
    ask.start()
    ask.wait()
    distance = 2 - 4 * lax.axis_index("core")
    fetches = in_parts(tiles.at[0, slot_at(offsets.at[0], tiles.shape[1], distance)], buffer, arrival)
    for fetch, _ in fetches:
        fetch.start()
    for fetch, at in fetches:
        fetch.wait()
        lent[at, :] = buffer[at, :].astype(jnp.float32)


def arrange_kernel(facts, wet, tiles, inverse, ordered, shared, upper, arrival):
    slots = tiles.shape[1]
    direction = 2 * facts[CORE_AT] - 1
    uses = (direction, 2 * direction, 0, -direction)
    fetches = [
        pltpu.make_async_copy(tiles.at[0, slot_at(facts, slots, distance)], ordered.at[n], arrival.at[n])
        for n, distance in enumerate(uses)
    ]
    for fetch in fetches:
        fetch.start()
    columns, levels, _ = inverse.shape
    lane = lax.broadcasted_iota(jnp.int32, (levels, levels), 1)
    row = lax.broadcasted_iota(jnp.int32, (8, levels), 1)
    for c in range(columns):
        at = slice(c * levels, (c + 1) * levels)
        shared[0:levels, at] = jnp.where(lane < wet[c], inverse[c], 0.0)
        shared[levels : levels + 8, at] = jnp.where(row < wet[c], 1.0, 0.0)
    lending = jnp.where(slot_live(facts, slots, -2 * direction), 1.0, 0.0)
    shared[levels + 4 :, :] = jnp.full((4, shared.shape[1]), lending, jnp.float32)
    upper[...] = jnp.full(upper.shape, facts[CORE_AT], jnp.int32).astype(jnp.float32)
    for fetch in fetches:
        fetch.wait()
    for n, distance in enumerate(uses):

        @pl.when(jnp.logical_not(slot_live(facts, slots, distance)))
        def _():
            ordered[n] = jnp.zeros(ordered.shape[1:], ordered.dtype)


def gathered_kernel(gathered, shared, uptake_weight, start, slopes):
    peers, _, few, _ = gathered.shape
    tracers = uptake_weight.shape[0]
    start[tracers:, :] = shared[...]
    for t in range(peers):
        at = slice(t * few, (t + 1) * few)
        start[at, :] = gathered[t, 0]
        for n in range(slopes.shape[0]):
            slopes[n, at, :] = gathered[t, 1 + n]
    weight_high, weight_low = halves(uptake_weight[...])
    for n in range(slopes.shape[0]):
        state_high, state_low = halves(slopes[n])
        reach = jnp.tanh(dot_split(weight_high, weight_low, state_high, state_low))
        slopes[n] = 1.0 - reach * reach


def lay_out_blocks(adjoint, is_upper, tracers, levels, blocks, wet):
    spans = adjoint.shape[2] // SPAN
    same = (
        lax.broadcasted_iota(jnp.int32, (SPAN, SPAN), 0) // levels
        == lax.broadcasted_iota(jnp.int32, (SPAN, SPAN), 1) // levels
    )
    for side in range(2):

        def rows(at):
            return jnp.where(is_upper, adjoint[1 - side, at, :], adjoint[side, at, :])

        inverses = rows(slice(tracers, tracers + levels))
        for s in range(spans):
            high, low = halves(inverses[:, s * SPAN : (s + 1) * SPAN])
            full_high = jnp.concatenate([high] * (SPAN // levels), axis=0)
            full_low = jnp.concatenate([low] * (SPAN // levels), axis=0)
            blocks[0, side * spans + s] = jnp.where(same, full_high, jnp.zeros_like(full_high))
            blocks[1, side * spans + s] = jnp.where(same, full_low, jnp.zeros_like(full_low))
        wet[side : side + 1, :] = rows(slice(tracers + levels, tracers + levels + 1))
        wet[2 + side : 3 + side, :] = rows(slice(tracers + levels + 4, tracers + levels + 5))


def settle(value, blocks, side):
    spans = value.shape[1] // SPAN
    high, low = halves(value)
    pieces = []
    for s in range(spans):
        at = slice(s * SPAN, (s + 1) * SPAN)
        k = side * spans + s
        pieces.append(dot_split(high[:, at], low[:, at], blocks[0, k], blocks[1, k]))
    return jnp.concatenate(pieces, axis=1)


def step_kernel(adjoint, ordered, borrowed, upper, slopes, uptake_t, release_t, *rest, section, levels, first):
    tracers = uptake_t.shape[0]
    is_upper = upper[0:1, :] > 0.5
    if first:
        send, keep, blocks, wet, tile, buffer, arrival = rest
        fetches = in_parts(borrowed, buffer, arrival)
        for fetch, _ in fetches:
            fetch.start()
        lay_out_blocks(adjoint, is_upper, tracers, levels, blocks, wet)
        lower, higher = adjoint[0, 0:tracers, :], adjoint[1, 0:tracers, :]
    else:
        blocks, wet, send, keep = rest
        tile = borrowed
        lower = adjoint[0, 0:tracers, :] + adjoint[1, tracers:, :]
        higher = adjoint[1, 0:tracers, :] + adjoint[0, tracers:, :]
    own, other = jnp.where(is_upper, higher, lower), jnp.where(is_upper, lower, higher)
    if not first:
        own, other = wet[0:1, :] * own, wet[1:2, :] * other
    own_high, own_low = halves(settle(own, blocks, 0))
    other_high = (wet[3:4, :] * settle(other, blocks, 1)).astype(jnp.bfloat16)
    send[tracers:, :] = dot(own_high, ordered[1])
    release_high, release_low = halves(release_t[...])
    pushed = slopes[section] * dot_split(release_high, release_low, own_high, own_low)
    pushed_high, pushed_low = halves(pushed)
    uptake_high, uptake_low = halves(uptake_t[...])
    keep[0:tracers, :] = dot(own_high, ordered[2]) + dot_split(uptake_high, uptake_low, pushed_high, pushed_low)
    keep[tracers:, :] = dot(own_high, ordered[3])
    if first:
        for fetch, at in fetches:
            fetch.wait()
            tile[at, :] = buffer[at, :].astype(jnp.bfloat16)
    send[0:tracers, :] = dot(own_high, ordered[0]) + dot(other_high, tile[...])


def local(
    cotangent,
    states,
    implicit_inverse,
    wet_levels,
    explicit_tiles,
    tile_offset,
    tile_count,
    uptake_weight,
    release_weight,
    *,
    sizes,
):
    tracers_here, boxes = cotangent.shape
    sections = states.shape[0]
    _, levels, _ = implicit_inverse.shape
    tracers = uptake_weight.shape[0]
    spans = boxes // SPAN
    peers = tracers // tracers_here
    f32, bf16 = jnp.float32, jnp.bfloat16
    shape = jax.ShapeDtypeStruct
    vmem = pl.BlockSpec(memory_space=pltpu.VMEM)
    smem = pl.BlockSpec(memory_space=pltpu.SMEM)
    hbm = pl.BlockSpec(memory_space=pltpu.HBM)
    lean = pltpu.CompilerParams(vmem_limit_bytes=VMEM_LIMIT)
    dma = pltpu.SemaphoreType.DMA
    core_index = lax.axis_index("core")
    core = core_index.astype(jnp.int32).reshape(1)
    ylo_index, ylo_size = lax.axis_index("ylo"), lax.axis_size("ylo")
    groups = neighbour_groups(sizes)

    def in_hbm(array):
        return pltpu.with_memory_space_constraint(array, pltpu.HBM)

    copies = pl.pallas_call(
        pack_kernel,
        in_specs=[hbm] * 2,
        out_specs=vmem,
        out_shape=shape((peers, 1 + sections, tracers_here, boxes), f32),
        scratch_shapes=[pltpu.VMEM((1 + sections, tracers_here, boxes), f32), dma((2,))],
        compiler_params=lean,
        name="pack",
    )(in_hbm(cotangent), in_hbm(states))
    gathered = lax.all_to_all(copies, TRACER, split_axis=0, concat_axis=0, tiled=True)
    facts = jnp.concatenate([tile_offset.reshape(-1), tile_count, core])
    lent = pl.pallas_call(
        lend_kernel,
        in_specs=[hbm] * 2,
        out_specs=vmem,
        out_shape=shape((boxes, boxes), f32),
        scratch_shapes=[pltpu.SMEM(tile_offset.shape, jnp.int32), pltpu.VMEM((boxes, boxes), bf16), dma, dma((4,))],
        compiler_params=lean,
        name="lend",
    )(in_hbm(tile_offset), in_hbm(explicit_tiles))
    borrowed = in_hbm(lax.ppermute(lent, "core", [(0, 1), (1, 0)]))
    ordered, shared, upper = pl.pallas_call(
        arrange_kernel,
        in_specs=[smem] * 2 + [hbm, vmem],
        out_specs=[vmem] * 3,
        out_shape=[
            shape((4, boxes, boxes), bf16),
            shape((levels + 8, boxes), f32),
            shape((8, boxes), f32),
        ],
        scratch_shapes=[dma((4,))],
        compiler_params=lean,
        name="arrange",
    )(facts, wet_levels, in_hbm(explicit_tiles), implicit_inverse)
    start, slopes = pl.pallas_call(
        gathered_kernel,
        in_specs=[vmem] * 3,
        out_specs=[vmem] * 2,
        out_shape=[shape((tracers + levels + 8, boxes), f32), shape((sections, tracers, boxes), f32)],
        compiler_params=lean,
        name="gathered",
    )(gathered, shared, uptake_weight)
    adjoint = lax.all_gather(start, "core")
    uptake_t, release_t = uptake_weight.T, release_weight.T
    kept_shapes = [shape((2, 2 * spans, SPAN, SPAN), bf16), shape((4, boxes), f32)]
    kept = []
    for section in range(sections - 1, -1, -1):
        first = section == sections - 1

        def step(*refs, section=section, first=first):
            step_kernel(*refs, section=section, levels=levels, first=first)

        out_shape = [shape((2 * tracers, boxes), f32)] * 2 + (kept_shapes + [shape((boxes, boxes), bf16)]) * first
        send, keep, *made = pl.pallas_call(
            step,
            in_specs=[vmem] * 2 + [hbm if first else vmem] + [vmem] * (4 + len(kept)),
            out_specs=[vmem] * len(out_shape),
            out_shape=out_shape,
            scratch_shapes=[pltpu.VMEM((boxes, boxes), f32), dma((4,))] * first,
            compiler_params=lean,
        )(adjoint, ordered, borrowed, upper, slopes, uptake_t, release_t, *kept)
        if first:
            *kept, borrowed = made
        if section == 0:
            rows = ylo_size * tracers_here
            at = (0, lax.axis_index("x") * rows, 0)
            send, keep = (
                lax.dynamic_slice(part.reshape(2, tracers, boxes), at, (2, rows, boxes)).reshape(2 * rows, boxes)
                for part in (send, keep)
            )
        arrived = lax.all_gather(send, EVERY, axis_index_groups=groups)
        keep = keep + lax.dynamic_index_in_dim(arrived, core_index, 0, keepdims=False)
        if section > 0:
            adjoint = lax.all_gather(keep, "core")
    final = lax.all_gather(keep, EVERY, axis_index_groups=chip_groups(sizes))
    joined = 2 * (1 - lax.axis_index("yhi"))
    row = ylo_index * tracers_here
    mine = lax.dynamic_slice(final, (joined + core_index, row, 0), (1, tracers_here, boxes))[0]
    theirs = lax.dynamic_slice(final, (joined + 1 - core_index, rows + row, 0), (1, tracers_here, boxes))[0]
    return kept[1][0:1] * (mine + theirs)


def solution(mesh):
    regions, tracer_devices = mesh.devices.shape
    nq, nx, ny = regions // 2, tracer_devices // 2, 2
    fine = Mesh(mesh.devices.reshape(nq // 2, 2, 2, nx, ny), EVERY)
    placed = (
        P(TRACER, REGION),
        P(None, TRACER, REGION),
        P(REGION, None, None),
        P(REGION),
        P(REGION, None, None, None),
        P(REGION, None),
        P(REGION),
        P(),
        P(),
    )

    def body(*args):
        return local(*args, sizes=(nq, nx, ny))

    return jax.shard_map(body, mesh=fine, in_specs=placed, out_specs=P(TRACER, REGION), check_vma=False)
```

```python
import jax
import jax.numpy as jnp
from jax import lax
from jax.experimental import pallas as pl
from jax.experimental.pallas import tpu as pltpu
from jax.sharding import Mesh, PartitionSpec as P


REGION = ("z", "yhi", "core")
TRACER = ("x", "ylo")
EVERY = REGION + TRACER
SPAN = 128
VMEM_LIMIT = 8 * 2**20
COUNT_AT, CORE_AT = 5, 6


def neighbour_groups(sizes):
    nq, nx, ny = sizes

    def at(chip, core, x, ylo):
        return (((chip % nq) * 2 + core) * nx + x) * ny + ylo

    groups = []
    for q in range(nq):
        for x in range(nx):
            joined, alone = (1, 0) if q % 2 == 0 else (0, 1)
            groups.append([at(q, 1, x, joined), at(q + 1, 0, x, 1 - joined)])
            groups.append([at(q, 1, x, alone), at(q, 0, x, alone)])
    return groups


def halves(value):
    high = value.astype(jnp.bfloat16)
    low = (value - high.astype(jnp.float32)).astype(jnp.bfloat16)
    return high, low


def dot(a, b):
    return lax.dot_general(a, b, (((1,), (0,)), ((), ())), preferred_element_type=jnp.float32)


def dot_split(a_high, a_low, b_high, b_low):
    rows = a_high.shape[0]
    both = dot(jnp.concatenate([a_high, a_low], axis=0), b_high)
    return both[:rows] + both[rows:] + dot(a_high, b_low)


def slot_at(offsets, slots, distance):
    slot = jnp.int32(0)
    for k in range(slots):
        slot = slot + jnp.where(offsets[k] == distance, k, 0)
    return slot


def slot_live(offsets, slots, distance):
    live = jnp.int32(0)
    for k in range(slots):
        live = live + jnp.where((offsets[k] == distance) & (k < offsets[COUNT_AT]), 1, 0)
    return live > 0


def pack_kernel(cotangent, states, copies, buffer, fetched):
    first = pltpu.make_async_copy(cotangent, buffer.at[0], fetched.at[0])
    rest = pltpu.make_async_copy(states, buffer.at[pl.ds(1, states.shape[0])], fetched.at[1])
    first.start()
    rest.start()
    first.wait()
    rest.wait()
    for t in range(copies.shape[0]):
        copies[t] = buffer[...]


def lend_kernel(offsets_hbm, tiles, lent, offsets, buffer, arrival):
    ask = pltpu.make_async_copy(offsets_hbm, offsets, arrival.at[0])
    ask.start()
    ask.wait()
    distance = 2 - 4 * lax.axis_index("core")
    fetch = pltpu.make_async_copy(tiles.at[0, slot_at(offsets.at[0], tiles.shape[1], distance)], buffer, arrival.at[1])
    fetch.start()
    fetch.wait()
    lent[...] = buffer[...].astype(jnp.float32)


def arrange_kernel(facts, wet, tiles, inverse, ordered, shared, upper, arrival):
    slots = tiles.shape[1]
    direction = 2 * facts[CORE_AT] - 1
    uses = (direction, 2 * direction, 0, -direction)
    fetches = [
        pltpu.make_async_copy(tiles.at[0, slot_at(facts, slots, distance)], ordered.at[n], arrival.at[n])
        for n, distance in enumerate(uses)
    ]
    for fetch in fetches:
        fetch.start()
    columns, levels, _ = inverse.shape
    lane = lax.broadcasted_iota(jnp.int32, (levels, levels), 1)
    row = lax.broadcasted_iota(jnp.int32, (8, levels), 1)
    for c in range(columns):
        at = slice(c * levels, (c + 1) * levels)
        shared[0:levels, at] = jnp.where(lane < wet[c], inverse[c], 0.0)
        shared[levels : levels + 8, at] = jnp.where(row < wet[c], 1.0, 0.0)
    lending = jnp.where(slot_live(facts, slots, -2 * direction), 1.0, 0.0)
    shared[levels + 4 :, :] = jnp.full((4, shared.shape[1]), lending, jnp.float32)
    upper[...] = jnp.full(upper.shape, facts[CORE_AT], jnp.int32).astype(jnp.float32)
    for fetch in fetches:
        fetch.wait()
    for n, distance in enumerate(uses):

        @pl.when(jnp.logical_not(slot_live(facts, slots, distance)))
        def _():
            ordered[n] = jnp.zeros(ordered.shape[1:], ordered.dtype)


def gathered_kernel(gathered, shared, uptake_weight, start, slopes):
    peers, _, few, _ = gathered.shape
    tracers = uptake_weight.shape[0]
    start[tracers:, :] = shared[...]
    for t in range(peers):
        at = slice(t * few, (t + 1) * few)
        start[at, :] = gathered[t, 0]
        for n in range(slopes.shape[0]):
            slopes[n, at, :] = gathered[t, 1 + n]
    weight_high, weight_low = halves(uptake_weight[...])
    for n in range(slopes.shape[0]):
        state_high, state_low = halves(slopes[n])
        reach = jnp.tanh(dot_split(weight_high, weight_low, state_high, state_low))
        slopes[n] = 1.0 - reach * reach


def lay_out_blocks(adjoint, is_upper, tracers, levels, blocks, wet):
    spans = adjoint.shape[2] // SPAN
    same = (
        lax.broadcasted_iota(jnp.int32, (SPAN, SPAN), 0) // levels
        == lax.broadcasted_iota(jnp.int32, (SPAN, SPAN), 1) // levels
    )
    for side in range(2):

        def rows(at):
            return jnp.where(is_upper, adjoint[1 - side, at, :], adjoint[side, at, :])

        inverses = rows(slice(tracers, tracers + levels))
        for s in range(spans):
            high, low = halves(inverses[:, s * SPAN : (s + 1) * SPAN])
            full_high = jnp.concatenate([high] * (SPAN // levels), axis=0)
            full_low = jnp.concatenate([low] * (SPAN // levels), axis=0)
            blocks[0, side * spans + s] = jnp.where(same, full_high, jnp.zeros_like(full_high))
            blocks[1, side * spans + s] = jnp.where(same, full_low, jnp.zeros_like(full_low))
        wet[side : side + 1, :] = rows(slice(tracers + levels, tracers + levels + 1))
        wet[2 + side : 3 + side, :] = rows(slice(tracers + levels + 4, tracers + levels + 5))


def settle(value, blocks, side):
    spans = value.shape[1] // SPAN
    high, low = halves(value)
    pieces = []
    for s in range(spans):
        at = slice(s * SPAN, (s + 1) * SPAN)
        k = side * spans + s
        pieces.append(dot_split(high[:, at], low[:, at], blocks[0, k], blocks[1, k]))
    return jnp.concatenate(pieces, axis=1)


def step_kernel(adjoint, ordered, borrowed, upper, slopes, uptake_t, release_t, *rest, section, levels, first):
    tracers = uptake_t.shape[0]
    is_upper = upper[0:1, :] > 0.5
    if first:
        send, keep, blocks, wet, tile, buffer, arrival = rest
        fetch = pltpu.make_async_copy(borrowed, buffer, arrival)
        fetch.start()
        lay_out_blocks(adjoint, is_upper, tracers, levels, blocks, wet)
        lower, higher = adjoint[0, 0:tracers, :], adjoint[1, 0:tracers, :]
    else:
        blocks, wet, send, keep = rest
        tile = borrowed
        lower = adjoint[0, 0:tracers, :] + adjoint[1, tracers:, :]
        higher = adjoint[1, 0:tracers, :] + adjoint[0, tracers:, :]
    own, other = jnp.where(is_upper, higher, lower), jnp.where(is_upper, lower, higher)
    if not first:
        own, other = wet[0:1, :] * own, wet[1:2, :] * other
    own_high, own_low = halves(settle(own, blocks, 0))
    other_high = (wet[3:4, :] * settle(other, blocks, 1)).astype(jnp.bfloat16)
    send[tracers:, :] = dot(own_high, ordered[1])
    release_high, release_low = halves(release_t[...])
    pushed = slopes[section] * dot_split(release_high, release_low, own_high, own_low)
    pushed_high, pushed_low = halves(pushed)
    uptake_high, uptake_low = halves(uptake_t[...])
    keep[0:tracers, :] = dot(own_high, ordered[2]) + dot_split(uptake_high, uptake_low, pushed_high, pushed_low)
    keep[tracers:, :] = dot(own_high, ordered[3])
    if first:
        fetch.wait()
        tile[...] = buffer[...].astype(jnp.bfloat16)
    send[0:tracers, :] = dot(own_high, ordered[0]) + dot(other_high, tile[...])


def local(
    cotangent,
    states,
    implicit_inverse,
    wet_levels,
    explicit_tiles,
    tile_offset,
    tile_count,
    uptake_weight,
    release_weight,
    *,
    sizes,
):
    tracers_here, boxes = cotangent.shape
    sections = states.shape[0]
    _, levels, _ = implicit_inverse.shape
    tracers = uptake_weight.shape[0]
    spans = boxes // SPAN
    peers = tracers // tracers_here
    f32, bf16 = jnp.float32, jnp.bfloat16
    shape = jax.ShapeDtypeStruct
    vmem = pl.BlockSpec(memory_space=pltpu.VMEM)
    smem = pl.BlockSpec(memory_space=pltpu.SMEM)
    hbm = pl.BlockSpec(memory_space=pltpu.HBM)
    lean = pltpu.CompilerParams(vmem_limit_bytes=VMEM_LIMIT)
    dma = pltpu.SemaphoreType.DMA
    core_index = lax.axis_index("core")
    core = core_index.astype(jnp.int32).reshape(1)
    ylo_index, ylo_size = lax.axis_index("ylo"), lax.axis_size("ylo")
    joined = lax.axis_index("yhi") + ylo_index == 1
    groups = neighbour_groups(sizes)

    def in_hbm(array):
        return pltpu.with_memory_space_constraint(array, pltpu.HBM)

    copies = pl.pallas_call(
        pack_kernel,
        in_specs=[hbm] * 2,
        out_specs=vmem,
        out_shape=shape((peers, 1 + sections, tracers_here, boxes), f32),
        scratch_shapes=[pltpu.VMEM((1 + sections, tracers_here, boxes), f32), dma((2,))],
        compiler_params=lean,
        name="pack",
    )(in_hbm(cotangent), in_hbm(states))
    gathered = lax.all_to_all(copies, TRACER, split_axis=0, concat_axis=0, tiled=True)
    facts = jnp.concatenate([tile_offset.reshape(-1), tile_count, core])
    lent = pl.pallas_call(
        lend_kernel,
        in_specs=[hbm] * 2,
        out_specs=vmem,
        out_shape=shape((boxes, boxes), f32),
        scratch_shapes=[pltpu.SMEM(tile_offset.shape, jnp.int32), pltpu.VMEM((boxes, boxes), bf16), dma((2,))],
        compiler_params=lean,
        name="lend",
    )(in_hbm(tile_offset), in_hbm(explicit_tiles))
    borrowed = in_hbm(lax.ppermute(lent, "core", [(0, 1), (1, 0)]))
    ordered, shared, upper = pl.pallas_call(
        arrange_kernel,
        in_specs=[smem] * 2 + [hbm, vmem],
        out_specs=[vmem] * 3,
        out_shape=[
            shape((4, boxes, boxes), bf16),
            shape((levels + 8, boxes), f32),
            shape((8, boxes), f32),
        ],
        scratch_shapes=[dma((4,))],
        compiler_params=lean,
        name="arrange",
    )(facts, wet_levels, in_hbm(explicit_tiles), implicit_inverse)
    start, slopes = pl.pallas_call(
        gathered_kernel,
        in_specs=[vmem] * 3,
        out_specs=[vmem] * 2,
        out_shape=[shape((tracers + levels + 8, boxes), f32), shape((sections, tracers, boxes), f32)],
        compiler_params=lean,
        name="gathered",
    )(gathered, shared, uptake_weight)
    adjoint = lax.all_gather(start, "core")
    uptake_t, release_t = uptake_weight.T, release_weight.T
    kept_shapes = [shape((2, 2 * spans, SPAN, SPAN), bf16), shape((4, boxes), f32)]
    kept = []
    for section in range(sections - 1, -1, -1):
        first = section == sections - 1

        def step(*refs, section=section, first=first):
            step_kernel(*refs, section=section, levels=levels, first=first)

        out_shape = [shape((2 * tracers, boxes), f32)] * 2 + (kept_shapes + [shape((boxes, boxes), bf16)]) * first
        send, keep, *made = pl.pallas_call(
            step,
            in_specs=[vmem] * 2 + [hbm if first else vmem] + [vmem] * (4 + len(kept)),
            out_specs=[vmem] * len(out_shape),
            out_shape=out_shape,
            scratch_shapes=[pltpu.VMEM((boxes, boxes), f32), dma] * first,
            compiler_params=lean,
        )(adjoint, ordered, borrowed, upper, slopes, uptake_t, release_t, *kept)
        if first:
            *kept, borrowed = made
        if section == 0:
            rows = ylo_size * tracers_here
            at = (0, lax.axis_index("x") * rows, 0)
            send, keep = (
                lax.dynamic_slice(part.reshape(2, tracers, boxes), at, (2, rows, boxes)).reshape(2 * rows, boxes)
                for part in (send, keep)
            )
        arrived = lax.all_gather(send, EVERY, axis_index_groups=groups)
        keep = keep + lax.dynamic_index_in_dim(arrived, core_index, 0, keepdims=False)
        adjoint = lax.all_gather(keep, "core")
    mine = lax.dynamic_index_in_dim(adjoint, core_index, 0, keepdims=False)[:rows]
    theirs = lax.dynamic_index_in_dim(adjoint, 1 - core_index, 0, keepdims=False)[rows:]
    wet = kept[1][0:1]
    result = (wet * (mine + theirs)).reshape(ylo_size, tracers_here, boxes)
    passed = lax.dynamic_index_in_dim(result, 1 - ylo_index, 0, keepdims=False)
    passed = lax.dynamic_index_in_dim(lax.all_gather(passed, "ylo"), 1 - ylo_index, 0, keepdims=False)
    return jnp.where(joined, lax.dynamic_index_in_dim(result, ylo_index, 0, keepdims=False), passed)


def solution(mesh):
    regions, tracer_devices = mesh.devices.shape
    nq, nx, ny = regions // 2, tracer_devices // 2, 2
    fine = Mesh(mesh.devices.reshape(nq // 2, 2, 2, nx, ny), EVERY)
    placed = (
        P(TRACER, REGION),
        P(None, TRACER, REGION),
        P(REGION, None, None),
        P(REGION),
        P(REGION, None, None, None),
        P(REGION, None),
        P(REGION),
        P(),
        P(),
    )

    def body(*args):
        return local(*args, sizes=(nq, nx, ny))

    return jax.shard_map(body, mesh=fine, in_specs=placed, out_specs=P(TRACER, REGION), check_vma=False)
```

```python
import jax
import jax.numpy as jnp
from jax import lax
from jax.experimental import pallas as pl
from jax.experimental.pallas import tpu as pltpu
from jax.sharding import Mesh, PartitionSpec as P


REGION = ("z", "yhi", "core")
TRACER = ("x", "ylo")
EVERY = REGION + TRACER
SPAN = 128
VMEM_LIMIT = 8 * 2**20
COUNT_AT, CORE_AT = 5, 6


def neighbour_groups(sizes):
    nq, nx, ny = sizes

    def at(chip, core, x, ylo):
        return (((chip % nq) * 2 + core) * nx + x) * ny + ylo

    groups = []
    for q in range(nq):
        for x in range(nx):
            joined, alone = (1, 0) if q % 2 == 0 else (0, 1)
            groups.append([at(q, 1, x, joined), at(q + 1, 0, x, 1 - joined)])
            groups.append([at(q, 1, x, alone), at(q, 0, x, alone)])
    return groups


def chip_groups(sizes):
    nq, nx, ny = sizes
    return [
        [((q * 2 + core) * nx + x) * ny + ylo for ylo in range(ny) for core in (1, 0)]
        for q in range(nq)
        for x in range(nx)
    ]


def halves(value):
    high = value.astype(jnp.bfloat16)
    low = (value - high.astype(jnp.float32)).astype(jnp.bfloat16)
    return high, low


def dot(a, b):
    return lax.dot_general(a, b, (((1,), (0,)), ((), ())), preferred_element_type=jnp.float32)


def dot_split(a_high, a_low, b_high, b_low):
    rows = a_high.shape[0]
    both = dot(jnp.concatenate([a_high, a_low], axis=0), b_high)
    return both[:rows] + both[rows:] + dot(a_high, b_low)


def slot_at(offsets, slots, distance):
    slot = jnp.int32(0)
    for k in range(slots):
        slot = slot + jnp.where(offsets[k] == distance, k, 0)
    return slot


def slot_live(offsets, slots, distance):
    live = jnp.int32(0)
    for k in range(slots):
        live = live + jnp.where((offsets[k] == distance) & (k < offsets[COUNT_AT]), 1, 0)
    return live > 0


def pack_kernel(cotangent, states, copies, buffer, fetched):
    first = pltpu.make_async_copy(cotangent, buffer.at[0], fetched.at[0])
    rest = pltpu.make_async_copy(states, buffer.at[pl.ds(1, states.shape[0])], fetched.at[1])
    first.start()
    rest.start()
    first.wait()
    rest.wait()
    for t in range(copies.shape[0]):
        copies[t] = buffer[...]


def lend_kernel(offsets_hbm, tiles, lent, offsets, buffer, arrival):
    ask = pltpu.make_async_copy(offsets_hbm, offsets, arrival.at[0])
    ask.start()
    ask.wait()
    distance = 2 - 4 * lax.axis_index("core")
    fetch = pltpu.make_async_copy(tiles.at[0, slot_at(offsets.at[0], tiles.shape[1], distance)], buffer, arrival.at[1])
    fetch.start()
    fetch.wait()
    lent[...] = buffer[...].astype(jnp.float32)


def arrange_kernel(facts, wet, tiles, inverse, ordered, shared, upper, arrival):
    slots = tiles.shape[1]
    direction = 2 * facts[CORE_AT] - 1
    uses = (direction, 2 * direction, 0, -direction)
    fetches = [
        pltpu.make_async_copy(tiles.at[0, slot_at(facts, slots, distance)], ordered.at[n], arrival.at[n])
        for n, distance in enumerate(uses)
    ]
    for fetch in fetches:
        fetch.start()
    columns, levels, _ = inverse.shape
    lane = lax.broadcasted_iota(jnp.int32, (levels, levels), 1)
    row = lax.broadcasted_iota(jnp.int32, (8, levels), 1)
    for c in range(columns):
        at = slice(c * levels, (c + 1) * levels)
        shared[0:levels, at] = jnp.where(lane < wet[c], inverse[c], 0.0)
        shared[levels : levels + 8, at] = jnp.where(row < wet[c], 1.0, 0.0)
    lending = jnp.where(slot_live(facts, slots, -2 * direction), 1.0, 0.0)
    shared[levels + 4 :, :] = jnp.full((4, shared.shape[1]), lending, jnp.float32)
    upper[...] = jnp.full(upper.shape, facts[CORE_AT], jnp.int32).astype(jnp.float32)
    for fetch in fetches:
        fetch.wait()
    for n, distance in enumerate(uses):

        @pl.when(jnp.logical_not(slot_live(facts, slots, distance)))
        def _():
            ordered[n] = jnp.zeros(ordered.shape[1:], ordered.dtype)


def gathered_kernel(gathered, shared, uptake_weight, start, slopes):
    peers, _, few, _ = gathered.shape
    tracers = uptake_weight.shape[0]
    start[tracers:, :] = shared[...]
    for t in range(peers):
        at = slice(t * few, (t + 1) * few)
        start[at, :] = gathered[t, 0]
        for n in range(slopes.shape[0]):
            slopes[n, at, :] = gathered[t, 1 + n]
    weight_high, weight_low = halves(uptake_weight[...])
    for n in range(slopes.shape[0]):
        state_high, state_low = halves(slopes[n])
        reach = jnp.tanh(dot_split(weight_high, weight_low, state_high, state_low))
        slopes[n] = 1.0 - reach * reach


def lay_out_blocks(adjoint, is_upper, tracers, levels, blocks, wet):
    spans = adjoint.shape[2] // SPAN
    same = (
        lax.broadcasted_iota(jnp.int32, (SPAN, SPAN), 0) // levels
        == lax.broadcasted_iota(jnp.int32, (SPAN, SPAN), 1) // levels
    )
    for side in range(2):

        def rows(at):
            return jnp.where(is_upper, adjoint[1 - side, at, :], adjoint[side, at, :])

        inverses = rows(slice(tracers, tracers + levels))
        for s in range(spans):
            high, low = halves(inverses[:, s * SPAN : (s + 1) * SPAN])
            full_high = jnp.concatenate([high] * (SPAN // levels), axis=0)
            full_low = jnp.concatenate([low] * (SPAN // levels), axis=0)
            blocks[0, side * spans + s] = jnp.where(same, full_high, jnp.zeros_like(full_high))
            blocks[1, side * spans + s] = jnp.where(same, full_low, jnp.zeros_like(full_low))
        wet[side : side + 1, :] = rows(slice(tracers + levels, tracers + levels + 1))
        wet[2 + side : 3 + side, :] = rows(slice(tracers + levels + 4, tracers + levels + 5))


def settle(value, blocks, side):
    spans = value.shape[1] // SPAN
    high, low = halves(value)
    pieces = []
    for s in range(spans):
        at = slice(s * SPAN, (s + 1) * SPAN)
        k = side * spans + s
        pieces.append(dot_split(high[:, at], low[:, at], blocks[0, k], blocks[1, k]))
    return jnp.concatenate(pieces, axis=1)


def step_kernel(adjoint, ordered, borrowed, upper, slopes, uptake_t, release_t, *rest, section, levels, first):
    tracers = uptake_t.shape[0]
    is_upper = upper[0:1, :] > 0.5
    if first:
        send, keep, blocks, wet, tile, buffer, arrival = rest
        fetch = pltpu.make_async_copy(borrowed, buffer, arrival)
        fetch.start()
        lay_out_blocks(adjoint, is_upper, tracers, levels, blocks, wet)
        lower, higher = adjoint[0, 0:tracers, :], adjoint[1, 0:tracers, :]
    else:
        blocks, wet, send, keep = rest
        tile = borrowed
        lower = adjoint[0, 0:tracers, :] + adjoint[1, tracers:, :]
        higher = adjoint[1, 0:tracers, :] + adjoint[0, tracers:, :]
    own, other = jnp.where(is_upper, higher, lower), jnp.where(is_upper, lower, higher)
    if not first:
        own, other = wet[0:1, :] * own, wet[1:2, :] * other
    own_high, own_low = halves(settle(own, blocks, 0))
    other_high = (wet[3:4, :] * settle(other, blocks, 1)).astype(jnp.bfloat16)
    send[tracers:, :] = dot(own_high, ordered[1])
    release_high, release_low = halves(release_t[...])
    pushed = slopes[section] * dot_split(release_high, release_low, own_high, own_low)
    pushed_high, pushed_low = halves(pushed)
    uptake_high, uptake_low = halves(uptake_t[...])
    keep[0:tracers, :] = dot(own_high, ordered[2]) + dot_split(uptake_high, uptake_low, pushed_high, pushed_low)
    keep[tracers:, :] = dot(own_high, ordered[3])
    if first:
        fetch.wait()
        tile[...] = buffer[...].astype(jnp.bfloat16)
    send[0:tracers, :] = dot(own_high, ordered[0]) + dot(other_high, tile[...])


def local(
    cotangent,
    states,
    implicit_inverse,
    wet_levels,
    explicit_tiles,
    tile_offset,
    tile_count,
    uptake_weight,
    release_weight,
    *,
    sizes,
):
    tracers_here, boxes = cotangent.shape
    sections = states.shape[0]
    _, levels, _ = implicit_inverse.shape
    tracers = uptake_weight.shape[0]
    spans = boxes // SPAN
    peers = tracers // tracers_here
    f32, bf16 = jnp.float32, jnp.bfloat16
    shape = jax.ShapeDtypeStruct
    vmem = pl.BlockSpec(memory_space=pltpu.VMEM)
    smem = pl.BlockSpec(memory_space=pltpu.SMEM)
    hbm = pl.BlockSpec(memory_space=pltpu.HBM)
    lean = pltpu.CompilerParams(vmem_limit_bytes=VMEM_LIMIT)
    dma = pltpu.SemaphoreType.DMA
    core_index = lax.axis_index("core")
    core = core_index.astype(jnp.int32).reshape(1)
    ylo_index, ylo_size = lax.axis_index("ylo"), lax.axis_size("ylo")
    groups = neighbour_groups(sizes)

    def in_hbm(array):
        return pltpu.with_memory_space_constraint(array, pltpu.HBM)

    copies = pl.pallas_call(
        pack_kernel,
        in_specs=[hbm] * 2,
        out_specs=vmem,
        out_shape=shape((peers, 1 + sections, tracers_here, boxes), f32),
        scratch_shapes=[pltpu.VMEM((1 + sections, tracers_here, boxes), f32), dma((2,))],
        compiler_params=lean,
        name="pack",
    )(in_hbm(cotangent), in_hbm(states))
    gathered = lax.all_to_all(copies, TRACER, split_axis=0, concat_axis=0, tiled=True)
    facts = jnp.concatenate([tile_offset.reshape(-1), tile_count, core])
    lent = pl.pallas_call(
        lend_kernel,
        in_specs=[hbm] * 2,
        out_specs=vmem,
        out_shape=shape((boxes, boxes), f32),
        scratch_shapes=[pltpu.SMEM(tile_offset.shape, jnp.int32), pltpu.VMEM((boxes, boxes), bf16), dma((2,))],
        compiler_params=lean,
        name="lend",
    )(in_hbm(tile_offset), in_hbm(explicit_tiles))
    borrowed = in_hbm(lax.ppermute(lent, "core", [(0, 1), (1, 0)]))
    ordered, shared, upper = pl.pallas_call(
        arrange_kernel,
        in_specs=[smem] * 2 + [hbm, vmem],
        out_specs=[vmem] * 3,
        out_shape=[
            shape((4, boxes, boxes), bf16),
            shape((levels + 8, boxes), f32),
            shape((8, boxes), f32),
        ],
        scratch_shapes=[dma((4,))],
        compiler_params=lean,
        name="arrange",
    )(facts, wet_levels, in_hbm(explicit_tiles), implicit_inverse)
    start, slopes = pl.pallas_call(
        gathered_kernel,
        in_specs=[vmem] * 3,
        out_specs=[vmem] * 2,
        out_shape=[shape((tracers + levels + 8, boxes), f32), shape((sections, tracers, boxes), f32)],
        compiler_params=lean,
        name="gathered",
    )(gathered, shared, uptake_weight)
    adjoint = lax.all_gather(start, "core")
    uptake_t, release_t = uptake_weight.T, release_weight.T
    kept_shapes = [shape((2, 2 * spans, SPAN, SPAN), bf16), shape((4, boxes), f32)]
    kept = []
    for section in range(sections - 1, -1, -1):
        first = section == sections - 1

        def step(*refs, section=section, first=first):
            step_kernel(*refs, section=section, levels=levels, first=first)

        out_shape = [shape((2 * tracers, boxes), f32)] * 2 + (kept_shapes + [shape((boxes, boxes), bf16)]) * first
        send, keep, *made = pl.pallas_call(
            step,
            in_specs=[vmem] * 2 + [hbm if first else vmem] + [vmem] * (4 + len(kept)),
            out_specs=[vmem] * len(out_shape),
            out_shape=out_shape,
            scratch_shapes=[pltpu.VMEM((boxes, boxes), f32), dma] * first,
            compiler_params=lean,
        )(adjoint, ordered, borrowed, upper, slopes, uptake_t, release_t, *kept)
        if first:
            *kept, borrowed = made
        if section == 0:
            rows = ylo_size * tracers_here
            at = (0, lax.axis_index("x") * rows, 0)
            send, keep = (
                lax.dynamic_slice(part.reshape(2, tracers, boxes), at, (2, rows, boxes)).reshape(2 * rows, boxes)
                for part in (send, keep)
            )
        arrived = lax.all_gather(send, EVERY, axis_index_groups=groups)
        keep = keep + lax.dynamic_index_in_dim(arrived, core_index, 0, keepdims=False)
        if section > 0:
            adjoint = lax.all_gather(keep, "core")
    final = lax.all_gather(keep, EVERY, axis_index_groups=chip_groups(sizes))
    joined = 2 * (1 - lax.axis_index("yhi"))
    row = ylo_index * tracers_here
    mine = lax.dynamic_slice(final, (joined + 1 - core_index, row, 0), (1, tracers_here, boxes))[0]
    theirs = lax.dynamic_slice(final, (joined + core_index, rows + row, 0), (1, tracers_here, boxes))[0]
    return kept[1][0:1] * (mine + theirs)


def solution(mesh):
    regions, tracer_devices = mesh.devices.shape
    nq, nx, ny = regions // 2, tracer_devices // 2, 2
    fine = Mesh(mesh.devices.reshape(nq // 2, 2, 2, nx, ny), EVERY)
    placed = (
        P(TRACER, REGION),
        P(None, TRACER, REGION),
        P(REGION, None, None),
        P(REGION),
        P(REGION, None, None, None),
        P(REGION, None),
        P(REGION),
        P(),
        P(),
    )

    def body(*args):
        return local(*args, sizes=(nq, nx, ny))

    return jax.shard_map(body, mesh=fine, in_specs=placed, out_specs=P(TRACER, REGION), check_vma=False)
```
